512 devices in a mesh: user: 32 (over x, y, core), item: 16 (over z).
Axes of the slice: x: 4, y: 4, z: 16, core: 2. Of those that a mesh axis runs over, the one named last changes fastest.
Arguments:
- tokens: bfloat16 [262144, 1024], P(('user', 'item')), may hold values from -6 to 6
- lengths: int32 [512, 32], P(('user', 'item')), may hold values from 1 to 16, as said below
- destination: int32 [512, 32], P(('user', 'item')), may hold values from 0 to 31, as said below
- worker_offset: int32 [512, 32], P(('user', 'item')), may hold values from 0 to 255
- positives: int32 [262144], P(('user', 'item')), may hold values from 0 to 4095, as said below
- negatives: int32 [16, 256], replicated, may hold values from 0 to 4095, as said below
- table: bfloat16 [4096, 1024], P('item'), may hold values from -6 to 6
- in_gain: float32 [1024], replicated, may hold values from 0.1 to 1.9
- w_uvqk: bfloat16 [1024, 2048], P('item'), may hold values from -0.1875 to 0.1875
- out_gain: float32 [512], replicated, may hold values from 0.1 to 1.9
- w_out: bfloat16 [512, 1024], P(None, 'item'), may hold values from -0.25 to 0.25
Outputs:
- layer_out: bfloat16 [131072, 1024], P(('user', 'item'))
- token_grad: bfloat16 [262144, 1024], P(('user', 'item'))
- item_grad: float32 [4096, 1024], P('item', 'user')
The draws below stay inside these ranges and needn't reach their ends.
Inputs may be any that keep to these rules, and one draw needn't show every extreme that they name: `lengths`: A device's histories lie in its rows in order from row 0 and fill at most 512 rows; every destination receives a history of exactly 16 tokens. `destination`: A device sends its 32 histories to 32 different destinations along user; the histories sent to one device by the devices of its item index, placed at their worker_offset, cover its 256 rows exactly once. `positives`: the target ids of a device lie among the 256 table rows of its item index. `negatives`: columns k * 16 to k * 16 + 15 of each group name rows held by item index k.
All inputs are finite; a program needn't handle non-finite values.
Results may differ from the reference program's by a relative error of at most 0.017.
Values may be sent and summed in bfloat16 or wider, within the bound.
No kernel may reach another device: no remote copies, remote signals or barrier semaphores. Data moves between devices by JAX's collectives and lax.ppermute only.
A program may use at most 64 MiB of HBM per device.

```python
import jax
import jax.numpy as jnp
from jax import lax

D = 1024
HEAD = 128
TOK_DEV = 256
HIST_DEV = 32
ITEM_DEV = 256
NEG = 256
HD = 512
MOST = 16
HOME = 512
ITEMS = 4096
NEG_SH = 16
N_USER = 32
N_ITEM = 16


def plan_tables(key):
    columns_count = N_ITEM
    users_count = N_USER
    hist_count = HIST_DEV
    longest = MOST
    total_rows = columns_count * users_count
    base_key = jax.random.fold_in(key, 9001)
    streams = jax.random.split(base_key, 6)
    slot = jnp.arange(hist_count, dtype=jnp.int32)
    opening = jnp.where(slot == 0, longest, 1).astype(jnp.int32)
    sizes_now = jnp.broadcast_to(opening, (total_rows, hist_count)).astype(jnp.int32)
    prefer = jax.random.randint(streams[0], (total_rows, hist_count), 1, 9).astype(jnp.int32)
    spare = TOK_DEV - longest - (hist_count - 1)

    def grow(step, current):
        raw = jax.random.randint(jax.random.fold_in(streams[1], step), (total_rows, hist_count), 0, 4096).astype(jnp.int32)
        ranked = raw * prefer * hist_count + slot[None, :]
        room = (current < longest - 1) & (slot[None, :] > 0)
        ranked = jnp.where(room, ranked, -1)
        chosen = jnp.argmax(ranked, axis=1).astype(jnp.int32)
        return current + (slot[None, :] == chosen[:, None]).astype(jnp.int32)
    sizes_now = lax.fori_loop(0, spare, grow, sizes_now)
    shuffle = jax.random.randint(streams[2], (total_rows, hist_count), 0, 4096).astype(jnp.int32) * hist_count + slot[None, :]
    order = jnp.argsort(shuffle, axis=1, stable=True)
    composed = jnp.take_along_axis(sizes_now, order, axis=1).reshape(columns_count, users_count, hist_count)

    def permutations(stream):
        keys_list = jax.random.split(stream, columns_count)
        return jax.vmap(lambda single: jax.random.permutation(single, users_count))(keys_list).astype(jnp.int32)
    alpha = permutations(streams[3])
    outer = permutations(streams[4])
    shifts = permutations(streams[5])[:, :hist_count]
    moved = (alpha[:, :, None] + shifts[:, None, :]) % users_count
    target = jnp.take_along_axis(outer, moved.reshape(columns_count, -1), axis=1).reshape(columns_count, users_count, hist_count)
    history_len = jnp.take_along_axis(composed, target, axis=1)
    starts = jnp.cumsum(composed, axis=2) - composed
    landing = jnp.take_along_axis(starts, target, axis=1)

    def layout(values):
        return jnp.transpose(values, (1, 0, 2)).reshape(users_count * columns_count, hist_count).astype(jnp.int32)
    return (layout(history_len), layout(target), layout(landing))


def draw_lengths(key, part):
    return plan_tables(key)[0]


def draw_destination(key, part):
    return plan_tables(key)[1]


def draw_worker_offset(key, part):
    return plan_tables(key)[2]


def draw_positives(key, part):
    total_rows = N_USER * N_ITEM * HOME
    item_of = jnp.arange(total_rows, dtype=jnp.int32) // HOME % N_ITEM
    chosen = jax.random.randint(jax.random.fold_in(key, 77), (total_rows,), 0, ITEM_DEV).astype(jnp.int32)
    return (item_of * ITEM_DEV + chosen).astype(jnp.int32)


def draw_negatives(key, part):
    block = (jnp.arange(NEG, dtype=jnp.int32) // NEG_SH).astype(jnp.int32)
    chosen = jax.random.randint(jax.random.fold_in(key, 55), (N_ITEM, NEG), 0, ITEM_DEV).astype(jnp.int32)
    return (block[None, :] * ITEM_DEV + chosen).astype(jnp.int32)


def block_levels(stream_key, extent, cuts, least, high):
    level, own = 1.0, jax.random.fold_in(stream_key, 6)
    for axis_at, shards_of in cuts:
        steps = jnp.exp(jax.random.uniform(jax.random.fold_in(own, axis_at), (shards_of,), jnp.float32, least / len(cuts), high / len(cuts)))
        level = level * jnp.repeat(steps, extent[axis_at] // shards_of).reshape([-1 if axis == axis_at else 1 for axis in range(len(extent))])
    return level


def gaussian(key, dims, scale, most, cuts=(), kind=jnp.bfloat16):
    loudness = block_levels(key, dims, cuts, -0.22, 0.18) if cuts else 1.0
    result = jax.random.normal(key, dims, jnp.float32) * scale * loudness
    return jnp.minimum(jnp.maximum(result, -most), most).astype(kind)


def setup_inputs(seed: int = 0) -> dict:
    seeds = jax.random.split(jax.random.key(seed), 12)
    return {
        "tokens": gaussian(seeds[0], (N_USER * N_ITEM * HOME, D), 1.0, 6.0, ((0, 512),)),
        "lengths": draw_lengths(jax.random.fold_in(seeds[11], 71), 0),
        "destination": draw_destination(jax.random.fold_in(seeds[11], 71), 0),
        "worker_offset": draw_worker_offset(jax.random.fold_in(seeds[11], 71), 0),
        "positives": draw_positives(jax.random.fold_in(seeds[11], 71), 0),
        "negatives": draw_negatives(jax.random.fold_in(seeds[11], 71), 0),
        "table": gaussian(seeds[6], (ITEMS, D), 1.0, 6.0, ((0, 16),)),
        "in_gain": jnp.clip(1.0 + 0.18 * jax.random.normal(seeds[7], (D,), jnp.float32), 0.1, 1.9),
        "w_uvqk": gaussian(seeds[8], (D, 4 * HD), D ** -0.5, 0.1875, ((0, 16),)),
        "out_gain": jnp.clip(1.0 + 0.18 * jax.random.normal(seeds[9], (HD,), jnp.float32), 0.1, 1.9),
        "w_out": gaussian(seeds[10], (HD, D), HD ** -0.5, 0.25, ((1, 16),)),
    }


norm_epsilon = 1e-05
scale_epsilon = 1e-06
inverse_temp = 20.0
loss_scale = 32.0

def layer_norm(values, gain):
    center = lax.optimization_barrier(jnp.mean(values, axis=-1, keepdims=True))
    shifted = values - center
    spread = lax.optimization_barrier(jnp.mean(shifted * shifted, axis=-1, keepdims=True))
    return shifted * lax.rsqrt(spread + norm_epsilon) * gain

def hstu_block(rows, segment, in_gain, w_uvqk, out_gain, w_out):
    count = rows.shape[0]
    rows_f = rows.astype(jnp.float32)
    normed = layer_norm(rows_f, in_gain).astype(jnp.bfloat16)
    active = jax.nn.silu(jnp.dot(normed, w_uvqk, preferred_element_type=jnp.float32)).astype(jnp.bfloat16)
    width = active.shape[1] // 4
    heads = width // HEAD

    def split_heads(block):
        return block.reshape(count, heads, HEAD).astype(jnp.float32)
    gate_u = active[:, :width]
    values_v = split_heads(active[:, width:2 * width])
    queries = split_heads(active[:, 2 * width:3 * width])
    key_rows = split_heads(active[:, 3 * width:])
    scores = jnp.einsum('qhd,khd->hqk', queries, key_rows) * HEAD ** (-0.5)
    order = jnp.arange(count, dtype=jnp.int32)
    allowed = (segment[:, None] == segment[None, :]) & (order[None, :] <= order[:, None])
    weights = jnp.where(allowed[None], jax.nn.silu(scores), 0.0).astype(jnp.bfloat16)
    mixed = jnp.einsum('hqk,khd->qhd', weights.astype(jnp.float32), values_v).reshape(count, width)
    gated = (layer_norm(mixed, out_gain) * gate_u.astype(jnp.float32)).astype(jnp.bfloat16)
    return (rows_f + jnp.dot(gated, w_out, preferred_element_type=jnp.float32)).astype(jnp.bfloat16)

def reference(tokens, lengths, destination, worker_offset, positives, negatives, table, in_gain, w_uvqk, out_gain, w_out):
    devices = N_USER * N_ITEM
    history_len = lengths.astype(jnp.int32)
    home_start = (jnp.cumsum(history_len, axis=1) - history_len).astype(jnp.int32)
    ends = (home_start + history_len).astype(jnp.int32)
    row_ids = jnp.arange(HOME, dtype=jnp.int32)
    segment = lax.optimization_barrier(jnp.sum((row_ids[None, :, None] >= ends[:, None, :]).astype(jnp.int32), axis=2)).astype(jnp.int32)
    valid = row_ids[None, :] < lax.optimization_barrier(jnp.sum(history_len, axis=1)).astype(jnp.int32)[:, None]
    history = jnp.minimum(segment, HIST_DEV - 1).astype(jnp.int32)
    item_of = (jnp.arange(devices, dtype=jnp.int32) % N_ITEM).astype(jnp.int32)
    worker_dev = (destination.astype(jnp.int32) * N_ITEM + item_of[:, None]).astype(jnp.int32)

    def pick(values):
        return jnp.take_along_axis(values, history, axis=1).astype(jnp.int32)
    target = pick(worker_dev) * TOK_DEV + pick(worker_offset.astype(jnp.int32)) + row_ids[None, :] - pick(home_start)
    target = jnp.where(valid, target, devices * TOK_DEV).reshape(-1).astype(jnp.int32)
    home_index = jnp.arange(devices * HOME, dtype=jnp.int32)
    source = jnp.zeros((devices * TOK_DEV,), jnp.int32).at[target].set(home_index, mode='drop')
    worker_input = tokens[source].reshape(devices, TOK_DEV, D)
    worker_segment = (source // HOME).astype(jnp.int32).reshape(devices, TOK_DEV)
    computed = lax.map(lambda pair: hstu_block(pair[0], pair[1], in_gain, w_uvqk, out_gain, w_out), (worker_input, worker_segment))
    layer_out = computed.reshape(devices * TOK_DEV, D)
    flat_valid = valid.reshape(-1)
    clipped = jnp.minimum(target, devices * TOK_DEV - 1).astype(jnp.int32)
    home_out = jnp.where(flat_valid[:, None], layer_out[clipped], jnp.zeros((), layer_out.dtype))
    table_f = table.astype(jnp.float32)
    table_scale = lax.rsqrt(lax.optimization_barrier(jnp.mean(table_f * table_f, axis=1)) + scale_epsilon)
    table_hat = table_f * table_scale[:, None]
    table_low = table_hat.astype(jnp.bfloat16)

    def by_column(values):
        shaped = values.reshape((N_USER, N_ITEM, HOME) + values.shape[1:])
        moved = jnp.moveaxis(shaped, 1, 0)
        return moved.reshape((N_ITEM, N_USER * HOME) + values.shape[1:])
    out_cols = by_column(home_out)
    valid_cols = by_column(flat_valid)
    positive_cols = by_column(positives.astype(jnp.int32))
    negative_rows = table_low[negatives.astype(jnp.int32)]
    factor = inverse_temp / D

    def column(inputs):
        out_rows, valid_rows, positive_ids, group_rows, column_index = inputs
        out_f = out_rows.astype(jnp.float32)
        out_scale = lax.rsqrt(lax.optimization_barrier(jnp.mean(out_f * out_f, axis=1)) + scale_epsilon)
        out_hat = out_f * out_scale[:, None]
        out_low = out_hat.astype(jnp.bfloat16)
        positive_rows = table_low[positive_ids]
        positive_logit = lax.optimization_barrier(jnp.sum(out_low.astype(jnp.float32) * positive_rows.astype(jnp.float32), axis=1)) * factor
        negative_logit = jnp.dot(out_low, group_rows.T, preferred_element_type=jnp.float32) * factor
        positive_exp = jnp.exp(positive_logit)
        negative_exp = jnp.exp(negative_logit)
        partition = positive_exp + lax.optimization_barrier(jnp.sum(negative_exp, axis=1))
        weight = jnp.where(valid_rows, loss_scale, 0.0)
        positive_grad = weight * (positive_exp / partition - 1.0)
        negative_grad = (weight[:, None] * negative_exp / partition[:, None]).astype(jnp.bfloat16)
        grad_hat = (positive_grad[:, None] * positive_rows.astype(jnp.float32) + jnp.dot(negative_grad, group_rows, preferred_element_type=jnp.float32)) * factor
        token_part = ((grad_hat - out_hat * lax.optimization_barrier(jnp.mean(grad_hat * out_hat, axis=1, keepdims=True))) * out_scale[:, None]).astype(jnp.bfloat16)
        negative_terms = jnp.dot(negative_grad.T, out_low, preferred_element_type=jnp.float32) * factor
        local_ids = (positive_ids - column_index * ITEM_DEV).astype(jnp.int32)
        positive_terms = jax.ops.segment_sum((positive_grad * factor)[:, None] * out_low.astype(jnp.float32), local_ids, num_segments=ITEM_DEV)
        return (token_part, negative_terms, positive_terms)
    token_cols, negative_terms, positive_terms = lax.map(column, (out_cols, valid_cols, positive_cols, negative_rows, jnp.arange(N_ITEM, dtype=jnp.int32)))
    token_grad = jnp.moveaxis(token_cols.reshape(N_ITEM, N_USER, HOME, D), 0, 1).reshape(devices * HOME, D)
    row_sums = positive_terms.reshape(ITEMS, D) + jnp.zeros((ITEMS, D), jnp.float32).at[negatives.reshape(-1).astype(jnp.int32)].add(negative_terms.reshape(-1, D))
    item_grad = (row_sums - table_hat * lax.optimization_barrier(jnp.mean(row_sums * table_hat, axis=1, keepdims=True))) * table_scale[:, None]
    return (layer_out, token_grad, item_grad)
```

```python
import jax
import jax.numpy as jnp
from jax import lax
from jax.experimental import pallas as pl
from jax.experimental.pallas import tpu as pltpu
from jax.sharding import PartitionSpec as P

norm_epsilon = 1e-05
scale_epsilon = 1e-06
inverse_temp = 20.0
loss_scale = 32.0

F32 = jnp.float32
BF16 = jnp.bfloat16

USERS = 32
ITEMS = 16
PLANE = 16
LANES = 128
ROWS = 512
MOST = 16
WIDTH = 1024
HEAD = 128

FIRST = [[x * 8 + y * 2 for x in range(4)] for y in range(4)] + [
    [x * 8 + y * 2 + 1 for y in range(4)] for x in range(4)
]
SECOND = [[x * 8 + y * 2 for y in range(4)] for x in range(4)] + [
    [x * 8 + y * 2 + 1 for x in range(4)] for y in range(4)
]
SAME_CORE = [[k * 2 + c for k in range(PLANE)] for c in range(2)]
PARTNER = [(k, k ^ 1) for k in range(USERS)]

VMEM = pl.BlockSpec(memory_space=pltpu.VMEM)
SMEM = pl.BlockSpec(memory_space=pltpu.SMEM)
W_ROWS = 512
REST = 208


def shape(dims, kind=BF16):
    return jax.ShapeDtypeStruct(dims, kind)


def dot(a, b, contract=((1,), (0,))):
    return lax.dot_general(a, b, (contract, ((), ())), preferred_element_type=F32)


def call(body, outs, specs, scratch=(), name=None):
    return pl.pallas_call(
        body,
        out_shape=outs,
        in_specs=specs,
        out_specs=jax.tree.map(lambda _: VMEM, outs),
        scratch_shapes=list(scratch),
        name=name,
        compiler_params=pltpu.CompilerParams(vmem_limit_bytes=56 * 2**20),
    )


def forward_body(got, label, out):
    for i in range(ITEMS):
        out[0, i * 32 : (i + 1) * 32, :] = got[i, 0:32, :]
    for b in range(8):
        out[0, W_ROWS + b * 16 : W_ROWS + (b + 1) * 16, :] = (
            got[2 * b, 32:48, :].astype(F32) + got[2 * b + 1, 32:48, :].astype(F32)
        ).astype(BF16)
    quads = got[:, 48:56, :].astype(F32)
    for b in range(4):
        out[0, W_ROWS + 128 + b * 16 : W_ROWS + 144 + b * 16, :] = quads[:, b, :].astype(BF16)
    out[0, W_ROWS + 192 : W_ROWS + 208, :] = label[...]
    for g in range(1, 4):
        out[g] = out[0]


def half_body(x_ref, w_ref, first_ref, u_ref, mixed_ref):
    x = x_ref[...]

    def part(q):
        w = jnp.concatenate([w_ref[2 * q], w_ref[2 * q + 1]], axis=1)
        return jax.nn.silu(dot(x, w)).astype(BF16)

    u_ref[...] = part(0)
    v = part(1)
    q = part(2)
    k = part(3)
    for b in range(4):
        lo, hi = b * 128, (b + 1) * 128
        at = max(lo - 128, 0)
        rows = lo + lax.broadcasted_iota(jnp.int32, (128, hi - at), 0)
        cols = at + lax.broadcasted_iota(jnp.int32, (128, hi - at), 1)
        first = first_ref[lo:hi, :]
        allowed = (cols >= first) & (cols <= rows)
        for h in range(2):
            d0, d1 = h * HEAD, (h + 1) * HEAD
            scores = dot(q[lo:hi, d0:d1], k[at:hi, d0:d1], ((1,), (1,))) * HEAD ** (-0.5)
            weights = jnp.where(allowed, jax.nn.silu(scores), 0.0).astype(BF16)
            mixed_ref[lo:hi, d0:d1] = dot(weights, v[at:hi, d0:d1])


def out_body(tok_ref, u0, m0, rest0, u1, m1, rest1, gain_ref, send_ref, out_ref, parcel_ref):
    a, b = m0[...], m1[...]
    width = 512.0
    center = (jnp.sum(a, axis=1, keepdims=True) + jnp.sum(b, axis=1, keepdims=True)) / width
    a, b = a - center, b - center
    spread = (
        jnp.sum(a * a, axis=1, keepdims=True) + jnp.sum(b * b, axis=1, keepdims=True)
    ) / width
    inv = lax.rsqrt(spread + norm_epsilon)
    ga = (a * inv * gain_ref[:, 0:256] * u0[...].astype(F32)).astype(BF16)
    gb = (b * inv * gain_ref[:, 256:512] * u1[...].astype(F32)).astype(BF16)

    def columns(rest):
        return jnp.concatenate(
            [rest[:, n * 16 : (n + 1) * 16, :].reshape(256, LANES) for n in range(8)], axis=1
        )

    delta = dot(ga, columns(rest0)) + dot(gb, columns(rest1))
    out = (tok_ref[...].astype(F32) + delta).astype(BF16)
    out_ref[...] = out
    parcel_ref[...] = dot(send_ref[...], out).astype(BF16)


def loss_body(core, out_ref, low_ref, rest0, rest1, pos_ref, weight_ref, grad_ref, own_ref, send_ref, own_inner, terms):
    c = core[0]

    def columns(rest):
        return jnp.concatenate(
            [rest[:, 128 + n * 16 : 144 + n * 16, :].reshape(256, LANES) for n in range(4)], axis=1
        ).astype(F32)

    g0, g1 = columns(rest0), columns(rest1)
    size = (jnp.sum(g0 * g0, axis=1, keepdims=True) + jnp.sum(g1 * g1, axis=1, keepdims=True)) / WIDTH
    scale = lax.rsqrt(size + scale_epsilon)
    g0, g1 = (g0 * scale).astype(BF16), (g1 * scale).astype(BF16)
    here = c == 0
    both = jnp.concatenate([jnp.where(here, g0, g1), jnp.where(here, g1, g0)], axis=1)
    row = lax.broadcasted_iota(jnp.int32, (256, 256), 0)
    col = lax.broadcasted_iota(jnp.int32, (256, 256), 1)
    swap = jnp.where(col == (row % 16) * 16 + row // 16, 1.0, 0.0).astype(BF16)
    group = dot(swap, both).astype(BF16)
    rows = jnp.concatenate([low_ref[...], group], axis=0)

    out = out_ref[...].astype(F32)
    out_scale = lax.rsqrt(jnp.mean(out * out, axis=1, keepdims=True) + scale_epsilon)
    hat = out * out_scale
    low = hat.astype(BF16)
    factor = inverse_temp / WIDTH
    raw = dot(low, rows, ((1,), (1,)))
    hit = lax.broadcasted_iota(jnp.int32, (ROWS, 256), 1) == pos_ref[...]
    pos = jnp.exp(jnp.sum(jnp.where(hit, raw[:, :256], 0.0), axis=1, keepdims=True) * factor)
    neg = jnp.exp(raw[:, 256:] * factor)
    total = pos + jnp.sum(neg, axis=1, keepdims=True)
    weight = weight_ref[...]
    pos_grad = weight * (pos / total - 1.0)
    grads = jnp.concatenate(
        [jnp.where(hit, pos_grad, 0.0).astype(BF16), (weight * neg / total).astype(BF16)], axis=1
    )
    grad_hat = dot(grads, rows) * factor
    inner = jnp.mean(grad_hat * hat, axis=1, keepdims=True)
    grad_ref[...] = ((grad_hat - hat * inner) * out_scale).astype(BF16)
    sums = dot(low, grads, ((0,), (0,))) * factor
    terms[...] = sums.astype(BF16).reshape(PLANE, 2, 32, ROWS)
    for k in range(PLANE):
        own_ref[k] = terms[k, c]
        send_ref[k * 32 : (k + 1) * 32, :] = terms[k, 1 - c]
    products = jnp.sum(grads.astype(F32) * raw, axis=0, keepdims=True) * factor
    own_inner[...] = products
    top = products.astype(BF16).astype(F32)
    send_ref[512:528, :] = split_rows(top, products - top).astype(BF16)


def split_rows(top, rest):
    at = lax.broadcasted_iota(jnp.int32, (16, ROWS), 0)
    return jnp.where(at == 0, top, jnp.where(at == 1, rest, 0.0))


def pair_body(own_ref, inner_ref, got_ref, out_ref):
    other = got_ref[512:528, :].astype(F32)
    inner = inner_ref[...] + other[0:1, :] + other[1:2, :]
    top = inner.astype(BF16).astype(F32)
    tail = split_rows(top, inner - top).astype(BF16)
    for k in range(PLANE):
        mine = own_ref[k].astype(F32) + got_ref[k * 32 : (k + 1) * 32, :].astype(F32)
        out_ref[k, 0:32, :] = mine.astype(BF16)
        out_ref[k, 32:48, :] = tail


def plane_body(got_ref, pos_ref, neg_ref):
    acc = got_ref[0].astype(F32)
    for k in range(1, PLANE):
        acc = acc + got_ref[k].astype(F32)
    inner = acc[32:33, :] + acc[33:34, :]
    top = inner.astype(BF16).astype(F32)
    full = jnp.concatenate(
        [acc[0:32, :], split_rows(top, inner - top), jnp.zeros((80, ROWS), F32)], axis=0
    )
    turned = jnp.transpose(full)
    pos_ref[...] = turned[0:256, :]
    neg_ref[...] = turned[256:512, :].astype(BF16)


def item_body(pos_ref, hits_ref, got_ref, hat_ref, scale_ref, out_ref):
    total = pos_ref[...] + dot(hits_ref[...], got_ref[...])
    inner = (total[:, 32:33] + total[:, 33:34]) / WIDTH
    out_ref[...] = (total[:, 0:32] - hat_ref[...] * inner) * scale_ref[...]


def layer_norm(values, gain):
    center = jnp.mean(values, axis=-1, keepdims=True)
    shifted = values - center
    spread = jnp.mean(shifted * shifted, axis=-1, keepdims=True)
    return shifted * lax.rsqrt(spread + norm_epsilon) * gain


def copies(block, count):
    return jnp.broadcast_to(block[None], (count, *block.shape))


def exchange(blocks, axis, groups=None):
    return lax.all_to_all(blocks, axis, 0, 0, tiled=True, axis_index_groups=groups)


def per_device(
    tokens,
    lengths,
    destination,
    worker_offset,
    positives,
    negatives,
    table,
    in_gain,
    w_uvqk,
    out_gain,
    w_out,
):
    item = lax.axis_index("item")
    user = lax.axis_index("user")
    x, y, core = user // 8, (user // 2) % 4, user % 2
    place = jnp.where(core == 0, y * 4 + x, x * 4 + y)
    item_rows = table.shape[0]

    chunk, half = place // 2, place % 2
    block = (chunk // 2) * 4 + core * 2 + chunk % 2
    w_part = lax.dynamic_slice(w_uvqk, (half * 32, block * LANES), (32, LANES))
    o_part = lax.dynamic_slice(w_out, (core * 256 + place * 16, 0), (16, 64))
    blank = jnp.zeros_like(o_part)
    odd = item % 2 == 1
    o_part = jnp.concatenate(
        [jnp.where(odd, blank, o_part), jnp.where(odd, o_part, blank)], axis=1
    )
    ids = lax.dynamic_slice(negatives, (0, item * 16 + place), (ITEMS, 1)) - item * item_rows
    pick = (ids == jnp.arange(item_rows, dtype=jnp.int32)[None, :]).astype(BF16)
    g_part = jnp.dot(pick, lax.dynamic_slice(table, (0, core * 512), (item_rows, 512)))
    first_message = jnp.concatenate(
        [
            copies(jnp.concatenate([w_part, o_part], axis=0), ITEMS),
            jnp.pad(g_part.reshape(ITEMS, 4, LANES), ((0, 0), (0, 4), (0, 0))),
        ],
        axis=1,
    )
    got = exchange(first_message, "item")

    history_len = lengths[0]
    home_start = jnp.cumsum(history_len) - history_len
    row_ids = jnp.arange(ROWS, dtype=jnp.int32)
    inside = (row_ids[:, None] >= home_start[None, :]) & (
        row_ids[:, None] < (home_start + history_len)[None, :]
    )
    valid = jnp.any(inside, axis=1, keepdims=True)
    first = jnp.where(
        valid,
        jnp.sum(jnp.where(inside, home_start[None, :], 0), axis=1, keepdims=True),
        row_ids[:, None],
    )
    weight = jnp.where(valid, loss_scale, 0.0).astype(F32)
    peers = jnp.arange(USERS, dtype=jnp.int32)
    chosen = (destination[0][None, :] == peers[:, None]).astype(jnp.int32)
    first_row = jnp.sum(chosen * home_start[None, :], axis=1)
    count = jnp.sum(chosen * history_len[None, :], axis=1)
    landing = jnp.sum(chosen * worker_offset[0][None, :], axis=1)
    label = jnp.concatenate([landing, count, jnp.zeros((64,), jnp.int32)]).astype(BF16)
    labels = jnp.broadcast_to(label[None], (16, LANES))
    within = jnp.arange(MOST, dtype=jnp.int32)
    source = jnp.where(within[None, :] < count[:, None], first_row[:, None] + within[None, :], -1)
    send = (source.reshape(-1)[:, None] == row_ids[None, :]).astype(BF16)

    message = call(
        forward_body, shape((4, W_ROWS + REST, LANES)), [VMEM, VMEM], name="forward"
    )(got, labels)
    mid = exchange(message, "user", FIRST)
    w_own = exchange(copies(mid[:, :W_ROWS], 4), "user", SECOND).reshape(8, 2 * W_ROWS, LANES)
    w_other = lax.ppermute(w_own, "user", PARTNER)
    rest_own = exchange(copies(mid[:, W_ROWS:], 4), "user", SECOND).reshape(16, REST, LANES)
    rest_other = lax.ppermute(rest_own, "user", PARTNER)

    normed = layer_norm(tokens.astype(F32), in_gain).astype(BF16)
    at = jnp.arange(WIDTH, dtype=jnp.int32)
    wanted = (at % 512) // 32 * 64 + at // 512 * 32 + at % 32
    order = (at[:, None] == wanted[None, :]).astype(BF16)
    normed = jnp.dot(normed, order, preferred_element_type=F32).astype(BF16)
    layer_half = call(
        half_body, (shape((ROWS, 256)), shape((ROWS, 256), F32)), [VMEM] * 3, name="half"
    )
    u_own, mixed_own = layer_half(normed, w_own, first)
    u_other, mixed_other = layer_half(normed, w_other, first)
    gain = jnp.where(core == 0, out_gain, jnp.roll(out_gain, 256))[None]
    home_out, parcels = call(
        out_body, (shape((ROWS, WIDTH)), shape((ROWS, WIDTH))), [VMEM] * 9, name="layer_out"
    )(tokens, u_own, mixed_own, rest_own, u_other, mixed_other, rest_other, gain, send)
    arrived = exchange(parcels.reshape(USERS, MOST, WIDTH), "user").reshape(ROWS, WIDTH)

    near, far = rest_own[:, 192, :], rest_other[:, 192, :]
    mine = (jnp.arange(LANES, dtype=jnp.int32)[None, :] == user).astype(F32)
    mine_count = (jnp.arange(LANES, dtype=jnp.int32)[None, :] == user + USERS).astype(F32)

    def by_user(select):
        a = jnp.sum(near.astype(F32) * select, axis=1)
        b = jnp.sum(far.astype(F32) * select, axis=1)
        even = jnp.where(core == 0, a, b).reshape(4, 4).T
        uneven = jnp.where(core == 0, b, a).reshape(4, 4)
        return jnp.stack([even, uneven], axis=2).reshape(USERS).astype(jnp.int32)

    lower, arrived_count = by_user(mine), by_user(mine_count)
    lands = jnp.where(within[None, :] < arrived_count[:, None], lower[:, None] + within[None, :], -1)
    receive = (jnp.arange(256, dtype=jnp.int32)[:, None] == lands.reshape(-1)[None, :]).astype(BF16)
    layer_out = jnp.dot(receive, arrived, preferred_element_type=F32).astype(BF16)

    table_f = table.astype(F32)
    table_scale = lax.rsqrt(jnp.mean(table_f * table_f, axis=1, keepdims=True) + scale_epsilon)
    table_hat = table_f * table_scale
    table_low = table_hat.astype(BF16)
    positive_local = (positives - item * item_rows)[:, None]
    token_grad, own, sent, own_inner = call(
        loss_body,
        (
            shape((ROWS, WIDTH)),
            shape((PLANE, 32, ROWS)),
            shape((528, ROWS)),
            shape((1, ROWS), F32),
        ),
        [SMEM] + [VMEM] * 6,
        scratch=[pltpu.VMEM((PLANE, 2, 32, ROWS), BF16)],
        name="loss",
    )(core.reshape(1), home_out, table_low, rest_own, rest_other, positive_local, weight)
    partner_terms = lax.ppermute(sent, "user", PARTNER)
    pair = call(pair_body, shape((PLANE, 48, ROWS)), [VMEM] * 3, name="pair")(
        own, own_inner, partner_terms
    )
    plane = exchange(pair, "user", SAME_CORE)
    positive_part, negative_part = call(
        plane_body, (shape((256, LANES), F32), shape((256, LANES))), [VMEM], name="plane"
    )(plane)
    owned = exchange(negative_part.reshape(ITEMS, 16, LANES), "item").reshape(256, LANES)
    owned_ids = lax.dynamic_slice_in_dim(negatives, item * 16, 16, 1) - item * item_rows
    hits = (
        jnp.arange(item_rows, dtype=jnp.int32)[:, None] == owned_ids.reshape(-1)[None, :]
    ).astype(BF16)
    hat_part = lax.dynamic_slice_in_dim(table_hat, user * 32, 32, 1)
    item_grad = call(item_body, shape((256, 32), F32), [VMEM] * 5, name="item_grad")(
        positive_part, hits, owned, hat_part, table_scale
    )
    return (layer_out, token_grad, item_grad)


def solution(mesh):
    return jax.shard_map(
        per_device,
        mesh=mesh,
        in_specs=(
            P(("user", "item"), None),
            P(("user", "item"), None),
            P(("user", "item"), None),
            P(("user", "item"), None),
            P(("user", "item")),
            P(),
            P("item", None),
            P(),
            P("item", None),
            P(),
            P(None, "item"),
        ),
        out_specs=(P(("user", "item"), None), P(("user", "item"), None), P("item", "user")),
        check_vma=False,
    )
```

```python
import jax
import jax.numpy as jnp
from jax import lax
from jax.experimental import pallas as pl
from jax.experimental.pallas import tpu as pltpu
from jax.sharding import PartitionSpec as P


norm_epsilon = 1e-05
scale_epsilon = 1e-06
inverse_temp = 20.0
loss_scale = 32.0

F32 = jnp.float32
BF16 = jnp.bfloat16

USERS = 32
ITEMS = 16
PLANE = 16
LANES = 128
ROWS = 512
MOST = 16
WIDTH = 1024
HEAD = 128

FIRST = [[x * 8 + y * 2 for x in range(4)] for y in range(4)] + [
    [x * 8 + y * 2 + 1 for y in range(4)] for x in range(4)
]
SECOND = [[x * 8 + y * 2 for y in range(4)] for x in range(4)] + [
    [x * 8 + y * 2 + 1 for x in range(4)] for y in range(4)
]
SAME_CORE = [[k * 2 + c for k in range(PLANE)] for c in range(2)]
PARTNER = [(k, k ^ 1) for k in range(USERS)]

VMEM = pl.BlockSpec(memory_space=pltpu.VMEM)
SMEM = pl.BlockSpec(memory_space=pltpu.SMEM)
W_ROWS = 512
REST = 208


def shape(dims, kind=BF16):
    return jax.ShapeDtypeStruct(dims, kind)


def dot(a, b, contract=((1,), (0,))):
    return lax.dot_general(a, b, (contract, ((), ())), preferred_element_type=F32)


def call(body, outs, specs, scratch=(), mib=8):
    return pl.pallas_call(
        body,
        out_shape=outs,
        in_specs=specs,
        out_specs=jax.tree.map(lambda _: VMEM, outs),
        scratch_shapes=list(scratch),
        compiler_params=pltpu.CompilerParams(vmem_limit_bytes=mib * 2**20),
    )


def forward_body(got, label, out):
    for i in range(ITEMS):
        out[0, i * 32 : (i + 1) * 32, :] = got[i, 0:32, :]
    for b in range(8):
        out[0, W_ROWS + b * 16 : W_ROWS + (b + 1) * 16, :] = (
            got[2 * b, 32:48, :].astype(F32) + got[2 * b + 1, 32:48, :].astype(F32)
        ).astype(BF16)
    quads = got[:, 48:56, :].astype(F32)
    for b in range(4):
        out[0, W_ROWS + 128 + b * 16 : W_ROWS + 144 + b * 16, :] = quads[:, b, :].astype(BF16)
    out[0, W_ROWS + 192 : W_ROWS + 208, :] = label[...]
    for g in range(1, 4):
        out[g] = out[0]


def half_body(x_ref, w_ref, first_ref, u_ref, mixed_ref, o_ref, g_ref, label_ref):
    x = x_ref[...]
    for n in range(8):
        o_ref[:, n * LANES : (n + 1) * LANES] = w_ref[
            :, W_ROWS + n * 16 : W_ROWS + (n + 1) * 16, :
        ].reshape(256, LANES)
    for n in range(4):
        g_ref[:, n * LANES : (n + 1) * LANES] = w_ref[
            :, W_ROWS + 128 + n * 16 : W_ROWS + 144 + n * 16, :
        ].reshape(256, LANES)
    for n in range(PLANE):
        label_ref[n : n + 1, :] = w_ref[n, W_ROWS + 192 : W_ROWS + 208, :].astype(F32)[0:1, :]

    def part(q):
        w = jnp.concatenate(
            [
                jnp.concatenate([w_ref[n, :W_ROWS, :], w_ref[n + 1, :W_ROWS, :]], axis=0)
                for n in (4 * q, 4 * q + 2)
            ],
            axis=1,
        )
        return jax.nn.silu(dot(x, w)).astype(BF16)

    u_ref[...] = part(0)
    v = part(1)
    q = part(2)
    k = part(3)
    for b in range(4):
        lo, hi = b * 128, (b + 1) * 128
        at = max(lo - 128, 0)
        rows = lo + lax.broadcasted_iota(jnp.int32, (128, hi - at), 0)
        cols = at + lax.broadcasted_iota(jnp.int32, (128, hi - at), 1)
        first = first_ref[lo:hi, :]
        allowed = (cols >= first) & (cols <= rows)
        for h in range(2):
            d0, d1 = h * HEAD, (h + 1) * HEAD
            scores = dot(q[lo:hi, d0:d1], k[at:hi, d0:d1], ((1,), (1,))) * HEAD ** (-0.5)
            weights = jnp.where(allowed, jax.nn.silu(scores), 0.0).astype(BF16)
            mixed_ref[lo:hi, d0:d1] = dot(weights, v[at:hi, d0:d1])


def out_body(tok_ref, u0, m0, o0, u1, m1, o1, gain_ref, send_ref, out_ref, parcel_ref):
    a, b = m0[...], m1[...]
    width = 512.0
    center = (jnp.sum(a, axis=1, keepdims=True) + jnp.sum(b, axis=1, keepdims=True)) / width
    a, b = a - center, b - center
    spread = (
        jnp.sum(a * a, axis=1, keepdims=True) + jnp.sum(b * b, axis=1, keepdims=True)
    ) / width
    inv = lax.rsqrt(spread + norm_epsilon)
    ga = (a * inv * gain_ref[:, 0:256] * u0[...].astype(F32)).astype(BF16)
    gb = (b * inv * gain_ref[:, 256:512] * u1[...].astype(F32)).astype(BF16)

    delta = dot(ga, o0[...]) + dot(gb, o1[...])
    out = (tok_ref[...].astype(F32) + delta).astype(BF16)
    out_ref[...] = out
    parcel_ref[...] = dot(send_ref[...], out).astype(BF16)


def loss_body(core, out_ref, low_ref, g0_ref, g1_ref, pos_ref, weight_ref, grad_ref, own_ref, send_ref, own_inner, terms):
    c = core[0]

    g0, g1 = g0_ref[...].astype(F32), g1_ref[...].astype(F32)
    size = (jnp.sum(g0 * g0, axis=1, keepdims=True) + jnp.sum(g1 * g1, axis=1, keepdims=True)) / WIDTH
    scale = lax.rsqrt(size + scale_epsilon)
    g0, g1 = (g0 * scale).astype(BF16), (g1 * scale).astype(BF16)
    here = c == 0
    both = jnp.concatenate([jnp.where(here, g0, g1), jnp.where(here, g1, g0)], axis=1)
    row = lax.broadcasted_iota(jnp.int32, (256, 256), 0)
    col = lax.broadcasted_iota(jnp.int32, (256, 256), 1)
    swap = jnp.where(col == (row % 16) * 16 + row // 16, 1.0, 0.0).astype(BF16)
    group = dot(swap, both).astype(BF16)
    rows = jnp.concatenate([low_ref[...], group], axis=0)

    out = out_ref[...].astype(F32)
    out_scale = lax.rsqrt(jnp.mean(out * out, axis=1, keepdims=True) + scale_epsilon)
    hat = out * out_scale
    low = hat.astype(BF16)
    factor = inverse_temp / WIDTH
    raw = dot(low, rows, ((1,), (1,)))
    hit = lax.broadcasted_iota(jnp.int32, (ROWS, 256), 1) == pos_ref[...]
    pos = jnp.exp(jnp.sum(jnp.where(hit, raw[:, :256], 0.0), axis=1, keepdims=True) * factor)
    neg = jnp.exp(raw[:, 256:] * factor)
    total = pos + jnp.sum(neg, axis=1, keepdims=True)
    weight = weight_ref[...]
    pos_grad = weight * (pos / total - 1.0)
    grads = jnp.concatenate(
        [jnp.where(hit, pos_grad, 0.0).astype(BF16), (weight * neg / total).astype(BF16)], axis=1
    )
    grad_hat = dot(grads, rows) * factor
    inner = jnp.mean(grad_hat * hat, axis=1, keepdims=True)
    grad_ref[...] = ((grad_hat - hat * inner) * out_scale).astype(BF16)
    sums = dot(low, grads, ((0,), (0,))) * factor
    terms[...] = sums.astype(BF16).reshape(PLANE, 2, 32, ROWS)
    for k in range(PLANE):
        own_ref[k] = terms[k, c]
        send_ref[k * 32 : (k + 1) * 32, :] = terms[k, 1 - c]
    products = jnp.sum(grads.astype(F32) * raw, axis=0, keepdims=True) * factor
    own_inner[...] = products
    top = products.astype(BF16).astype(F32)
    send_ref[512:528, :] = split_rows(top, products - top).astype(BF16)


def split_rows(top, rest):
    at = lax.broadcasted_iota(jnp.int32, (16, ROWS), 0)
    return jnp.where(at == 0, top, jnp.where(at == 1, rest, 0.0))


def pair_body(own_ref, inner_ref, got_ref, out_ref):
    other = got_ref[512:528, :].astype(F32)
    inner = inner_ref[...] + other[0:1, :] + other[1:2, :]
    top = inner.astype(BF16).astype(F32)
    tail = split_rows(top, inner - top).astype(BF16)
    for k in range(PLANE):
        mine = own_ref[k].astype(F32) + got_ref[k * 32 : (k + 1) * 32, :].astype(F32)
        out_ref[k, 0:32, :] = mine.astype(BF16)
        out_ref[k, 32:48, :] = tail


def plane_body(got_ref, pos_ref, neg_ref):
    acc = got_ref[0].astype(F32)
    for k in range(1, PLANE):
        acc = acc + got_ref[k].astype(F32)
    inner = acc[32:33, :] + acc[33:34, :]
    top = inner.astype(BF16).astype(F32)
    full = jnp.concatenate([acc[0:32, :], split_rows(top, inner - top)], axis=0)
    pos_ref[...] = full[:, 0:256]
    tail = jnp.concatenate([full[:, 256:512], jnp.zeros((80, 256), F32)], axis=0)
    neg_ref[...] = jnp.transpose(tail).astype(BF16)


def item_body(pos_ref, hits_ref, got_ref, hat_ref, scale_ref, out_ref):
    total = pos_ref[...] + dot(got_ref[...], hits_ref[...], ((0,), (0,)))[0:48, :]
    inner = (total[32:33, :] + total[33:34, :]) / WIDTH
    out_ref[...] = (total[0:32, :] - hat_ref[...] * inner) * scale_ref[...]


def layer_norm(values, gain):
    center = jnp.mean(values, axis=-1, keepdims=True)
    shifted = values - center
    spread = jnp.mean(shifted * shifted, axis=-1, keepdims=True)
    return shifted * lax.rsqrt(spread + norm_epsilon) * gain


def copies(block, count):
    return jnp.broadcast_to(block[None], (count, *block.shape))


def exchange(blocks, axis, groups=None):
    return lax.all_to_all(blocks, axis, 0, 0, tiled=True, axis_index_groups=groups)


def per_device(
    tokens,
    lengths,
    destination,
    worker_offset,
    positives,
    negatives,
    table,
    in_gain,
    w_uvqk,
    out_gain,
    w_out,
):
    item = lax.axis_index("item")
    user = lax.axis_index("user")
    x, y, core = user // 8, (user // 2) % 4, user % 2
    place = jnp.where(core == 0, y * 4 + x, x * 4 + y)
    item_rows = table.shape[0]

    chunk, half = place // 2, place % 2
    block = (chunk // 2) * 4 + core * 2 + chunk % 2
    w_part = lax.dynamic_slice(w_uvqk, (half * 32, block * LANES), (32, LANES))
    o_part = lax.dynamic_slice(w_out, (core * 256 + place * 16, 0), (16, 64))
    blank = jnp.zeros_like(o_part)
    odd = item % 2 == 1
    o_part = jnp.concatenate(
        [jnp.where(odd, blank, o_part), jnp.where(odd, o_part, blank)], axis=1
    )
    ids = lax.dynamic_slice(negatives, (0, item * 16 + place), (ITEMS, 1)) - item * item_rows
    pick = (ids == jnp.arange(item_rows, dtype=jnp.int32)[None, :]).astype(BF16)
    g_part = jnp.dot(pick, lax.dynamic_slice(table, (0, core * 512), (item_rows, 512)))
    first_message = jnp.concatenate(
        [
            copies(jnp.concatenate([w_part, o_part], axis=0), ITEMS),
            jnp.pad(g_part.reshape(ITEMS, 4, LANES), ((0, 0), (0, 4), (0, 0))),
        ],
        axis=1,
    )
    got = exchange(first_message, "item")

    history_len = lengths[0]
    home_start = jnp.cumsum(history_len) - history_len
    row_ids = jnp.arange(ROWS, dtype=jnp.int32)
    inside = (row_ids[:, None] >= home_start[None, :]) & (
        row_ids[:, None] < (home_start + history_len)[None, :]
    )
    valid = jnp.any(inside, axis=1, keepdims=True)
    first = jnp.where(
        valid,
        jnp.sum(jnp.where(inside, home_start[None, :], 0), axis=1, keepdims=True),
        row_ids[:, None],
    )
    weight = jnp.where(valid, loss_scale, 0.0).astype(F32)
    peers = jnp.arange(USERS, dtype=jnp.int32)
    chosen = (destination[0][None, :] == peers[:, None]).astype(jnp.int32)
    first_row = jnp.sum(chosen * home_start[None, :], axis=1)
    count = jnp.sum(chosen * history_len[None, :], axis=1)
    landing = jnp.sum(chosen * worker_offset[0][None, :], axis=1)
    label = jnp.concatenate([landing, count, jnp.zeros((64,), jnp.int32)]).astype(BF16)
    labels = jnp.broadcast_to(label[None], (16, LANES))
    within = jnp.arange(MOST, dtype=jnp.int32)
    source = jnp.where(within[None, :] < count[:, None], first_row[:, None] + within[None, :], -1)
    send = (source.reshape(-1)[:, None] == row_ids[None, :]).astype(BF16)

    normed = layer_norm(tokens.astype(F32), in_gain).astype(BF16)
    at = jnp.arange(WIDTH, dtype=jnp.int32)
    wanted = (at % 512) // 32 * 64 + at // 512 * 32 + at % 32
    order = (at[:, None] == wanted[None, :]).astype(BF16)
    normed = jnp.dot(normed, order, preferred_element_type=F32).astype(BF16)
    got, normed, first, labels = lax.optimization_barrier((got, normed, first, labels))

    message = call(forward_body, shape((4, W_ROWS + REST, LANES)), [VMEM, VMEM])(got, labels)
    mid = exchange(message, "user", FIRST)
    mid = mid.reshape(4 * (W_ROWS + REST), LANES)
    held = exchange(copies(mid, 4), "user", SECOND).reshape(PLANE, W_ROWS + REST, LANES)

    table_f = table.astype(F32)
    table_scale = lax.rsqrt(jnp.mean(table_f * table_f, axis=1, keepdims=True) + scale_epsilon)
    table_hat = table_f * table_scale
    table_low = table_hat.astype(BF16)
    positive_local = (positives - item * item_rows)[:, None]
    owned_ids = lax.dynamic_slice_in_dim(negatives, item * 16, 16, 1) - item * item_rows
    hits = (
        owned_ids.reshape(-1)[:, None] == jnp.arange(item_rows, dtype=jnp.int32)[None, :]
    ).astype(BF16)
    hat_part = lax.dynamic_slice_in_dim(table_hat, user * 32, 32, 1).T
    table_scale = table_scale.reshape(1, item_rows)
    gain = jnp.where(core == 0, out_gain, jnp.roll(out_gain, 256))[None]
    held, send, positive_local, weight, table_low, table_scale, hits, hat_part, gain = (
        lax.optimization_barrier(
            (held, send, positive_local, weight, table_low, table_scale, hits, hat_part, gain)
        )
    )
    held_other = lax.ppermute(held, "user", PARTNER)

    layer_half = call(
        half_body,
        (
            shape((ROWS, 256)),
            shape((ROWS, 256), F32),
            shape((256, WIDTH)),
            shape((256, 512)),
            shape((PLANE, LANES), F32),
        ),
        [VMEM] * 3,
        mib=12,
    )
    u_own, mixed_own, o_own, g_own, near = layer_half(normed, held, first)
    u_other, mixed_other, o_other, g_other, far = layer_half(normed, held_other, first)
    home_out, parcels = call(
        out_body, (shape((ROWS, WIDTH)), shape((ROWS, WIDTH))), [VMEM] * 9, mib=12
    )(tokens, u_own, mixed_own, o_own, u_other, mixed_other, o_other, gain, send)
    arrived = exchange(parcels.reshape(USERS, MOST, WIDTH), "user").reshape(ROWS, WIDTH)

    token_grad, own, sent, own_inner = call(
        loss_body,
        (
            shape((ROWS, WIDTH)),
            shape((PLANE, 32, ROWS)),
            shape((528, ROWS)),
            shape((1, ROWS), F32),
        ),
        [SMEM] + [VMEM] * 6,
        scratch=[pltpu.VMEM((PLANE, 2, 32, ROWS), BF16)],
        mib=16,
    )(core.reshape(1), home_out, table_low, g_own, g_other, positive_local, weight)
    partner_terms = lax.ppermute(sent, "user", PARTNER)
    pair = call(pair_body, shape((PLANE, 48, ROWS)), [VMEM] * 3)(own, own_inner, partner_terms)
    pair, arrived = lax.optimization_barrier((pair, arrived))
    plane = exchange(pair, "user", SAME_CORE)

    mine = (jnp.arange(LANES, dtype=jnp.int32)[None, :] == user).astype(F32)
    mine_count = (jnp.arange(LANES, dtype=jnp.int32)[None, :] == user + USERS).astype(F32)

    def by_user(select):
        a = jnp.sum(near * select, axis=1)
        b = jnp.sum(far * select, axis=1)
        even = jnp.where(core == 0, a, b).reshape(4, 4).T
        uneven = jnp.where(core == 0, b, a).reshape(4, 4)
        return jnp.stack([even, uneven], axis=2).reshape(USERS).astype(jnp.int32)

    lower, arrived_count = by_user(mine), by_user(mine_count)
    lands = jnp.where(within[None, :] < arrived_count[:, None], lower[:, None] + within[None, :], -1)
    receive = (jnp.arange(256, dtype=jnp.int32)[:, None] == lands.reshape(-1)[None, :]).astype(BF16)
    layer_out = jnp.dot(receive, arrived, preferred_element_type=F32).astype(BF16)

    positive_part, negative_part = call(
        plane_body, (shape((48, 256), F32), shape((256, LANES))), [VMEM]
    )(plane)
    owned = exchange(negative_part.reshape(ITEMS, 16, LANES), "item").reshape(256, LANES)
    item_grad = call(item_body, shape((32, 256), F32), [VMEM] * 5)(
        positive_part, hits, owned, hat_part, table_scale
    ).T
    return (layer_out, token_grad, item_grad)


def solution(mesh):
    return jax.shard_map(
        per_device,
        mesh=mesh,
        in_specs=(
            P(("user", "item"), None),
            P(("user", "item"), None),
            P(("user", "item"), None),
            P(("user", "item"), None),
            P(("user", "item")),
            P(),
            P("item", None),
            P(),
            P("item", None),
            P(),
            P(None, "item"),
        ),
        out_specs=(P(("user", "item"), None), P(("user", "item"), None), P("item", "user")),
        check_vma=False,
    )
```

```python
import jax
import jax.numpy as jnp
from jax import lax
from jax.experimental import pallas as pl
from jax.experimental.pallas import tpu as pltpu
from jax.sharding import PartitionSpec as P


norm_epsilon = 1e-05
scale_epsilon = 1e-06
inverse_temp = 20.0
loss_scale = 32.0

F32 = jnp.float32
BF16 = jnp.bfloat16

USERS = 32
ITEMS = 16
PLANE = 16
LANES = 128
ROWS = 512
MOST = 16
WIDTH = 1024
HEAD = 128

FIRST = [[x * 8 + y * 2 for x in range(4)] for y in range(4)] + [
    [x * 8 + y * 2 + 1 for y in range(4)] for x in range(4)
]
SECOND = [[x * 8 + y * 2 for y in range(4)] for x in range(4)] + [
    [x * 8 + y * 2 + 1 for x in range(4)] for y in range(4)
]
SAME_CORE = [[k * 2 + c for k in range(PLANE)] for c in range(2)]
PARTNER = [(k, k ^ 1) for k in range(USERS)]

VMEM = pl.BlockSpec(memory_space=pltpu.VMEM)
SMEM = pl.BlockSpec(memory_space=pltpu.SMEM)
W_ROWS = 512
REST = 208


def shape(dims, kind=BF16):
    return jax.ShapeDtypeStruct(dims, kind)


def dot(a, b, contract=((1,), (0,))):
    return lax.dot_general(a, b, (contract, ((), ())), preferred_element_type=F32)


def call(body, outs, specs, scratch=(), mib=8):
    return pl.pallas_call(
        body,
        out_shape=outs,
        in_specs=specs,
        out_specs=jax.tree.map(lambda _: VMEM, outs),
        scratch_shapes=list(scratch),
        compiler_params=pltpu.CompilerParams(vmem_limit_bytes=mib * 2**20),
    )


def forward_body(got, label, out):
    for i in range(ITEMS):
        out[0, i * 32 : (i + 1) * 32, :] = got[i, 0:32, :]
    left = lax.broadcasted_iota(jnp.int32, (8, LANES), 1) < 64
    for b in range(8):
        even, odd = got[2 * b, 32:40, :].astype(F32), got[2 * b + 1, 32:40, :].astype(F32)
        top = jnp.where(left, even, pltpu.roll(odd, 64, 1))
        bottom = jnp.where(left, pltpu.roll(even, 64, 1), odd)
        out[0, W_ROWS + b * 16 : W_ROWS + (b + 1) * 16, :] = jnp.concatenate(
            [top, bottom], axis=0
        ).astype(BF16)
    quads = got[:, 40:48, :].astype(F32)
    for b in range(4):
        out[0, W_ROWS + 128 + b * 16 : W_ROWS + 144 + b * 16, :] = quads[:, b, :].astype(BF16)
    out[0, W_ROWS + 192 : W_ROWS + 208, :] = label[...]
    for g in range(1, 4):
        out[g] = out[0]


def project(x, w_ref, q):
    w = jnp.concatenate(
        [
            jnp.concatenate([w_ref[n, :W_ROWS, :], w_ref[n + 1, :W_ROWS, :]], axis=0)
            for n in (4 * q, 4 * q + 2)
        ],
        axis=1,
    )
    return jax.nn.silu(dot(x, w)).astype(BF16)


def attend(x, w_ref, first, u_ref, mixed_ref):
    u_ref[...] = project(x, w_ref, 0)
    v = project(x, w_ref, 1)
    q = project(x, w_ref, 2)
    k = project(x, w_ref, 3)
    for b in range(x.shape[0] // 128):
        lo, hi = b * 128, (b + 1) * 128
        at = max(lo - 128, 0)
        rows = lo + lax.broadcasted_iota(jnp.int32, (128, hi - at), 0)
        cols = at + lax.broadcasted_iota(jnp.int32, (128, hi - at), 1)
        allowed = (cols >= first[lo:hi, :]) & (cols <= rows)
        for h in range(2):
            d0, d1 = h * HEAD, (h + 1) * HEAD
            scores = dot(q[lo:hi, d0:d1], k[at:hi, d0:d1], ((1,), (1,))) * HEAD ** (-0.5)
            weights = jnp.where(allowed, jax.nn.silu(scores), 0.0).astype(BF16)
            mixed_ref[lo:hi, d0:d1] = dot(weights, v[at:hi, d0:d1])


def half_body(x_ref, w_ref, first_ref, u_ref, mixed_ref, o_ref, g_ref, label_ref):
    for n in range(8):
        o_ref[:, n * LANES : (n + 1) * LANES] = w_ref[
            :, W_ROWS + n * 16 : W_ROWS + (n + 1) * 16, :
        ].reshape(256, LANES)
    for n in range(4):
        g_ref[:, n * LANES : (n + 1) * LANES] = w_ref[
            :, W_ROWS + 128 + n * 16 : W_ROWS + 144 + n * 16, :
        ].reshape(256, LANES)
    for n in range(PLANE):
        label_ref[n : n + 1, :] = w_ref[n, W_ROWS + 192 : W_ROWS + 208, :].astype(F32)[0:1, :]
    attend(x_ref[...], w_ref, first_ref[...], u_ref, mixed_ref)


def gated_out(rows, u0, m0, o0, u1, m1, o1, gain_ref):
    a, b = m0[...], m1[...]
    width = 512.0
    center = (jnp.sum(a, axis=1, keepdims=True) + jnp.sum(b, axis=1, keepdims=True)) / width
    a, b = a - center, b - center
    spread = (
        jnp.sum(a * a, axis=1, keepdims=True) + jnp.sum(b * b, axis=1, keepdims=True)
    ) / width
    inv = lax.rsqrt(spread + norm_epsilon)
    ga = (a * inv * gain_ref[:, 0:256] * u0[...].astype(F32)).astype(BF16)
    gb = (b * inv * gain_ref[:, 256:512] * u1[...].astype(F32)).astype(BF16)
    delta = dot(ga, o0[...]) + dot(gb, o1[...])
    return (rows.astype(F32) + delta).astype(BF16)


def out_body(tok_ref, u0, m0, o0, u1, m1, o1, gain_ref, out_ref):
    out_ref[...] = gated_out(tok_ref[...], u0, m0, o0, u1, m1, o1, gain_ref)


def worker_body(
    lands, lowers, got_ref, order_ref, in_gain, w0, w1, o0, o1, gain_ref, out_ref, u0, u1, m0, m1
):
    at = lax.broadcasted_iota(jnp.int32, (256, ROWS), 0)
    here = at == lands[...]
    first = jnp.sum(jnp.where(here, lowers[...], 0.0), axis=1, keepdims=True).astype(jnp.int32)
    rows = dot(jnp.where(here, 1.0, 0.0).astype(BF16), got_ref[...]).astype(BF16)
    normed = layer_norm(rows.astype(F32), in_gain[...]).astype(BF16)
    x = dot(normed, order_ref[...]).astype(BF16)
    attend(x, w0, first, u0, m0)
    attend(x, w1, first, u1, m1)
    out_ref[...] = gated_out(rows, u0, m0, o0, u1, m1, o1, gain_ref)


def loss_body(core, out_ref, low_ref, g0_ref, g1_ref, pos_ref, weight_ref, grad_ref, own_ref, send_ref, own_inner, terms):
    c = core[0]

    g0, g1 = g0_ref[...].astype(F32), g1_ref[...].astype(F32)
    size = (jnp.sum(g0 * g0, axis=1, keepdims=True) + jnp.sum(g1 * g1, axis=1, keepdims=True)) / WIDTH
    scale = lax.rsqrt(size + scale_epsilon)
    g0, g1 = (g0 * scale).astype(BF16), (g1 * scale).astype(BF16)
    here = c == 0
    both = jnp.concatenate([jnp.where(here, g0, g1), jnp.where(here, g1, g0)], axis=1)
    row = lax.broadcasted_iota(jnp.int32, (256, 256), 0)
    col = lax.broadcasted_iota(jnp.int32, (256, 256), 1)
    swap = jnp.where(col == (row % 16) * 16 + row // 16, 1.0, 0.0).astype(BF16)
    group = dot(swap, both).astype(BF16)
    rows = jnp.concatenate([low_ref[...], group], axis=0)

    out = out_ref[...].astype(F32)
    out_scale = lax.rsqrt(jnp.mean(out * out, axis=1, keepdims=True) + scale_epsilon)
    hat = out * out_scale
    low = hat.astype(BF16)
    factor = inverse_temp / WIDTH
    raw = dot(low, rows, ((1,), (1,)))
    hit = lax.broadcasted_iota(jnp.int32, (ROWS, 256), 1) == pos_ref[...]
    pos = jnp.exp(jnp.sum(jnp.where(hit, raw[:, :256], 0.0), axis=1, keepdims=True) * factor)
    neg = jnp.exp(raw[:, 256:] * factor)
    total = pos + jnp.sum(neg, axis=1, keepdims=True)
    weight = weight_ref[...]
    pos_grad = weight * (pos / total - 1.0)
    grads = jnp.concatenate(
        [jnp.where(hit, pos_grad, 0.0).astype(BF16), (weight * neg / total).astype(BF16)], axis=1
    )
    grad_hat = dot(grads, rows) * factor
    inner = jnp.mean(grad_hat * hat, axis=1, keepdims=True)
    grad_ref[...] = ((grad_hat - hat * inner) * out_scale).astype(BF16)
    sums = dot(low, grads, ((0,), (0,))) * factor
    terms[...] = sums.astype(BF16).reshape(PLANE, 2, 32, ROWS)
    for k in range(PLANE):
        own_ref[k] = terms[k, c]
        send_ref[k * 32 : (k + 1) * 32, :] = terms[k, 1 - c]
    products = jnp.sum(grads.astype(F32) * raw, axis=0, keepdims=True) * factor
    own_inner[...] = products
    top = products.astype(BF16).astype(F32)
    send_ref[512:528, :] = split_rows(top, products - top).astype(BF16)


def split_rows(top, rest):
    at = lax.broadcasted_iota(jnp.int32, (16, ROWS), 0)
    return jnp.where(at == 0, top, jnp.where(at == 1, rest, 0.0))


def pair_body(own_ref, inner_ref, got_ref, out_ref):
    other = got_ref[512:528, :].astype(F32)
    inner = inner_ref[...] + other[0:1, :] + other[1:2, :]
    top = inner.astype(BF16).astype(F32)
    tail = split_rows(top, inner - top).astype(BF16)
    for k in range(PLANE):
        mine = own_ref[k].astype(F32) + got_ref[k * 32 : (k + 1) * 32, :].astype(F32)
        out_ref[k, 0:32, :] = mine.astype(BF16)
        out_ref[k, 32:40, :] = tail[0:8, :]


def plane_body(got_ref, pos_ref, neg_ref):
    acc = got_ref[0].astype(F32)
    for k in range(1, PLANE):
        acc = acc + got_ref[k].astype(F32)
    inner = acc[32:33, :] + acc[33:34, :]
    top = inner.astype(BF16).astype(F32)
    full = jnp.concatenate([acc[0:32, :], split_rows(top, inner - top)], axis=0)
    pos_ref[...] = full[:, 0:256]
    tail = jnp.concatenate([full[:, 256:512], jnp.zeros((80, 256), F32)], axis=0)
    neg_ref[...] = jnp.transpose(tail).astype(BF16)


def item_body(pos_ref, hits_ref, got_ref, hat_ref, scale_ref, out_ref):
    total = pos_ref[...] + dot(got_ref[...], hits_ref[...], ((0,), (0,)))[0:48, :]
    inner = (total[32:33, :] + total[33:34, :]) / WIDTH
    out_ref[...] = (total[0:32, :] - hat_ref[...] * inner) * scale_ref[...]


def layer_norm(values, gain):
    center = jnp.mean(values, axis=-1, keepdims=True)
    shifted = values - center
    spread = jnp.mean(shifted * shifted, axis=-1, keepdims=True)
    return shifted * lax.rsqrt(spread + norm_epsilon) * gain


def copies(block, count):
    return jnp.broadcast_to(block[None], (count, *block.shape))


def exchange(blocks, axis, groups=None):
    return lax.all_to_all(blocks, axis, 0, 0, tiled=True, axis_index_groups=groups)


def per_device(
    tokens,
    lengths,
    destination,
    worker_offset,
    positives,
    negatives,
    table,
    in_gain,
    w_uvqk,
    out_gain,
    w_out,
):
    item = lax.axis_index("item")
    user = lax.axis_index("user")
    x, y, core = user // 8, (user // 2) % 4, user % 2
    place = jnp.where(core == 0, y * 4 + x, x * 4 + y)
    item_rows = table.shape[0]

    chunk, half = place // 2, place % 2
    block = (chunk // 2) * 4 + core * 2 + chunk % 2
    w_part = lax.dynamic_slice(w_uvqk, (half * 32, block * LANES), (32, LANES))
    o_part = lax.dynamic_slice(w_out, (core * 256 + place * 16, 0), (16, 64))
    o_part = jnp.concatenate([o_part[:8], o_part[8:]], axis=1)
    ids = lax.dynamic_slice(negatives, (0, item * 16 + place), (ITEMS, 1)) - item * item_rows
    pick = (ids == jnp.arange(item_rows, dtype=jnp.int32)[None, :]).astype(BF16)
    g_part = jnp.dot(pick, lax.dynamic_slice(table, (0, core * 512), (item_rows, 512)))
    first_message = jnp.concatenate(
        [
            copies(jnp.concatenate([w_part, o_part], axis=0), ITEMS),
            jnp.pad(g_part.reshape(ITEMS, 4, LANES), ((0, 0), (0, 4), (0, 0))),
        ],
        axis=1,
    )
    got = exchange(first_message, "item")

    history_len = lengths[0]
    home_start = jnp.cumsum(history_len) - history_len
    row_ids = jnp.arange(ROWS, dtype=jnp.int32)
    inside = (row_ids[:, None] >= home_start[None, :]) & (
        row_ids[:, None] < (home_start + history_len)[None, :]
    )
    valid = jnp.any(inside, axis=1, keepdims=True)
    first = jnp.where(
        valid,
        jnp.sum(jnp.where(inside, home_start[None, :], 0), axis=1, keepdims=True),
        row_ids[:, None],
    )
    weight = jnp.where(valid, loss_scale, 0.0).astype(F32)
    peers = jnp.arange(USERS, dtype=jnp.int32)
    chosen = (destination[0][None, :] == peers[:, None]).astype(jnp.int32)
    first_row = jnp.sum(chosen * home_start[None, :], axis=1)
    count = jnp.sum(chosen * history_len[None, :], axis=1)
    landing = jnp.sum(chosen * worker_offset[0][None, :], axis=1)
    label = jnp.concatenate([landing, count, jnp.zeros((64,), jnp.int32)]).astype(BF16)
    labels = jnp.broadcast_to(label[None], (16, LANES))
    within = jnp.arange(MOST, dtype=jnp.int32)
    source = jnp.where(within[None, :] < count[:, None], first_row[:, None] + within[None, :], -1)
    send = (source.reshape(-1)[:, None] == row_ids[None, :]).astype(BF16)

    normed = layer_norm(tokens.astype(F32), in_gain).astype(BF16)
    at = jnp.arange(WIDTH, dtype=jnp.int32)
    wanted = (at % 512) // 32 * 64 + at // 512 * 32 + at % 32
    order = (at[:, None] == wanted[None, :]).astype(BF16)
    normed = jnp.dot(normed, order, preferred_element_type=F32).astype(BF16)
    parcels = jnp.dot(send, tokens, preferred_element_type=F32).astype(BF16)
    got, normed, first, labels = lax.optimization_barrier((got, normed, first, labels))

    message = call(forward_body, shape((4, W_ROWS + REST, LANES)), [VMEM, VMEM])(got, labels)
    mid = exchange(message, "user", FIRST)
    mid = mid.reshape(4 * (W_ROWS + REST), LANES)
    held = exchange(copies(mid, 4), "user", SECOND).reshape(PLANE, W_ROWS + REST, LANES)

    table_f = table.astype(F32)
    table_scale = lax.rsqrt(jnp.mean(table_f * table_f, axis=1, keepdims=True) + scale_epsilon)
    table_hat = table_f * table_scale
    table_low = table_hat.astype(BF16)
    positive_local = (positives - item * item_rows)[:, None]
    owned_ids = lax.dynamic_slice_in_dim(negatives, item * 16, 16, 1) - item * item_rows
    hits = (
        owned_ids.reshape(-1)[:, None] == jnp.arange(item_rows, dtype=jnp.int32)[None, :]
    ).astype(BF16)
    hat_part = lax.dynamic_slice_in_dim(table_hat, user * 32, 32, 1).T
    table_scale = table_scale.reshape(1, item_rows)
    gain = jnp.where(core == 0, out_gain, jnp.roll(out_gain, 256))[None]
    held, parcels, order, positive_local, weight, table_low, table_scale, hits, hat_part, gain = (
        lax.optimization_barrier(
            (
                held,
                parcels,
                order,
                positive_local,
                weight,
                table_low,
                table_scale,
                hits,
                hat_part,
                gain,
            )
        )
    )
    held_other = lax.ppermute(held, "user", PARTNER)
    arrived = exchange(parcels.reshape(USERS, MOST, WIDTH), "user").reshape(ROWS, WIDTH)

    layer_half = call(
        half_body,
        (
            shape((ROWS, 256)),
            shape((ROWS, 256), F32),
            shape((256, WIDTH)),
            shape((256, 512)),
            shape((PLANE, LANES), F32),
        ),
        [VMEM] * 3,
        mib=12,
    )
    u_own, mixed_own, o_own, g_own, near = layer_half(normed, held, first)
    u_other, mixed_other, o_other, g_other, far = layer_half(normed, held_other, first)
    home_out = call(out_body, shape((ROWS, WIDTH)), [VMEM] * 8, mib=8)(
        tokens, u_own, mixed_own, o_own, u_other, mixed_other, o_other, gain
    )

    token_grad, own, sent, own_inner = call(
        loss_body,
        (
            shape((ROWS, WIDTH)),
            shape((PLANE, 32, ROWS)),
            shape((528, ROWS)),
            shape((1, ROWS), F32),
        ),
        [SMEM] + [VMEM] * 6,
        scratch=[pltpu.VMEM((PLANE, 2, 32, ROWS), BF16)],
        mib=16,
    )(core.reshape(1), home_out, table_low, g_own, g_other, positive_local, weight)
    partner_terms = lax.ppermute(sent, "user", PARTNER)
    pair = call(pair_body, shape((PLANE, 40, ROWS)), [VMEM] * 3)(own, own_inner, partner_terms)
    pair, arrived = lax.optimization_barrier((pair, arrived))
    plane = exchange(pair, "user", SAME_CORE)

    mine = (jnp.arange(LANES, dtype=jnp.int32)[None, :] == user).astype(F32)
    mine_count = (jnp.arange(LANES, dtype=jnp.int32)[None, :] == user + USERS).astype(F32)

    def by_user(select):
        a = jnp.sum(near * select, axis=1)
        b = jnp.sum(far * select, axis=1)
        even = jnp.where(core == 0, a, b).reshape(4, 4).T
        uneven = jnp.where(core == 0, b, a).reshape(4, 4)
        return jnp.stack([even, uneven], axis=2).reshape(USERS).astype(jnp.int32)

    lower, arrived_count = by_user(mine), by_user(mine_count)
    lands = jnp.where(within[None, :] < arrived_count[:, None], lower[:, None] + within[None, :], -1)
    lowers = jnp.broadcast_to(lower[:, None], (USERS, MOST)).astype(F32)
    layer_out = call(
        worker_body,
        shape((256, WIDTH)),
        [VMEM] * 10,
        scratch=[
            pltpu.VMEM((256, 256), BF16),
            pltpu.VMEM((256, 256), BF16),
            pltpu.VMEM((256, 256), F32),
            pltpu.VMEM((256, 256), F32),
        ],
        mib=12,
    )(
        lands.reshape(1, ROWS),
        lowers.reshape(1, ROWS),
        arrived,
        order,
        in_gain[None],
        held,
        held_other,
        o_own,
        o_other,
        gain,
    )

    positive_part, negative_part = call(
        plane_body, (shape((48, 256), F32), shape((256, LANES))), [VMEM]
    )(plane)
    owned = exchange(negative_part.reshape(ITEMS, 16, LANES), "item").reshape(256, LANES)
    item_grad = call(item_body, shape((32, 256), F32), [VMEM] * 5)(
        positive_part, hits, owned, hat_part, table_scale
    ).T
    return (layer_out, token_grad, item_grad)


def solution(mesh):
    return jax.shard_map(
        per_device,
        mesh=mesh,
        in_specs=(
            P(("user", "item"), None),
            P(("user", "item"), None),
            P(("user", "item"), None),
            P(("user", "item"), None),
            P(("user", "item")),
            P(),
            P("item", None),
            P(),
            P("item", None),
            P(),
            P(None, "item"),
        ),
        out_specs=(P(("user", "item"), None), P(("user", "item"), None), P("item", "user")),
        check_vma=False,
    )
```

```python
import jax
import jax.numpy as jnp
from jax import lax
from jax.experimental import pallas as pl
from jax.experimental.pallas import tpu as pltpu
from jax.sharding import PartitionSpec as P


norm_epsilon = 1e-05
scale_epsilon = 1e-06
inverse_temp = 20.0
loss_scale = 32.0

F32 = jnp.float32
BF16 = jnp.bfloat16

USERS = 32
ITEMS = 16
PLANE = 16
LANES = 128
ROWS = 512
MOST = 16
WIDTH = 1024
HEAD = 128

FIRST = [[x * 8 + y * 2 for x in range(4)] for y in range(4)] + [
    [x * 8 + y * 2 + 1 for y in range(4)] for x in range(4)
]
SECOND = [[x * 8 + y * 2 for y in range(4)] for x in range(4)] + [
    [x * 8 + y * 2 + 1 for x in range(4)] for y in range(4)
]
PIECE = 4 * 720


def shifted(groups, step):
    return [(g[n], g[(n + step) % 4]) for g in groups for n in range(4)]


SAME_CORE = [[k * 2 + c for k in range(PLANE)] for c in range(2)]
PARTNER = [(k, k ^ 1) for k in range(USERS)]

VMEM = pl.BlockSpec(memory_space=pltpu.VMEM)
ANY = pl.BlockSpec(memory_space=pl.ANY)
HBM = pl.BlockSpec(memory_space=pltpu.HBM)
SMEM = pl.BlockSpec(memory_space=pltpu.SMEM)
W_ROWS = 512
REST = 208


def shape(dims, kind=BF16):
    return jax.ShapeDtypeStruct(dims, kind)


def dot(a, b, contract=((1,), (0,))):
    return lax.dot_general(a, b, (contract, ((), ())), preferred_element_type=F32)


def call(body, outs, specs, scratch=(), mib=8, out_specs=None):
    return pl.pallas_call(
        body,
        out_shape=outs,
        in_specs=specs,
        out_specs=out_specs or jax.tree.map(lambda _: VMEM, outs),
        scratch_shapes=list(scratch),
        compiler_params=pltpu.CompilerParams(vmem_limit_bytes=mib * 2**20),
    )


def column_of(row, n):
    eye = lax.broadcasted_iota(jnp.int32, (n, n), 0) == lax.broadcasted_iota(jnp.int32, (n, n), 1)
    return jnp.sum(jnp.where(eye, row, 0.0), axis=1, keepdims=True)


def reordered(rows):
    at = lax.broadcasted_iota(jnp.int32, (1, WIDTH), 1)
    wanted = (at % 512) // 32 * 64 + at // 512 * 32 + at % 32
    order = lax.broadcasted_iota(jnp.int32, (WIDTH, WIDTH), 0) == wanted
    return dot(rows, jnp.where(order, 1.0, 0.0).astype(BF16)).astype(BF16)


def message_body(
    where, neg_ref, w_ref, o_ref, table_ref, out_ref, w_part, o_part, rows, turned, quads, sems
):
    item, core, place = where[0], where[1], where[2]
    chunk = lax.div(place, 2)
    block = lax.div(chunk, 2) * 4 + core * 2 + lax.rem(chunk, 2)
    copies = (
        pltpu.make_async_copy(
            w_ref.at[pl.ds((place % 2) * 32, 32), pl.ds(block * LANES, LANES)], w_part, sems.at[0]
        ),
        pltpu.make_async_copy(
            o_ref.at[:, pl.ds((core * 2 + place // 8) * LANES, LANES)], o_part, sems.at[1]
        ),
        pltpu.make_async_copy(table_ref.at[:, pl.ds(core * 512, 512)], rows, sems.at[2]),
    )
    for copy in copies:
        copy.start()
    lane = lax.broadcasted_iota(jnp.int32, (ITEMS, 256), 1)
    ids = jnp.sum(
        jnp.where(lane == item * 16 + place, neg_ref[...].astype(F32), 0.0), axis=1, keepdims=True
    ).astype(jnp.int32)
    pick = jnp.where(lane == ids - item * 256, 1.0, 0.0).astype(BF16)
    for copy in copies:
        copy.wait()
    turned[...] = jnp.transpose(o_part[...].astype(F32))
    part = turned[pl.ds((place % 8) * 16, 16), :]
    part = jnp.concatenate([part[0:8, :], part[8:16, :]], axis=1).astype(BF16)
    group = dot(pick, rows[...])
    quads[...] = jnp.zeros_like(quads)
    for b in range(4):
        quads[:, b, :] = group[:, b * LANES : (b + 1) * LANES]
    for i in range(ITEMS):
        out_ref[i, 0:32, :] = w_part[...]
        out_ref[i, 32:40, :] = part
    out_ref[:, 40:48, :] = quads[...].astype(BF16)


def prepare_body(
    where,
    tok_ref,
    len_ref,
    dest_ref,
    off_ref,
    pos_ref,
    in_gain,
    table_ref,
    neg_ref,
    x_ref,
    cols_ref,
    label_ref,
    parcel_ref,
    low_ref,
    hat_ref,
    scale_ref,
    hits_ref,
    tok,
    tab,
    hat,
    turned,
    sems,
):
    item, user = where[0], where[3]
    copies = (
        pltpu.make_async_copy(tok_ref, tok, sems.at[0]),
        pltpu.make_async_copy(table_ref, tab, sems.at[1]),
    )
    for copy in copies:
        copy.start()
    for copy in copies:
        copy.wait()
    normed = layer_norm(tok[...].astype(F32), in_gain[...]).astype(BF16)
    x_ref[...] = reordered(normed)

    lens, dest, off = (r[...].astype(F32) for r in (len_ref, dest_ref, off_ref))
    sub = lax.broadcasted_iota(jnp.int32, (32, 32), 0)
    lane = lax.broadcasted_iota(jnp.int32, (32, 32), 1)
    len_col, dest_col, off_col = (column_of(v, 32) for v in (lens, dest, off))
    start_row = jnp.sum(jnp.where(sub < lane, len_col, 0.0), axis=0, keepdims=True)
    start_col = column_of(start_row, 32)
    row = lax.broadcasted_iota(jnp.int32, (ROWS, 32), 0).astype(F32)
    inside = (row >= start_row) & (row < start_row + lens)
    valid = jnp.sum(jnp.where(inside, 1.0, 0.0), axis=1, keepdims=True) > 0.5
    first = jnp.sum(jnp.where(inside, start_row, 0.0), axis=1, keepdims=True)
    first = jnp.where(valid, first, row[:, 0:1])
    weight = jnp.where(valid, loss_scale, 0.0)
    pos = jnp.transpose(jnp.broadcast_to(pos_ref[...].astype(F32), (LANES, ROWS)))
    at = lax.broadcasted_iota(jnp.int32, (ROWS, LANES), 1)
    local = pos - (item * 256).astype(F32)
    cols_ref[...] = jnp.where(at == 0, first, jnp.where(at == 1, weight, local))

    wide = lax.broadcasted_iota(jnp.int32, (32, LANES), 1).astype(F32)
    to_land = jnp.sum(jnp.where(wide == dest_col, off_col, 0.0), axis=0, keepdims=True)
    to_count = jnp.sum(jnp.where(wide - 32.0 == dest_col, len_col, 0.0), axis=0, keepdims=True)
    label_ref[...] = jnp.broadcast_to(to_land + to_count, (16, LANES)).astype(BF16)

    lane_f = lane.astype(F32)
    first_row = jnp.sum(jnp.where(lane_f == dest_col, start_col, 0.0), axis=0, keepdims=True)
    count_row = jnp.sum(jnp.where(lane_f == dest_col, len_col, 0.0), axis=0, keepdims=True)
    slot = lax.broadcasted_iota(jnp.int32, (ROWS, 32), 0)
    peer = lax.broadcasted_iota(jnp.int32, (ROWS, 32), 1) == slot // MOST
    begin = jnp.sum(jnp.where(peer, first_row, 0.0), axis=1, keepdims=True)
    count = jnp.sum(jnp.where(peer, count_row, 0.0), axis=1, keepdims=True)
    within = (slot[:, 0:1] % MOST).astype(F32)
    source = jnp.where(within < count, begin + within, -1.0)
    send = lax.broadcasted_iota(jnp.int32, (ROWS, ROWS), 1).astype(F32) == source
    parcel_ref[...] = dot(jnp.where(send, 1.0, 0.0).astype(BF16), tok[...]).astype(BF16)

    table = tab[...].astype(F32)
    scale = lax.rsqrt(jnp.mean(table * table, axis=1, keepdims=True) + scale_epsilon)
    hat[...] = table * scale
    low_ref[...] = hat[...].astype(BF16)
    turned[...] = jnp.transpose(hat[:, pl.ds((user // 4) * LANES, LANES)])
    hat_ref[...] = turned[pl.ds((user % 4) * 32, 32), :]
    scale_ref[...] = jnp.transpose(jnp.broadcast_to(scale, (256, LANES)))[0:1, :]

    ids = jnp.broadcast_to(neg_ref[...].astype(F32)[:, None, :], (ITEMS, 16, 256)).reshape(256, 256)
    spot = lax.broadcasted_iota(jnp.int32, (256, 256), 0) % 16 + item * 16
    lanes = lax.broadcasted_iota(jnp.int32, (256, 256), 1)
    ids = jnp.sum(jnp.where(lanes == spot, ids, 0.0), axis=1, keepdims=True)
    hits_ref[...] = jnp.where(lanes.astype(F32) == ids - (item * 256).astype(F32), 1.0, 0.0).astype(BF16)


def forward_body(got, label, out):
    for i in range(ITEMS):
        out[i * 32 : (i + 1) * 32, :] = got[i, 0:32, :]
    left = lax.broadcasted_iota(jnp.int32, (8, LANES), 1) < 64
    for b in range(8):
        even, odd = got[2 * b, 32:40, :].astype(F32), got[2 * b + 1, 32:40, :].astype(F32)
        top = jnp.where(left, even, pltpu.roll(odd, 64, 1))
        bottom = jnp.where(left, pltpu.roll(even, 64, 1), odd)
        out[W_ROWS + b * 16 : W_ROWS + (b + 1) * 16, :] = jnp.concatenate(
            [top, bottom], axis=0
        ).astype(BF16)
    quads = got[:, 40:48, :].astype(F32)
    for b in range(4):
        out[W_ROWS + 128 + b * 16 : W_ROWS + 144 + b * 16, :] = quads[:, b, :].astype(BF16)
    out[W_ROWS + 192 : W_ROWS + 208, :] = label[...]


def collect_body(where, p0, p1, p2, p3, out_ref, sems):
    copies = [
        pltpu.make_async_copy(
            p, out_ref.at[lax.rem(where[5] + 4 - n, 4)], sems.at[n]
        )
        for n, p in enumerate((p0, p1, p2, p3))
    ]
    for copy in copies:
        copy.start()
    for copy in copies:
        copy.wait()


def fetches(pieces, w, sems):
    return [pltpu.make_async_copy(p, w.at[n], sems.at[n]) for n, p in enumerate(pieces)]


def kind_of(position, n):
    return lax.rem(position + 4 - n, 4)


def project(x, w, n):
    parts = [w[n, i * 720 : i * 720 + W_ROWS, :] for i in range(4)]
    both = jnp.concatenate(
        [jnp.concatenate(parts[0:2], axis=0), jnp.concatenate(parts[2:4], axis=0)], axis=1
    )
    return jax.nn.silu(dot(x, both)).astype(BF16)


def attend(act, first, mixed_ref):
    v, q, k = act[1], act[2], act[3]
    for b in range(first.shape[0] // 128):
        lo, hi = b * 128, (b + 1) * 128
        at = max(lo - 128, 0)
        rows = lo + lax.broadcasted_iota(jnp.int32, (128, hi - at), 0)
        cols = at + lax.broadcasted_iota(jnp.int32, (128, hi - at), 1)
        allowed = (cols >= first[lo:hi, :]) & (cols <= rows)
        for h in range(2):
            d0, d1 = h * HEAD, (h + 1) * HEAD
            scores = dot(q[lo:hi, d0:d1], k[at:hi, d0:d1], ((1,), (1,))) * HEAD ** (-0.5)
            weights = jnp.where(allowed, jax.nn.silu(scores), 0.0).astype(BF16)
            mixed_ref[lo:hi, d0:d1] = dot(weights, v[at:hi, d0:d1])


def half_body(
    where,
    x_ref,
    p0,
    p1,
    p2,
    p3,
    cols_ref,
    u_ref,
    mixed_ref,
    o_ref,
    g_ref,
    label_ref,
    x,
    w,
    act,
    sems,
):
    copies = fetches((p0, p1, p2, p3), w, sems)
    first_copy = pltpu.make_async_copy(x_ref, x, sems.at[4])
    first_copy.start()
    for copy in copies:
        copy.start()
    first_copy.wait()
    for n, copy in enumerate(copies):
        copy.wait()
        kind = kind_of(where[0], n)
        act[kind] = project(x[...], w, n)
        row = pl.multiple_of(kind * 64, 64)

        def columns(at):
            return jnp.concatenate(
                [w[n, i * 720 + at : i * 720 + at + 16, :] for i in range(4)], axis=0
            )

        for b in range(8):
            o_ref[pl.ds(row, 64), b * LANES : (b + 1) * LANES] = columns(W_ROWS + b * 16)
        for b in range(4):
            g_ref[pl.ds(row, 64), b * LANES : (b + 1) * LANES] = columns(W_ROWS + 128 + b * 16)
        labels = [
            w[n, i * 720 + W_ROWS + 192 : (i + 1) * 720, :].astype(F32)[0:1, :] for i in range(4)
        ]
        label_ref[kind] = jnp.concatenate(labels + [jnp.zeros((4, LANES), F32)], axis=0)
    u_ref[...] = act[0]
    attend(act, cols_ref[:, 0:1].astype(jnp.int32), mixed_ref)


def gated_out(rows, u0, m0, o0, u1, m1, o1, gain_ref):
    a, b = m0[...], m1[...]
    width = 512.0
    center = (jnp.sum(a, axis=1, keepdims=True) + jnp.sum(b, axis=1, keepdims=True)) / width
    a, b = a - center, b - center
    spread = (
        jnp.sum(a * a, axis=1, keepdims=True) + jnp.sum(b * b, axis=1, keepdims=True)
    ) / width
    inv = lax.rsqrt(spread + norm_epsilon)
    ga = (a * inv * gain_ref[:, 0:256] * u0[...].astype(F32)).astype(BF16)
    gb = (b * inv * gain_ref[:, 256:512] * u1[...].astype(F32)).astype(BF16)
    delta = dot(ga, o0[...]) + dot(gb, o1[...])
    return (rows.astype(F32) + delta).astype(BF16)


def out_body(tok_ref, u0, m0, o0, u1, m1, o1, gain_ref, out_ref):
    out_ref[...] = gated_out(tok_ref[...], u0, m0, o0, u1, m1, o1, gain_ref)


def worker_body(where, near_ref, far_ref, got_ref, in_gain, o0, o1, gain_ref, *rest):
    pieces, (out_ref, w0, w1, a0, a1, m0, m1, sems) = rest[:8], rest[8:]
    core, user = where[1], where[3]
    copies = (
        fetches(pieces[:4], w0, sems.at[0]),
        fetches(pieces[4:], w1, sems.at[1]),
    )
    for copy in copies[0] + copies[1]:
        copy.start()
    lane = lax.broadcasted_iota(jnp.int32, (32, LANES), 1)
    sub = lax.broadcasted_iota(jnp.int32, (32, ROWS), 0)
    slot = lax.broadcasted_iota(jnp.int32, (1, ROWS), 1)
    peer = slot // MOST
    x, y, c = peer // 8, peer // 2 % 4, peer % 2
    spot = jnp.where(c == 0, y * 8 + x, x * 8 + y)

    def of_peer(at):
        total = 0.0
        for ref, mine in ((near_ref, c == core), (far_ref, c != core)):
            labels = ref[...].reshape(32, LANES)
            value = jnp.sum(jnp.where(lane == at, labels, 0.0), axis=1, keepdims=True)
            total = total + jnp.sum(
                jnp.where((sub == spot) & mine, value, 0.0), axis=0, keepdims=True
            )
        return total

    lower, count = of_peer(user), of_peer(user + USERS)
    within = (slot % MOST).astype(F32)
    lands = jnp.where(within < count, lower + within, -1.0)
    here = lax.broadcasted_iota(jnp.int32, (256, ROWS), 0).astype(F32) == lands
    first = jnp.sum(jnp.where(here, lower, 0.0), axis=1, keepdims=True).astype(jnp.int32)
    rows = dot(jnp.where(here, 1.0, 0.0).astype(BF16), got_ref[...]).astype(BF16)
    normed = layer_norm(rows.astype(F32), in_gain[...]).astype(BF16)
    moved = reordered(normed)
    for position, group, w, act, mixed in (
        (where[4], copies[0], w0, a0, m0),
        (where[5], copies[1], w1, a1, m1),
    ):
        for n, copy in enumerate(group):
            copy.wait()
            act[kind_of(position, n)] = project(moved, w, n)
        attend(act, first, mixed)
    out_ref[...] = gated_out(rows, a0.at[0], m0, o0, a1.at[0], m1, o1, gain_ref)


def loss_body(core, out_ref, low_ref, g0_ref, g1_ref, cols_ref, grad_ref, own_ref, send_ref, own_inner, terms):
    c = core[0]

    g0, g1 = g0_ref[...].astype(F32), g1_ref[...].astype(F32)
    size = (jnp.sum(g0 * g0, axis=1, keepdims=True) + jnp.sum(g1 * g1, axis=1, keepdims=True)) / WIDTH
    scale = lax.rsqrt(size + scale_epsilon)
    g0, g1 = (g0 * scale).astype(BF16), (g1 * scale).astype(BF16)
    here = c == 0
    both = jnp.concatenate([jnp.where(here, g0, g1), jnp.where(here, g1, g0)], axis=1)
    row = lax.broadcasted_iota(jnp.int32, (256, 256), 0)
    col = lax.broadcasted_iota(jnp.int32, (256, 256), 1)
    swap = jnp.where(col == (row % 16) * 16 + row // 16, 1.0, 0.0).astype(BF16)
    group = dot(swap, both).astype(BF16)
    rows = jnp.concatenate([low_ref[...], group], axis=0)

    out = out_ref[...].astype(F32)
    out_scale = lax.rsqrt(jnp.mean(out * out, axis=1, keepdims=True) + scale_epsilon)
    hat = out * out_scale
    low = hat.astype(BF16)
    factor = inverse_temp / WIDTH
    raw = dot(low, rows, ((1,), (1,)))
    hit = lax.broadcasted_iota(jnp.int32, (ROWS, 256), 1) == cols_ref[:, 2:3].astype(jnp.int32)
    pos = jnp.exp(jnp.sum(jnp.where(hit, raw[:, :256], 0.0), axis=1, keepdims=True) * factor)
    neg = jnp.exp(raw[:, 256:] * factor)
    total = pos + jnp.sum(neg, axis=1, keepdims=True)
    weight = cols_ref[:, 1:2]
    pos_grad = weight * (pos / total - 1.0)
    grads = jnp.concatenate(
        [jnp.where(hit, pos_grad, 0.0).astype(BF16), (weight * neg / total).astype(BF16)], axis=1
    )
    grad_hat = dot(grads, rows) * factor
    inner = jnp.mean(grad_hat * hat, axis=1, keepdims=True)
    grad_ref[...] = ((grad_hat - hat * inner) * out_scale).astype(BF16)
    sums = dot(low, grads, ((0,), (0,))) * factor
    terms[...] = sums.astype(BF16).reshape(PLANE, 2, 32, ROWS)
    for k in range(PLANE):
        own_ref[k] = terms[k, c]
        send_ref[k * 32 : (k + 1) * 32, :] = terms[k, 1 - c]
    products = jnp.sum(grads.astype(F32) * raw, axis=0, keepdims=True) * factor
    own_inner[...] = products
    top = products.astype(BF16).astype(F32)
    send_ref[512:528, :] = split_rows(top, products - top).astype(BF16)


def split_rows(top, rest):
    at = lax.broadcasted_iota(jnp.int32, (16, ROWS), 0)
    return jnp.where(at == 0, top, jnp.where(at == 1, rest, 0.0))


def pair_body(own_ref, inner_ref, got_ref, out_ref):
    other = got_ref[512:528, :].astype(F32)
    inner = inner_ref[...] + other[0:1, :] + other[1:2, :]
    top = inner.astype(BF16).astype(F32)
    tail = split_rows(top, inner - top).astype(BF16)
    for k in range(PLANE):
        mine = own_ref[k].astype(F32) + got_ref[k * 32 : (k + 1) * 32, :].astype(F32)
        out_ref[k, 0:32, :] = mine.astype(BF16)
        out_ref[k, 32:40, :] = tail[0:8, :]


def plane_body(got_ref, pos_ref, neg_ref):
    acc = got_ref[0].astype(F32)
    for k in range(1, PLANE):
        acc = acc + got_ref[k].astype(F32)
    inner = acc[32:33, :] + acc[33:34, :]
    top = inner.astype(BF16).astype(F32)
    full = jnp.concatenate([acc[0:32, :], split_rows(top, inner - top)], axis=0)
    pos_ref[...] = full[:, 0:256]
    tail = jnp.concatenate([full[:, 256:512], jnp.zeros((80, 256), F32)], axis=0)
    neg_ref[...] = jnp.transpose(tail).astype(BF16)


def item_body(pos_ref, hits_ref, got_ref, hat_ref, scale_ref, out_ref):
    total = pos_ref[...] + dot(got_ref[...], hits_ref[...], ((0,), (0,)))[0:48, :]
    inner = (total[32:33, :] + total[33:34, :]) / WIDTH
    out_ref[...] = (total[0:32, :] - hat_ref[...] * inner) * scale_ref[...]


def layer_norm(values, gain):
    center = jnp.mean(values, axis=-1, keepdims=True)
    shifted = values - center
    spread = jnp.mean(shifted * shifted, axis=-1, keepdims=True)
    return shifted * lax.rsqrt(spread + norm_epsilon) * gain


def in_hbm(values):
    return pltpu.with_memory_space_constraint(values, pltpu.HBM)


def exchange(blocks, axis, groups=None):
    return lax.all_to_all(blocks, axis, 0, 0, tiled=True, axis_index_groups=groups)


def per_device(
    tokens,
    lengths,
    destination,
    worker_offset,
    positives,
    negatives,
    table,
    in_gain,
    w_uvqk,
    out_gain,
    w_out,
):
    item = lax.axis_index("item")
    user = lax.axis_index("user")
    core = user & 1
    x, y = user >> 3, (user >> 1) & 3
    place = jnp.where(core == 0, y * 4 + x, x * 4 + y)
    second = jnp.where(core == 0, y, x)
    first = jnp.where(core == 0, x, y)
    where = jnp.stack([item, core, place, user, second, first]).astype(jnp.int32)

    first_message = call(
        message_body,
        shape((ITEMS, 48, LANES)),
        [SMEM, VMEM, HBM, HBM, HBM],
        scratch=[
            pltpu.VMEM((32, LANES), BF16),
            pltpu.VMEM((64, LANES), BF16),
            pltpu.VMEM((256, 512), BF16),
            pltpu.VMEM((LANES, 64), F32),
            pltpu.VMEM((ITEMS, 8, LANES), F32),
            pltpu.SemaphoreType.DMA((3,)),
        ],
    )(where, negatives, in_hbm(w_uvqk), in_hbm(w_out.T), in_hbm(table))
    got = exchange(first_message, "item")

    x_rows, cols, labels, parcels, table_low, hat_part, table_scale, hits = call(
        prepare_body,
        (
            shape((ROWS, WIDTH)),
            shape((ROWS, LANES), F32),
            shape((16, LANES)),
            shape((ROWS, WIDTH)),
            shape((256, WIDTH)),
            shape((32, 256), F32),
            shape((1, 256), F32),
            shape((256, 256)),
        ),
        [SMEM, HBM] + [VMEM] * 5 + [HBM, VMEM],
        scratch=[
            pltpu.VMEM((ROWS, WIDTH), BF16),
            pltpu.VMEM((256, WIDTH), BF16),
            pltpu.VMEM((256, WIDTH), F32),
            pltpu.VMEM((LANES, 256), F32),
            pltpu.SemaphoreType.DMA((2,)),
        ],
        mib=24,
    )(
        where,
        in_hbm(tokens),
        lengths,
        destination,
        worker_offset,
        positives[None],
        in_gain[None],
        in_hbm(table),
        negatives,
    )
    gain = jnp.where(core == 0, out_gain, jnp.roll(out_gain, 256))[None]
    got, x_rows, gain = lax.optimization_barrier((got, x_rows, gain))

    message = call(forward_body, shape((W_ROWS + REST, LANES)), [VMEM, VMEM])(got, labels)
    line = [message]
    for step in (1, 3, 2):
        line.append(lax.ppermute(message, "user", shifted(FIRST, step)))
    line = [line[0], line[1], line[3], line[2]]
    mid = call(
        collect_body,
        shape((4, W_ROWS + REST, LANES)),
        [SMEM] + [ANY] * 4,
        scratch=[pltpu.SemaphoreType.DMA((4,))],
        out_specs=VMEM,
    )(where, *line).reshape(PIECE, LANES)
    mid, parcels = lax.optimization_barrier((mid, parcels))
    own = {0: mid}
    for step in (1, 3, 2):
        own[step] = lax.ppermute(mid, "user", shifted(SECOND, step))
    other = {}
    for step in (0, 1, 3, 2):
        other[step] = lax.ppermute(own[step], "user", PARTNER)
    own, other = ([d[n] for n in range(4)] for d in (own, other))
    _, parcels = lax.optimization_barrier((own[2], parcels))
    arrived = exchange(parcels.reshape(USERS, MOST, WIDTH), "user").reshape(ROWS, WIDTH)

    layer_half = call(
        half_body,
        (
            shape((ROWS, 256)),
            shape((ROWS, 256), F32),
            shape((256, WIDTH)),
            shape((256, 512)),
            shape((4, 8, LANES), F32),
        ),
        [SMEM] + [ANY] * 5 + [VMEM],
        scratch=[
            pltpu.VMEM((ROWS, WIDTH), BF16),
            pltpu.VMEM((4, PIECE, LANES), BF16),
            pltpu.VMEM((4, ROWS, 256), BF16),
            pltpu.SemaphoreType.DMA((5,)),
        ],
        mib=16,
    )
    u_own, mixed_own, o_own, g_own, near = layer_half(where[4:5], x_rows, *own, cols)
    u_other, mixed_other, o_other, g_other, far = layer_half(where[5:6], x_rows, *other, cols)
    home_out = call(out_body, shape((ROWS, WIDTH)), [VMEM] * 8, mib=8)(
        tokens, u_own, mixed_own, o_own, u_other, mixed_other, o_other, gain
    )

    token_grad, own_terms, sent, own_inner = call(
        loss_body,
        (
            shape((ROWS, WIDTH)),
            shape((PLANE, 32, ROWS)),
            shape((528, ROWS)),
            shape((1, ROWS), F32),
        ),
        [SMEM] + [VMEM] * 5,
        scratch=[pltpu.VMEM((PLANE, 2, 32, ROWS), BF16)],
        mib=16,
    )(core.reshape(1), home_out, table_low, g_own, g_other, cols)
    partner_terms = lax.ppermute(sent, "user", PARTNER)
    pair = call(pair_body, shape((PLANE, 40, ROWS)), [VMEM] * 3)(
        own_terms, own_inner, partner_terms
    )
    pair, arrived = lax.optimization_barrier((pair, arrived))
    plane = exchange(pair, "user", SAME_CORE)

    layer_out = call(
        worker_body,
        shape((256, WIDTH)),
        [SMEM] + [VMEM] * 7 + [ANY] * 8,
        scratch=[
            pltpu.VMEM((4, PIECE, LANES), BF16),
            pltpu.VMEM((4, PIECE, LANES), BF16),
            pltpu.VMEM((4, 256, 256), BF16),
            pltpu.VMEM((4, 256, 256), BF16),
            pltpu.VMEM((256, 256), F32),
            pltpu.VMEM((256, 256), F32),
            pltpu.SemaphoreType.DMA((2, 4)),
        ],
        mib=24,
    )(where, near, far, arrived, in_gain[None], o_own, o_other, gain, *own, *other)

    positive_part, negative_part = call(
        plane_body, (shape((48, 256), F32), shape((256, LANES))), [VMEM]
    )(plane)
    owned = exchange(negative_part.reshape(ITEMS, 16, LANES), "item").reshape(256, LANES)
    item_grad = call(item_body, shape((32, 256), F32), [VMEM] * 5)(
        positive_part, hits, owned, hat_part, table_scale
    ).T
    return (layer_out, token_grad, item_grad)


def solution(mesh):
    return jax.shard_map(
        per_device,
        mesh=mesh,
        in_specs=(
            P(("user", "item"), None),
            P(("user", "item"), None),
            P(("user", "item"), None),
            P(("user", "item"), None),
            P(("user", "item")),
            P(),
            P("item", None),
            P(),
            P("item", None),
            P(),
            P(None, "item"),
        ),
        out_specs=(P(("user", "item"), None), P(("user", "item"), None), P("item", "user")),
        check_vma=False,
    )
```

```python
import jax
import jax.numpy as jnp
from jax import lax
from jax.experimental import pallas as pl
from jax.experimental.pallas import tpu as pltpu
from jax.sharding import PartitionSpec as P


norm_epsilon = 1e-05
scale_epsilon = 1e-06
inverse_temp = 20.0
loss_scale = 32.0

F32 = jnp.float32
BF16 = jnp.bfloat16

USERS = 32
ITEMS = 16
PLANE = 16
LANES = 128
ROWS = 512
MOST = 16
WIDTH = 1024
HEAD = 128

FIRST = [[x * 8 + y * 2 for x in range(4)] for y in range(4)] + [
    [x * 8 + y * 2 + 1 for y in range(4)] for x in range(4)
]
SECOND = [[x * 8 + y * 2 for y in range(4)] for x in range(4)] + [
    [x * 8 + y * 2 + 1 for x in range(4)] for y in range(4)
]
PIECE = 4 * 720


def shifted(groups, step):
    return [(g[n], g[(n + step) % 4]) for g in groups for n in range(4)]


SAME_CORE = [[k * 2 + c for k in range(PLANE)] for c in range(2)]
PARTNER = [(k, k ^ 1) for k in range(USERS)]

VMEM = pl.BlockSpec(memory_space=pltpu.VMEM)
ANY = pl.BlockSpec(memory_space=pl.ANY)
HBM = pl.BlockSpec(memory_space=pltpu.HBM)
SMEM = pl.BlockSpec(memory_space=pltpu.SMEM)
W_ROWS = 512
REST = 208


def shape(dims, kind=BF16):
    return jax.ShapeDtypeStruct(dims, kind)


def dot(a, b, contract=((1,), (0,))):
    return lax.dot_general(a, b, (contract, ((), ())), preferred_element_type=F32)


def call(body, outs, specs, scratch=(), mib=8, out_specs=None):
    return pl.pallas_call(
        body,
        out_shape=outs,
        in_specs=specs,
        out_specs=out_specs or jax.tree.map(lambda _: VMEM, outs),
        scratch_shapes=list(scratch),
        compiler_params=pltpu.CompilerParams(vmem_limit_bytes=mib * 2**20),
    )


def column_of(row, n):
    eye = lax.broadcasted_iota(jnp.int32, (n, n), 0) == lax.broadcasted_iota(jnp.int32, (n, n), 1)
    return jnp.sum(jnp.where(eye, row, 0.0), axis=1, keepdims=True)


def reordered(rows):
    at = lax.broadcasted_iota(jnp.int32, (1, WIDTH), 1)
    wanted = (at % 512) // 32 * 64 + at // 512 * 32 + at % 32
    order = lax.broadcasted_iota(jnp.int32, (WIDTH, WIDTH), 0) == wanted
    return dot(rows, jnp.where(order, 1.0, 0.0).astype(BF16)).astype(BF16)


def message_body(
    where, neg_ref, w_ref, o_ref, table_ref, out_ref, w_part, o_part, rows, turned, quads, sems
):
    item, core, place = where[0], where[1], where[2]
    chunk = lax.div(place, 2)
    block = lax.div(chunk, 2) * 4 + core * 2 + lax.rem(chunk, 2)
    copies = (
        pltpu.make_async_copy(
            w_ref.at[pl.ds((place % 2) * 32, 32), pl.ds(block * LANES, LANES)], w_part, sems.at[0]
        ),
        pltpu.make_async_copy(
            o_ref.at[:, pl.ds((core * 2 + place // 8) * LANES, LANES)], o_part, sems.at[1]
        ),
        pltpu.make_async_copy(table_ref.at[:, pl.ds(core * 512, 512)], rows, sems.at[2]),
    )
    for copy in copies:
        copy.start()
    lane = lax.broadcasted_iota(jnp.int32, (ITEMS, 256), 1)
    ids = jnp.sum(
        jnp.where(lane == item * 16 + place, neg_ref[...].astype(F32), 0.0), axis=1, keepdims=True
    ).astype(jnp.int32)
    pick = jnp.where(lane == ids - item * 256, 1.0, 0.0).astype(BF16)
    for copy in copies:
        copy.wait()
    turned[...] = jnp.transpose(o_part[...].astype(F32))
    part = turned[pl.ds((place % 8) * 16, 16), :]
    part = jnp.concatenate([part[0:8, :], part[8:16, :]], axis=1).astype(BF16)
    group = dot(pick, rows[...])
    quads[...] = jnp.zeros_like(quads)
    for b in range(4):
        quads[:, b, :] = group[:, b * LANES : (b + 1) * LANES]
    for i in range(ITEMS):
        out_ref[i, 0:32, :] = w_part[...]
        out_ref[i, 32:40, :] = part
    out_ref[:, 40:48, :] = quads[...].astype(BF16)


def prepare_body(
    where,
    tok_ref,
    len_ref,
    dest_ref,
    off_ref,
    pos_ref,
    in_gain,
    table_ref,
    neg_ref,
    x_ref,
    cols_ref,
    label_ref,
    parcel_ref,
    low_ref,
    hat_ref,
    scale_ref,
    hits_ref,
    tok,
    tab,
    hat,
    turned,
    sems,
):
    item, user = where[0], where[3]
    copies = (
        pltpu.make_async_copy(tok_ref, tok, sems.at[0]),
        pltpu.make_async_copy(table_ref, tab, sems.at[1]),
    )
    for copy in copies:
        copy.start()
    for copy in copies:
        copy.wait()
    normed = layer_norm(tok[...].astype(F32), in_gain[...]).astype(BF16)
    x_ref[...] = reordered(normed)

    lens, dest, off = (r[...].astype(F32) for r in (len_ref, dest_ref, off_ref))
    sub = lax.broadcasted_iota(jnp.int32, (32, 32), 0)
    lane = lax.broadcasted_iota(jnp.int32, (32, 32), 1)
    len_col, dest_col, off_col = (column_of(v, 32) for v in (lens, dest, off))
    start_row = jnp.sum(jnp.where(sub < lane, len_col, 0.0), axis=0, keepdims=True)
    start_col = column_of(start_row, 32)
    row = lax.broadcasted_iota(jnp.int32, (ROWS, 32), 0).astype(F32)
    inside = (row >= start_row) & (row < start_row + lens)
    valid = jnp.sum(jnp.where(inside, 1.0, 0.0), axis=1, keepdims=True) > 0.5
    first = jnp.sum(jnp.where(inside, start_row, 0.0), axis=1, keepdims=True)
    first = jnp.where(valid, first, row[:, 0:1])
    weight = jnp.where(valid, loss_scale, 0.0)
    pos = jnp.transpose(jnp.broadcast_to(pos_ref[...].astype(F32), (LANES, ROWS)))
    at = lax.broadcasted_iota(jnp.int32, (ROWS, LANES), 1)
    local = pos - (item * 256).astype(F32)
    cols_ref[...] = jnp.where(at == 0, first, jnp.where(at == 1, weight, local))

    wide = lax.broadcasted_iota(jnp.int32, (32, LANES), 1).astype(F32)
    to_land = jnp.sum(jnp.where(wide == dest_col, off_col, 0.0), axis=0, keepdims=True)
    to_count = jnp.sum(jnp.where(wide - 32.0 == dest_col, len_col, 0.0), axis=0, keepdims=True)
    label_ref[...] = jnp.broadcast_to(to_land + to_count, (16, LANES)).astype(BF16)

    lane_f = lane.astype(F32)
    first_row = jnp.sum(jnp.where(lane_f == dest_col, start_col, 0.0), axis=0, keepdims=True)
    count_row = jnp.sum(jnp.where(lane_f == dest_col, len_col, 0.0), axis=0, keepdims=True)
    slot = lax.broadcasted_iota(jnp.int32, (ROWS, 32), 0)
    peer = lax.broadcasted_iota(jnp.int32, (ROWS, 32), 1) == slot // MOST
    begin = jnp.sum(jnp.where(peer, first_row, 0.0), axis=1, keepdims=True)
    count = jnp.sum(jnp.where(peer, count_row, 0.0), axis=1, keepdims=True)
    within = (slot[:, 0:1] % MOST).astype(F32)
    source = jnp.where(within < count, begin + within, -1.0)
    send = lax.broadcasted_iota(jnp.int32, (ROWS, ROWS), 1).astype(F32) == source
    parcel_ref[...] = dot(jnp.where(send, 1.0, 0.0).astype(BF16), tok[...]).astype(BF16)

    table = tab[...].astype(F32)
    scale = lax.rsqrt(jnp.mean(table * table, axis=1, keepdims=True) + scale_epsilon)
    hat[...] = table * scale
    low_ref[...] = hat[...].astype(BF16)
    turned[...] = jnp.transpose(hat[:, pl.ds((user // 4) * LANES, LANES)])
    hat_ref[...] = turned[pl.ds((user % 4) * 32, 32), :]
    scale_ref[...] = jnp.transpose(jnp.broadcast_to(scale, (256, LANES)))[0:1, :]

    ids = jnp.broadcast_to(neg_ref[...].astype(F32)[:, None, :], (ITEMS, 16, 256)).reshape(256, 256)
    spot = lax.broadcasted_iota(jnp.int32, (256, 256), 0) % 16 + item * 16
    lanes = lax.broadcasted_iota(jnp.int32, (256, 256), 1)
    ids = jnp.sum(jnp.where(lanes == spot, ids, 0.0), axis=1, keepdims=True)
    hits_ref[...] = jnp.where(lanes.astype(F32) == ids - (item * 256).astype(F32), 1.0, 0.0).astype(BF16)


def forward_body(got, label, out):
    for i in range(ITEMS):
        out[0, i * 32 : (i + 1) * 32, :] = got[i, 0:32, :]
    left = lax.broadcasted_iota(jnp.int32, (8, LANES), 1) < 64
    for b in range(8):
        even, odd = got[2 * b, 32:40, :].astype(F32), got[2 * b + 1, 32:40, :].astype(F32)
        top = jnp.where(left, even, pltpu.roll(odd, 64, 1))
        bottom = jnp.where(left, pltpu.roll(even, 64, 1), odd)
        out[0, W_ROWS + b * 16 : W_ROWS + (b + 1) * 16, :] = jnp.concatenate(
            [top, bottom], axis=0
        ).astype(BF16)
    quads = got[:, 40:48, :].astype(F32)
    for b in range(4):
        out[0, W_ROWS + 128 + b * 16 : W_ROWS + 144 + b * 16, :] = quads[:, b, :].astype(BF16)
    out[0, W_ROWS + 192 : W_ROWS + 208, :] = label[...]
    for g in range(1, 4):
        out[g] = out[0]


def fetches(pieces, w, sems):
    return [pltpu.make_async_copy(p, w.at[n], sems.at[n]) for n, p in enumerate(pieces)]


def kind_of(position, n):
    return lax.rem(position + 4 - n, 4)


def project(x, w):
    parts = [w[i * 720 : i * 720 + W_ROWS, :] for i in range(4)]
    both = jnp.concatenate(
        [jnp.concatenate(parts[0:2], axis=0), jnp.concatenate(parts[2:4], axis=0)], axis=1
    )
    return jax.nn.silu(dot(x, both)).astype(BF16)


def attend(act, first, mixed_ref):
    v, q, k = act[1], act[2], act[3]
    for b in range(first.shape[0] // 128):
        lo, hi = b * 128, (b + 1) * 128
        at = max(lo - 128, 0)
        rows = lo + lax.broadcasted_iota(jnp.int32, (128, hi - at), 0)
        cols = at + lax.broadcasted_iota(jnp.int32, (128, hi - at), 1)
        allowed = (cols >= first[lo:hi, :]) & (cols <= rows)
        for h in range(2):
            d0, d1 = h * HEAD, (h + 1) * HEAD
            scores = dot(q[lo:hi, d0:d1], k[at:hi, d0:d1], ((1,), (1,))) * HEAD ** (-0.5)
            weights = jnp.where(allowed, jax.nn.silu(scores), 0.0).astype(BF16)
            mixed_ref[lo:hi, d0:d1] = dot(weights, v[at:hi, d0:d1])


def project_body(x_ref, w, act_ref, o_ref, g_ref, label_ref):
    act_ref[...] = project(x_ref[...], w)

    def columns(at):
        return jnp.concatenate(
            [w[i * 720 + at : i * 720 + at + 16, :] for i in range(4)], axis=0
        )

    for b in range(8):
        o_ref[:, b * LANES : (b + 1) * LANES] = columns(W_ROWS + b * 16)
    for b in range(4):
        g_ref[:, b * LANES : (b + 1) * LANES] = columns(W_ROWS + 128 + b * 16)
    labels = [
        w[i * 720 + W_ROWS + 192 : (i + 1) * 720, :].astype(F32)[0:1, :] for i in range(4)
    ]
    label_ref[...] = jnp.concatenate(labels + [jnp.zeros((4, LANES), F32)], axis=0)


def finish_body(where, tok_ref, cols_ref, gain_ref, *rest):
    acts, parts = rest[:8], rest[8:16]
    out_ref, o0, o1, act, m0, m1 = rest[16:]
    first = cols_ref[:, 0:1].astype(jnp.int32)
    for half, (o, m) in enumerate(((o0, m0), (o1, m1))):
        for n in range(4):
            kind = kind_of(where[4 + half], n)
            act[half, kind] = acts[4 * half + n][...]
            o[pl.ds(pl.multiple_of(kind * 64, 64), 64), :] = parts[4 * half + n][...]
        attend(act.at[half], first, m)
    out_ref[...] = gated_out(tok_ref[...], act.at[0, 0], m0, o0, act.at[1, 0], m1, o1, gain_ref)


def gated_out(rows, u0, m0, o0, u1, m1, o1, gain_ref):
    a, b = m0[...], m1[...]
    width = 512.0
    center = (jnp.sum(a, axis=1, keepdims=True) + jnp.sum(b, axis=1, keepdims=True)) / width
    a, b = a - center, b - center
    spread = (
        jnp.sum(a * a, axis=1, keepdims=True) + jnp.sum(b * b, axis=1, keepdims=True)
    ) / width
    inv = lax.rsqrt(spread + norm_epsilon)
    ga = (a * inv * gain_ref[:, 0:256] * u0[...].astype(F32)).astype(BF16)
    gb = (b * inv * gain_ref[:, 256:512] * u1[...].astype(F32)).astype(BF16)
    delta = dot(ga, o0[...]) + dot(gb, o1[...])
    return (rows.astype(F32) + delta).astype(BF16)


def worker_body(where, got_ref, in_gain, o0, o1, gain_ref, *rest):
    labels, pieces = rest[:8], rest[8:16]
    out_ref, w0, w1, a0, a1, m0, m1, sems = rest[16:]
    core, user = where[1], where[3]
    copies = (
        fetches(pieces[:4], w0, sems.at[0]),
        fetches(pieces[4:], w1, sems.at[1]),
    )
    for copy in copies[0] + copies[1]:
        copy.start()
    lane = lax.broadcasted_iota(jnp.int32, (32, LANES), 1)
    sub = lax.broadcasted_iota(jnp.int32, (32, ROWS), 0)
    slot = lax.broadcasted_iota(jnp.int32, (1, ROWS), 1)
    peer = slot // MOST
    x, y, c = peer // 8, peer // 2 % 4, peer % 2
    outer, inner = jnp.where(c == 0, y, x), jnp.where(c == 0, x, y)

    def of_peer(at):
        total = 0.0
        for half, mine in ((0, c == core), (1, c != core)):
            table = jnp.concatenate([r[...] for r in labels[4 * half : 4 * half + 4]], axis=0)
            value = jnp.sum(jnp.where(lane == at, table, 0.0), axis=1, keepdims=True)
            spot = lax.rem(where[4 + half] + 4 - outer, 4) * 8 + inner
            total = total + jnp.sum(
                jnp.where((sub == spot) & mine, value, 0.0), axis=0, keepdims=True
            )
        return total

    lower, count = of_peer(user), of_peer(user + USERS)
    within = (slot % MOST).astype(F32)
    lands = jnp.where(within < count, lower + within, -1.0)
    here = lax.broadcasted_iota(jnp.int32, (256, ROWS), 0).astype(F32) == lands
    first = jnp.sum(jnp.where(here, lower, 0.0), axis=1, keepdims=True).astype(jnp.int32)
    rows = dot(jnp.where(here, 1.0, 0.0).astype(BF16), got_ref[...]).astype(BF16)
    normed = layer_norm(rows.astype(F32), in_gain[...]).astype(BF16)
    moved = reordered(normed)
    for position, group, w, act, mixed in (
        (where[4], copies[0], w0, a0, m0),
        (where[5], copies[1], w1, a1, m1),
    ):
        for n, copy in enumerate(group):
            copy.wait()
            act[kind_of(position, n)] = project(moved, w.at[n])
        attend(act, first, mixed)
    out_ref[...] = gated_out(rows, a0.at[0], m0, o0, a1.at[0], m1, o1, gain_ref)


def loss_body(where, out_ref, low_ref, cols_ref, *rest):
    groups = rest[:8]
    grad_ref, own_ref, send_ref, own_inner, terms = rest[8:]
    c = where[1]

    row = lax.broadcasted_iota(jnp.int32, (256, 256), 0)
    col = lax.broadcasted_iota(jnp.int32, (256, 256), 1)
    halves = []
    for half in range(2):
        taken = lax.rem(where[4 + half] + 4 - row % 16 // 4, 4) * 64 + row % 4 * 16 + row // 16
        swap = jnp.where(col == taken, 1.0, 0.0).astype(BF16)
        raw = jnp.concatenate([r[...] for r in groups[4 * half : 4 * half + 4]], axis=0)
        halves.append(dot(swap, raw))
    g0, g1 = halves
    size = (jnp.sum(g0 * g0, axis=1, keepdims=True) + jnp.sum(g1 * g1, axis=1, keepdims=True)) / WIDTH
    scale = lax.rsqrt(size + scale_epsilon)
    g0, g1 = (g0 * scale).astype(BF16), (g1 * scale).astype(BF16)
    here = c == 0
    group = jnp.concatenate([jnp.where(here, g0, g1), jnp.where(here, g1, g0)], axis=1)
    rows = jnp.concatenate([low_ref[...], group], axis=0)

    out = out_ref[...].astype(F32)
    out_scale = lax.rsqrt(jnp.mean(out * out, axis=1, keepdims=True) + scale_epsilon)
    hat = out * out_scale
    low = hat.astype(BF16)
    factor = inverse_temp / WIDTH
    raw = dot(low, rows, ((1,), (1,)))
    hit = lax.broadcasted_iota(jnp.int32, (ROWS, 256), 1) == cols_ref[:, 2:3].astype(jnp.int32)
    pos = jnp.exp(jnp.sum(jnp.where(hit, raw[:, :256], 0.0), axis=1, keepdims=True) * factor)
    neg = jnp.exp(raw[:, 256:] * factor)
    total = pos + jnp.sum(neg, axis=1, keepdims=True)
    weight = cols_ref[:, 1:2]
    pos_grad = weight * (pos / total - 1.0)
    grads = jnp.concatenate(
        [jnp.where(hit, pos_grad, 0.0).astype(BF16), (weight * neg / total).astype(BF16)], axis=1
    )
    grad_hat = dot(grads, rows) * factor
    inner = jnp.mean(grad_hat * hat, axis=1, keepdims=True)
    grad_ref[...] = ((grad_hat - hat * inner) * out_scale).astype(BF16)
    sums = dot(low, grads, ((0,), (0,))) * factor
    terms[...] = sums.astype(BF16).reshape(PLANE, 2, 32, ROWS)
    for k in range(PLANE):
        own_ref[k] = terms[k, c]
        send_ref[k * 32 : (k + 1) * 32, :] = terms[k, 1 - c]
    products = jnp.sum(grads.astype(F32) * raw, axis=0, keepdims=True) * factor
    own_inner[...] = products
    top = products.astype(BF16).astype(F32)
    send_ref[512:528, :] = split_rows(top, products - top).astype(BF16)


def split_rows(top, rest):
    at = lax.broadcasted_iota(jnp.int32, (16, ROWS), 0)
    return jnp.where(at == 0, top, jnp.where(at == 1, rest, 0.0))


def pair_body(own_ref, inner_ref, got_ref, out_ref):
    other = got_ref[512:528, :].astype(F32)
    inner = inner_ref[...] + other[0:1, :] + other[1:2, :]
    top = inner.astype(BF16).astype(F32)
    tail = split_rows(top, inner - top).astype(BF16)
    for k in range(PLANE):
        mine = own_ref[k].astype(F32) + got_ref[k * 32 : (k + 1) * 32, :].astype(F32)
        out_ref[k, 0:32, :] = mine.astype(BF16)
        out_ref[k, 32:40, :] = tail[0:8, :]


def plane_body(got_ref, pos_ref, neg_ref):
    acc = got_ref[0].astype(F32)
    for k in range(1, PLANE):
        acc = acc + got_ref[k].astype(F32)
    inner = acc[32:33, :] + acc[33:34, :]
    top = inner.astype(BF16).astype(F32)
    full = jnp.concatenate([acc[0:32, :], split_rows(top, inner - top)], axis=0)
    pos_ref[...] = full[:, 0:256]
    tail = jnp.concatenate([full[:, 256:512], jnp.zeros((80, 256), F32)], axis=0)
    neg_ref[...] = jnp.transpose(tail).astype(BF16)


def item_body(pos_ref, hits_ref, got_ref, hat_ref, scale_ref, out_ref):
    total = pos_ref[...] + dot(got_ref[...], hits_ref[...], ((0,), (0,)))[0:48, :]
    inner = (total[32:33, :] + total[33:34, :]) / WIDTH
    out_ref[...] = (total[0:32, :] - hat_ref[...] * inner) * scale_ref[...]


def layer_norm(values, gain):
    center = jnp.mean(values, axis=-1, keepdims=True)
    shifted = values - center
    spread = jnp.mean(shifted * shifted, axis=-1, keepdims=True)
    return shifted * lax.rsqrt(spread + norm_epsilon) * gain


def in_hbm(values):
    return pltpu.with_memory_space_constraint(values, pltpu.HBM)


def exchange(blocks, axis, groups=None):
    return lax.all_to_all(blocks, axis, 0, 0, tiled=True, axis_index_groups=groups)


def per_device(
    tokens,
    lengths,
    destination,
    worker_offset,
    positives,
    negatives,
    table,
    in_gain,
    w_uvqk,
    out_gain,
    w_out,
):
    item = lax.axis_index("item")
    user = lax.axis_index("user")
    core = user & 1
    x, y = user >> 3, (user >> 1) & 3
    place = jnp.where(core == 0, y * 4 + x, x * 4 + y)
    second = jnp.where(core == 0, y, x)
    first = jnp.where(core == 0, x, y)
    where = jnp.stack([item, core, place, user, second, first]).astype(jnp.int32)

    first_message = call(
        message_body,
        shape((ITEMS, 48, LANES)),
        [SMEM, VMEM, HBM, HBM, HBM],
        scratch=[
            pltpu.VMEM((32, LANES), BF16),
            pltpu.VMEM((64, LANES), BF16),
            pltpu.VMEM((256, 512), BF16),
            pltpu.VMEM((LANES, 64), F32),
            pltpu.VMEM((ITEMS, 8, LANES), F32),
            pltpu.SemaphoreType.DMA((3,)),
        ],
    )(where, negatives, in_hbm(w_uvqk), in_hbm(w_out.T), in_hbm(table))
    got = exchange(first_message, "item")

    x_rows, cols, labels, parcels, table_low, hat_part, table_scale, hits = call(
        prepare_body,
        (
            shape((ROWS, WIDTH)),
            shape((ROWS, LANES), F32),
            shape((16, LANES)),
            shape((ROWS, WIDTH)),
            shape((256, WIDTH)),
            shape((32, 256), F32),
            shape((1, 256), F32),
            shape((256, 256)),
        ),
        [SMEM, HBM] + [VMEM] * 5 + [HBM, VMEM],
        scratch=[
            pltpu.VMEM((ROWS, WIDTH), BF16),
            pltpu.VMEM((256, WIDTH), BF16),
            pltpu.VMEM((256, WIDTH), F32),
            pltpu.VMEM((LANES, 256), F32),
            pltpu.SemaphoreType.DMA((2,)),
        ],
        mib=24,
    )(
        where,
        in_hbm(tokens),
        lengths,
        destination,
        worker_offset,
        positives[None],
        in_gain[None],
        in_hbm(table),
        negatives,
    )
    gain = jnp.where(core == 0, out_gain, jnp.roll(out_gain, 256))[None]
    got, x_rows, gain = lax.optimization_barrier((got, x_rows, gain))

    message = call(forward_body, shape((4, W_ROWS + REST, LANES)), [VMEM, VMEM])(got, labels)
    mid = exchange(message, "user", FIRST).reshape(PIECE, LANES)
    mid, parcels = lax.optimization_barrier((mid, parcels))
    own, other = {0: mid}, {}
    for step in (1, 3, 2):
        own[step] = lax.ppermute(mid, "user", shifted(SECOND, step))
    for step in (0, 1, 3, 2):
        other[step] = lax.ppermute(own[step], "user", PARTNER)
    arrived = exchange(parcels.reshape(USERS, MOST, WIDTH), "user").reshape(ROWS, WIDTH)

    layer_part = call(
        project_body,
        (shape((ROWS, 256)), shape((64, WIDTH)), shape((64, 512)), shape((8, LANES), F32)),
        [VMEM] * 2,
        mib=8,
    )
    parts = []
    for pieces in (own, other):
        for n in range(4):
            parts.append(layer_part(x_rows, pieces[n]))
    acts, o_parts, groups, tables = zip(*parts)
    pieces = [own[n] for n in range(4)] + [other[n] for n in range(4)]
    home_out, o_own, o_other = call(
        finish_body,
        (shape((ROWS, WIDTH)), shape((256, WIDTH)), shape((256, WIDTH))),
        [SMEM] + [VMEM] * 19,
        scratch=[
            pltpu.VMEM((2, 4, ROWS, 256), BF16),
            pltpu.VMEM((ROWS, 256), F32),
            pltpu.VMEM((ROWS, 256), F32),
        ],
        mib=16,
    )(where, tokens, cols, gain, *acts, *o_parts)

    token_grad, own_terms, sent, own_inner = call(
        loss_body,
        (
            shape((ROWS, WIDTH)),
            shape((PLANE, 32, ROWS)),
            shape((528, ROWS)),
            shape((1, ROWS), F32),
        ),
        [SMEM] + [VMEM] * 11,
        scratch=[pltpu.VMEM((PLANE, 2, 32, ROWS), BF16)],
        mib=16,
    )(where, home_out, table_low, cols, *groups)
    partner_terms = lax.ppermute(sent, "user", PARTNER)
    pair = call(pair_body, shape((PLANE, 40, ROWS)), [VMEM] * 3)(
        own_terms, own_inner, partner_terms
    )
    pair, arrived = lax.optimization_barrier((pair, arrived))
    plane = exchange(pair, "user", SAME_CORE)

    layer_out = call(
        worker_body,
        shape((256, WIDTH)),
        [SMEM] + [VMEM] * 13 + [ANY] * 8,
        scratch=[
            pltpu.VMEM((4, PIECE, LANES), BF16),
            pltpu.VMEM((4, PIECE, LANES), BF16),
            pltpu.VMEM((4, 256, 256), BF16),
            pltpu.VMEM((4, 256, 256), BF16),
            pltpu.VMEM((256, 256), F32),
            pltpu.VMEM((256, 256), F32),
            pltpu.SemaphoreType.DMA((2, 4)),
        ],
        mib=24,
    )(where, arrived, in_gain[None], o_own, o_other, gain, *tables, *pieces)

    positive_part, negative_part = call(
        plane_body, (shape((48, 256), F32), shape((256, LANES))), [VMEM]
    )(plane)
    owned = exchange(negative_part.reshape(ITEMS, 16, LANES), "item").reshape(256, LANES)
    item_grad = call(item_body, shape((32, 256), F32), [VMEM] * 5)(
        positive_part, hits, owned, hat_part, table_scale
    ).T
    return (layer_out, token_grad, item_grad)


def solution(mesh):
    return jax.shard_map(
        per_device,
        mesh=mesh,
        in_specs=(
            P(("user", "item"), None),
            P(("user", "item"), None),
            P(("user", "item"), None),
            P(("user", "item"), None),
            P(("user", "item")),
            P(),
            P("item", None),
            P(),
            P("item", None),
            P(),
            P(None, "item"),
        ),
        out_specs=(P(("user", "item"), None), P(("user", "item"), None), P("item", "user")),
        check_vma=False,
    )
```

```python
import jax
import jax.numpy as jnp
from jax import lax
from jax.experimental import pallas as pl
from jax.experimental.pallas import tpu as pltpu
from jax.sharding import PartitionSpec as P


norm_epsilon = 1e-05
scale_epsilon = 1e-06
inverse_temp = 20.0
loss_scale = 32.0

F32 = jnp.float32
BF16 = jnp.bfloat16

USERS = 32
ITEMS = 16
PLANE = 16
LANES = 128
ROWS = 512
MOST = 16
WIDTH = 1024
HEAD = 128

FIRST = [[x * 8 + y * 2 for x in range(4)] for y in range(4)] + [
    [x * 8 + y * 2 + 1 for y in range(4)] for x in range(4)
]
SECOND = [[x * 8 + y * 2 for y in range(4)] for x in range(4)] + [
    [x * 8 + y * 2 + 1 for x in range(4)] for y in range(4)
]
SAME_CORE = [[k * 2 + c for k in range(PLANE)] for c in range(2)]
PARTNER = [(k, k ^ 1) for k in range(USERS)]

VMEM = pl.BlockSpec(memory_space=pltpu.VMEM)
ANY = pl.BlockSpec(memory_space=pl.ANY)
HBM = pl.BlockSpec(memory_space=pltpu.HBM)
SMEM = pl.BlockSpec(memory_space=pltpu.SMEM)
W_ROWS = 512
REST = 208


def shape(dims, kind=BF16):
    return jax.ShapeDtypeStruct(dims, kind)


def dot(a, b, contract=((1,), (0,))):
    return lax.dot_general(a, b, (contract, ((), ())), preferred_element_type=F32)


def call(body, outs, specs, scratch=(), mib=8, out_specs=None):
    return pl.pallas_call(
        body,
        out_shape=outs,
        in_specs=specs,
        out_specs=out_specs or jax.tree.map(lambda _: VMEM, outs),
        scratch_shapes=list(scratch),
        compiler_params=pltpu.CompilerParams(vmem_limit_bytes=mib * 2**20),
    )


def column_of(row, n):
    eye = lax.broadcasted_iota(jnp.int32, (n, n), 0) == lax.broadcasted_iota(jnp.int32, (n, n), 1)
    return jnp.sum(jnp.where(eye, row, 0.0), axis=1, keepdims=True)


def reordered(rows):
    at = lax.broadcasted_iota(jnp.int32, (1, WIDTH), 1)
    wanted = (at % 512) // 32 * 64 + at // 512 * 32 + at % 32
    order = lax.broadcasted_iota(jnp.int32, (WIDTH, WIDTH), 0) == wanted
    return dot(rows, jnp.where(order, 1.0, 0.0).astype(BF16)).astype(BF16)


def message_body(
    where, neg_ref, w_ref, o_ref, table_ref, out_ref, w_part, o_part, rows, turned, quads, sems
):
    item, core, place = where[0], where[1], where[2]
    chunk = lax.div(place, 2)
    block = lax.div(chunk, 2) * 4 + core * 2 + lax.rem(chunk, 2)
    copies = (
        pltpu.make_async_copy(
            w_ref.at[pl.ds((place % 2) * 32, 32), pl.ds(block * LANES, LANES)], w_part, sems.at[0]
        ),
        pltpu.make_async_copy(
            o_ref.at[:, pl.ds((core * 2 + place // 8) * LANES, LANES)], o_part, sems.at[1]
        ),
        pltpu.make_async_copy(table_ref.at[:, pl.ds(core * 512, 512)], rows, sems.at[2]),
    )
    for copy in copies:
        copy.start()
    lane = lax.broadcasted_iota(jnp.int32, (ITEMS, 256), 1)
    ids = jnp.sum(
        jnp.where(lane == item * 16 + place, neg_ref[...].astype(F32), 0.0), axis=1, keepdims=True
    ).astype(jnp.int32)
    pick = jnp.where(lane == ids - item * 256, 1.0, 0.0).astype(BF16)
    for copy in copies:
        copy.wait()
    turned[...] = jnp.transpose(o_part[...].astype(F32))
    part = turned[pl.ds((place % 8) * 16, 16), :]
    part = jnp.concatenate([part[0:8, :], part[8:16, :]], axis=1).astype(BF16)
    group = dot(pick, rows[...])
    quads[...] = jnp.zeros_like(quads)
    for b in range(4):
        quads[:, b, :] = group[:, b * LANES : (b + 1) * LANES]
    for i in range(ITEMS):
        out_ref[i, 0:32, :] = w_part[...]
        out_ref[i, 32:40, :] = part
    out_ref[:, 40:48, :] = quads[...].astype(BF16)


def prepare_body(
    where,
    tok_ref,
    len_ref,
    dest_ref,
    off_ref,
    pos_ref,
    in_gain,
    table_ref,
    neg_ref,
    x_ref,
    cols_ref,
    label_ref,
    parcel_ref,
    low_ref,
    hat_ref,
    scale_ref,
    hits_ref,
    tok,
    tab,
    hat,
    turned,
    sems,
):
    item, user = where[0], where[3]
    copies = (
        pltpu.make_async_copy(tok_ref, tok, sems.at[0]),
        pltpu.make_async_copy(table_ref, tab, sems.at[1]),
    )
    for copy in copies:
        copy.start()
    for copy in copies:
        copy.wait()
    normed = layer_norm(tok[...].astype(F32), in_gain[...]).astype(BF16)
    x_ref[...] = reordered(normed)

    lens, dest, off = (r[...].astype(F32) for r in (len_ref, dest_ref, off_ref))
    sub = lax.broadcasted_iota(jnp.int32, (32, 32), 0)
    lane = lax.broadcasted_iota(jnp.int32, (32, 32), 1)
    len_col, dest_col, off_col = (column_of(v, 32) for v in (lens, dest, off))
    start_row = jnp.sum(jnp.where(sub < lane, len_col, 0.0), axis=0, keepdims=True)
    start_col = column_of(start_row, 32)
    row = lax.broadcasted_iota(jnp.int32, (ROWS, 32), 0).astype(F32)
    inside = (row >= start_row) & (row < start_row + lens)
    valid = jnp.sum(jnp.where(inside, 1.0, 0.0), axis=1, keepdims=True) > 0.5
    first = jnp.sum(jnp.where(inside, start_row, 0.0), axis=1, keepdims=True)
    first = jnp.where(valid, first, row[:, 0:1])
    weight = jnp.where(valid, loss_scale, 0.0)
    pos = jnp.transpose(jnp.broadcast_to(pos_ref[...].astype(F32), (LANES, ROWS)))
    at = lax.broadcasted_iota(jnp.int32, (ROWS, LANES), 1)
    local = pos - (item * 256).astype(F32)
    cols_ref[...] = jnp.where(at == 0, first, jnp.where(at == 1, weight, local))

    wide = lax.broadcasted_iota(jnp.int32, (32, LANES), 1).astype(F32)
    to_land = jnp.sum(jnp.where(wide == dest_col, off_col, 0.0), axis=0, keepdims=True)
    to_count = jnp.sum(jnp.where(wide - 32.0 == dest_col, len_col, 0.0), axis=0, keepdims=True)
    label_ref[...] = jnp.broadcast_to(to_land + to_count, (16, LANES)).astype(BF16)

    lane_f = lane.astype(F32)
    first_row = jnp.sum(jnp.where(lane_f == dest_col, start_col, 0.0), axis=0, keepdims=True)
    count_row = jnp.sum(jnp.where(lane_f == dest_col, len_col, 0.0), axis=0, keepdims=True)
    slot = lax.broadcasted_iota(jnp.int32, (ROWS, 32), 0)
    peer = lax.broadcasted_iota(jnp.int32, (ROWS, 32), 1) == slot // MOST
    begin = jnp.sum(jnp.where(peer, first_row, 0.0), axis=1, keepdims=True)
    count = jnp.sum(jnp.where(peer, count_row, 0.0), axis=1, keepdims=True)
    within = (slot[:, 0:1] % MOST).astype(F32)
    source = jnp.where(within < count, begin + within, -1.0)
    send = lax.broadcasted_iota(jnp.int32, (ROWS, ROWS), 1).astype(F32) == source
    parcel_ref[...] = dot(jnp.where(send, 1.0, 0.0).astype(BF16), tok[...]).astype(BF16)

    table = tab[...].astype(F32)
    scale = lax.rsqrt(jnp.mean(table * table, axis=1, keepdims=True) + scale_epsilon)
    hat[...] = table * scale
    low_ref[...] = hat[...].astype(BF16)
    turned[...] = jnp.transpose(hat[:, pl.ds((user // 4) * LANES, LANES)])
    hat_ref[...] = turned[pl.ds((user % 4) * 32, 32), :]
    scale_ref[...] = jnp.transpose(jnp.broadcast_to(scale, (256, LANES)))[0:1, :]

    ids = jnp.broadcast_to(neg_ref[...].astype(F32)[:, None, :], (ITEMS, 16, 256)).reshape(256, 256)
    spot = lax.broadcasted_iota(jnp.int32, (256, 256), 0) % 16 + item * 16
    lanes = lax.broadcasted_iota(jnp.int32, (256, 256), 1)
    ids = jnp.sum(jnp.where(lanes == spot, ids, 0.0), axis=1, keepdims=True)
    hits_ref[...] = jnp.where(lanes.astype(F32) == ids - (item * 256).astype(F32), 1.0, 0.0).astype(BF16)


def forward_body(got, label, out):
    for i in range(ITEMS):
        out[0, i * 32 : (i + 1) * 32, :] = got[i, 0:32, :]
    left = lax.broadcasted_iota(jnp.int32, (8, LANES), 1) < 64
    for b in range(8):
        even, odd = got[2 * b, 32:40, :].astype(F32), got[2 * b + 1, 32:40, :].astype(F32)
        top = jnp.where(left, even, pltpu.roll(odd, 64, 1))
        bottom = jnp.where(left, pltpu.roll(even, 64, 1), odd)
        out[0, W_ROWS + b * 16 : W_ROWS + (b + 1) * 16, :] = jnp.concatenate(
            [top, bottom], axis=0
        ).astype(BF16)
    quads = got[:, 40:48, :].astype(F32)
    for b in range(4):
        out[0, W_ROWS + 128 + b * 16 : W_ROWS + 144 + b * 16, :] = quads[:, b, :].astype(BF16)
    out[0, W_ROWS + 192 : W_ROWS + 208, :] = label[...]
    for g in range(1, 4):
        out[g] = out[0]


def project(x, w, q):
    both = jnp.concatenate(
        [
            jnp.concatenate([w[n, :W_ROWS, :], w[n + 1, :W_ROWS, :]], axis=0)
            for n in (4 * q, 4 * q + 2)
        ],
        axis=1,
    )
    return jax.nn.silu(dot(x, both)).astype(BF16)


def attend(act, first, mixed_ref):
    v, q, k = act[1], act[2], act[3]
    for b in range(first.shape[0] // 128):
        lo, hi = b * 128, (b + 1) * 128
        at = max(lo - 128, 0)
        rows = lo + lax.broadcasted_iota(jnp.int32, (128, hi - at), 0)
        cols = at + lax.broadcasted_iota(jnp.int32, (128, hi - at), 1)
        allowed = (cols >= first[lo:hi, :]) & (cols <= rows)
        for h in range(2):
            d0, d1 = h * HEAD, (h + 1) * HEAD
            scores = dot(q[lo:hi, d0:d1], k[at:hi, d0:d1], ((1,), (1,))) * HEAD ** (-0.5)
            weights = jnp.where(allowed, jax.nn.silu(scores), 0.0).astype(BF16)
            mixed_ref[lo:hi, d0:d1] = dot(weights, v[at:hi, d0:d1])


def split_rest(w, o_ref, g_ref, label_ref):
    for n in range(8):
        o_ref[:, n * LANES : (n + 1) * LANES] = w[
            :, W_ROWS + n * 16 : W_ROWS + (n + 1) * 16, :
        ].reshape(256, LANES)
    for n in range(4):
        g_ref[:, n * LANES : (n + 1) * LANES] = w[
            :, W_ROWS + 128 + n * 16 : W_ROWS + 144 + n * 16, :
        ].reshape(256, LANES)
    for n in range(PLANE):
        label_ref[n : n + 1, :] = w[n, W_ROWS + 192 : W_ROWS + 208, :].astype(F32)[0:1, :]


def layer_body(
    x_ref,
    w0,
    w1_ref,
    tok_ref,
    cols_ref,
    gain_ref,
    out_ref,
    o0,
    o1,
    g0,
    g1,
    near,
    far,
    kept_ref,
    x,
    w1,
    tok,
    act,
    m0,
    m1,
    sems,
):
    copies = [
        pltpu.make_async_copy(a, b, sems.at[n])
        for n, (a, b) in enumerate(((x_ref, x), (w1_ref, w1), (tok_ref, tok), (w0, kept_ref)))
    ]
    for copy in copies:
        copy.start()
    split_rest(w0, o0, g0, near)
    first = cols_ref[:, 0:1].astype(jnp.int32)
    copies[0].wait()
    rows = x[...]
    for q in range(4):
        act[0, q] = project(rows, w0, q)
    attend(act.at[0], first, m0)
    copies[1].wait()
    split_rest(w1, o1, g1, far)
    for q in range(4):
        act[1, q] = project(rows, w1, q)
    attend(act.at[1], first, m1)
    copies[2].wait()
    out_ref[...] = gated_out(tok[...], act.at[0, 0], m0, o0, act.at[1, 0], m1, o1, gain_ref)
    copies[3].wait()


def gated_out(rows, u0, m0, o0, u1, m1, o1, gain_ref):
    a, b = m0[...], m1[...]
    width = 512.0
    center = (jnp.sum(a, axis=1, keepdims=True) + jnp.sum(b, axis=1, keepdims=True)) / width
    a, b = a - center, b - center
    spread = (
        jnp.sum(a * a, axis=1, keepdims=True) + jnp.sum(b * b, axis=1, keepdims=True)
    ) / width
    inv = lax.rsqrt(spread + norm_epsilon)
    ga = (a * inv * gain_ref[:, 0:256] * u0[...].astype(F32)).astype(BF16)
    gb = (b * inv * gain_ref[:, 256:512] * u1[...].astype(F32)).astype(BF16)
    delta = dot(ga, o0[...]) + dot(gb, o1[...])
    return (rows.astype(F32) + delta).astype(BF16)


def worker_body(
    where,
    got_ref,
    in_gain,
    o0,
    o1,
    gain_ref,
    near,
    far,
    w0_ref,
    w1_ref,
    out_ref,
    w0,
    w1,
    act,
    m0,
    m1,
    sems,
):
    core, user = where[1], where[3]
    copies = [
        pltpu.make_async_copy(a, b, sems.at[n]) for n, (a, b) in enumerate(((w0_ref, w0), (w1_ref, w1)))
    ]
    for copy in copies:
        copy.start()
    lane = lax.broadcasted_iota(jnp.int32, (PLANE, LANES), 1)
    sub = lax.broadcasted_iota(jnp.int32, (PLANE, ROWS), 0)
    slot = lax.broadcasted_iota(jnp.int32, (1, ROWS), 1)
    peer = slot // MOST
    x, y, c = peer // 8, peer // 2 % 4, peer % 2
    spot = jnp.where(c == 0, y * 4 + x, x * 4 + y)

    def of_peer(at):
        total = 0.0
        for ref, mine in ((near, c == core), (far, c != core)):
            value = jnp.sum(jnp.where(lane == at, ref[...], 0.0), axis=1, keepdims=True)
            total = total + jnp.sum(
                jnp.where((sub == spot) & mine, value, 0.0), axis=0, keepdims=True
            )
        return total

    lower, count = of_peer(user), of_peer(user + USERS)
    within = (slot % MOST).astype(F32)
    lands = jnp.where(within < count, lower + within, -1.0)
    here = lax.broadcasted_iota(jnp.int32, (256, ROWS), 0).astype(F32) == lands
    first = jnp.sum(jnp.where(here, lower, 0.0), axis=1, keepdims=True).astype(jnp.int32)
    rows = dot(jnp.where(here, 1.0, 0.0).astype(BF16), got_ref[...]).astype(BF16)
    normed = layer_norm(rows.astype(F32), in_gain[...]).astype(BF16)
    moved = reordered(normed)
    for half, (w, m) in enumerate(((w0, m0), (w1, m1))):
        copies[half].wait()
        for q in range(4):
            act[half, q] = project(moved, w, q)
        attend(act.at[half], first, m)
    out_ref[...] = gated_out(rows, act.at[0, 0], m0, o0, act.at[1, 0], m1, o1, gain_ref)


def loss_body(
    where,
    out_ref,
    low_ref,
    cols_ref,
    g0_ref,
    g1_ref,
    grad_ref,
    own_ref,
    send_ref,
    own_inner,
    terms,
):
    c = where[1]

    row = lax.broadcasted_iota(jnp.int32, (256, 256), 0)
    col = lax.broadcasted_iota(jnp.int32, (256, 256), 1)
    swap = jnp.where(col == row % 16 * 16 + row // 16, 1.0, 0.0).astype(BF16)
    g0, g1 = dot(swap, g0_ref[...]), dot(swap, g1_ref[...])
    size = (jnp.sum(g0 * g0, axis=1, keepdims=True) + jnp.sum(g1 * g1, axis=1, keepdims=True)) / WIDTH
    scale = lax.rsqrt(size + scale_epsilon)
    g0, g1 = (g0 * scale).astype(BF16), (g1 * scale).astype(BF16)
    here = c == 0
    group = jnp.concatenate([jnp.where(here, g0, g1), jnp.where(here, g1, g0)], axis=1)
    rows = jnp.concatenate([low_ref[...], group], axis=0)

    out = out_ref[...].astype(F32)
    out_scale = lax.rsqrt(jnp.mean(out * out, axis=1, keepdims=True) + scale_epsilon)
    hat = out * out_scale
    low = hat.astype(BF16)
    factor = inverse_temp / WIDTH
    raw = dot(low, rows, ((1,), (1,)))
    hit = lax.broadcasted_iota(jnp.int32, (ROWS, 256), 1) == cols_ref[:, 2:3].astype(jnp.int32)
    pos = jnp.exp(jnp.sum(jnp.where(hit, raw[:, :256], 0.0), axis=1, keepdims=True) * factor)
    neg = jnp.exp(raw[:, 256:] * factor)
    total = pos + jnp.sum(neg, axis=1, keepdims=True)
    weight = cols_ref[:, 1:2]
    pos_grad = weight * (pos / total - 1.0)
    grads = jnp.concatenate(
        [jnp.where(hit, pos_grad, 0.0).astype(BF16), (weight * neg / total).astype(BF16)], axis=1
    )
    grad_hat = dot(grads, rows) * factor
    inner = jnp.mean(grad_hat * hat, axis=1, keepdims=True)
    grad_ref[...] = ((grad_hat - hat * inner) * out_scale).astype(BF16)
    sums = dot(low, grads, ((0,), (0,))) * factor
    terms[...] = sums.astype(BF16).reshape(PLANE, 2, 32, ROWS)
    for k in range(PLANE):
        own_ref[k] = terms[k, c]
        send_ref[k * 32 : (k + 1) * 32, :] = terms[k, 1 - c]
    products = jnp.sum(grads.astype(F32) * raw, axis=0, keepdims=True) * factor
    own_inner[...] = products
    top = products.astype(BF16).astype(F32)
    send_ref[512:528, :] = split_rows(top, products - top).astype(BF16)


def split_rows(top, rest):
    at = lax.broadcasted_iota(jnp.int32, (16, ROWS), 0)
    return jnp.where(at == 0, top, jnp.where(at == 1, rest, 0.0))


def pair_body(own_ref, inner_ref, got_ref, out_ref):
    other = got_ref[512:528, :].astype(F32)
    inner = inner_ref[...] + other[0:1, :] + other[1:2, :]
    top = inner.astype(BF16).astype(F32)
    tail = split_rows(top, inner - top).astype(BF16)
    for k in range(PLANE):
        mine = own_ref[k].astype(F32) + got_ref[k * 32 : (k + 1) * 32, :].astype(F32)
        out_ref[k, 0:32, :] = mine.astype(BF16)
        out_ref[k, 32:40, :] = tail[0:8, :]


def plane_body(got_ref, pos_ref, neg_ref):
    acc = got_ref[0].astype(F32)
    for k in range(1, PLANE):
        acc = acc + got_ref[k].astype(F32)
    inner = acc[32:33, :] + acc[33:34, :]
    top = inner.astype(BF16).astype(F32)
    full = jnp.concatenate([acc[0:32, :], split_rows(top, inner - top)], axis=0)
    pos_ref[...] = full[:, 0:256]
    tail = jnp.concatenate([full[:, 256:512], jnp.zeros((80, 256), F32)], axis=0)
    neg_ref[...] = jnp.transpose(tail).astype(BF16)


def item_body(pos_ref, hits_ref, got_ref, hat_ref, scale_ref, out_ref):
    total = pos_ref[...] + dot(got_ref[...], hits_ref[...], ((0,), (0,)))[0:48, :]
    inner = (total[32:33, :] + total[33:34, :]) / WIDTH
    out_ref[...] = (total[0:32, :] - hat_ref[...] * inner) * scale_ref[...]


def layer_norm(values, gain):
    center = jnp.mean(values, axis=-1, keepdims=True)
    shifted = values - center
    spread = jnp.mean(shifted * shifted, axis=-1, keepdims=True)
    return shifted * lax.rsqrt(spread + norm_epsilon) * gain


def in_hbm(values):
    return pltpu.with_memory_space_constraint(values, pltpu.HBM)


def copies(block, count):
    return jnp.broadcast_to(block[None], (count, *block.shape))


def exchange(blocks, axis, groups=None):
    return lax.all_to_all(blocks, axis, 0, 0, tiled=True, axis_index_groups=groups)


def per_device(
    tokens,
    lengths,
    destination,
    worker_offset,
    positives,
    negatives,
    table,
    in_gain,
    w_uvqk,
    out_gain,
    w_out,
):
    item = lax.axis_index("item")
    user = lax.axis_index("user")
    core = user & 1
    x, y = user >> 3, (user >> 1) & 3
    place = jnp.where(core == 0, y * 4 + x, x * 4 + y)
    where = jnp.stack([item, core, place, user]).astype(jnp.int32)

    first_message = call(
        message_body,
        shape((ITEMS, 48, LANES)),
        [SMEM, VMEM, HBM, HBM, HBM],
        scratch=[
            pltpu.VMEM((32, LANES), BF16),
            pltpu.VMEM((64, LANES), BF16),
            pltpu.VMEM((256, 512), BF16),
            pltpu.VMEM((LANES, 64), F32),
            pltpu.VMEM((ITEMS, 8, LANES), F32),
            pltpu.SemaphoreType.DMA((3,)),
        ],
    )(where, negatives, in_hbm(w_uvqk), in_hbm(w_out.T), in_hbm(table))
    got = exchange(first_message, "item")

    x_rows, cols, labels, parcels, table_low, hat_part, table_scale, hits = call(
        prepare_body,
        (
            shape((ROWS, WIDTH)),
            shape((ROWS, LANES), F32),
            shape((16, LANES)),
            shape((ROWS, WIDTH)),
            shape((256, WIDTH)),
            shape((32, 256), F32),
            shape((1, 256), F32),
            shape((256, 256)),
        ),
        [SMEM, HBM] + [VMEM] * 5 + [HBM, VMEM],
        scratch=[
            pltpu.VMEM((ROWS, WIDTH), BF16),
            pltpu.VMEM((256, WIDTH), BF16),
            pltpu.VMEM((256, WIDTH), F32),
            pltpu.VMEM((LANES, 256), F32),
            pltpu.SemaphoreType.DMA((2,)),
        ],
        mib=24,
    )(
        where,
        in_hbm(tokens),
        lengths,
        destination,
        worker_offset,
        positives[None],
        in_gain[None],
        in_hbm(table),
        negatives,
    )
    gain = jnp.where(core == 0, out_gain, jnp.roll(out_gain, 256))[None]
    got, x_rows, gain = lax.optimization_barrier((got, x_rows, gain))

    message = call(forward_body, shape((4, W_ROWS + REST, LANES)), [VMEM, VMEM])(got, labels)
    mid = exchange(message, "user", FIRST).reshape(4 * (W_ROWS + REST), LANES)
    held = exchange(copies(mid, 4), "user", SECOND).reshape(PLANE, W_ROWS + REST, LANES)
    held, parcels = lax.optimization_barrier((held, parcels))
    held_other = lax.ppermute(held, "user", PARTNER)
    arrived = exchange(parcels.reshape(USERS, MOST, WIDTH), "user").reshape(ROWS, WIDTH)

    home_out, o_own, o_other, g_own, g_other, near, far, kept = call(
        layer_body,
        (
            shape((ROWS, WIDTH)),
            shape((256, WIDTH)),
            shape((256, WIDTH)),
            shape((256, 512)),
            shape((256, 512)),
            shape((PLANE, LANES), F32),
            shape((PLANE, LANES), F32),
            pltpu.HBM((PLANE, W_ROWS + REST, LANES), BF16),
        ),
        [HBM, VMEM, HBM, HBM, VMEM, VMEM],
        scratch=[
            pltpu.VMEM((ROWS, WIDTH), BF16),
            pltpu.VMEM((PLANE, W_ROWS + REST, LANES), BF16),
            pltpu.VMEM((ROWS, WIDTH), BF16),
            pltpu.VMEM((2, 4, ROWS, 256), BF16),
            pltpu.VMEM((ROWS, 256), F32),
            pltpu.VMEM((ROWS, 256), F32),
            pltpu.SemaphoreType.DMA((4,)),
        ],
        mib=20,
        out_specs=(VMEM,) * 7 + (HBM,),
    )(in_hbm(x_rows), held, in_hbm(held_other), in_hbm(tokens), cols, gain)

    token_grad, own_terms, sent, own_inner = call(
        loss_body,
        (
            shape((ROWS, WIDTH)),
            shape((PLANE, 32, ROWS)),
            shape((528, ROWS)),
            shape((1, ROWS), F32),
        ),
        [SMEM] + [VMEM] * 5,
        scratch=[pltpu.VMEM((PLANE, 2, 32, ROWS), BF16)],
        mib=16,
    )(where, home_out, table_low, cols, g_own, g_other)
    partner_terms = lax.ppermute(sent, "user", PARTNER)
    pair = call(pair_body, pltpu.HBM((PLANE, 40, ROWS), BF16), [VMEM] * 3, out_specs=VMEM)(
        own_terms, own_inner, partner_terms
    )
    pair, arrived = lax.optimization_barrier((pair, arrived))
    plane = exchange(pair, "user", SAME_CORE)

    layer_out = call(
        worker_body,
        shape((256, WIDTH)),
        [SMEM] + [VMEM] * 7 + [HBM] * 2,
        scratch=[
            pltpu.VMEM((PLANE, W_ROWS + REST, LANES), BF16),
            pltpu.VMEM((PLANE, W_ROWS + REST, LANES), BF16),
            pltpu.VMEM((2, 4, 256, 256), BF16),
            pltpu.VMEM((256, 256), F32),
            pltpu.VMEM((256, 256), F32),
            pltpu.SemaphoreType.DMA((2,)),
        ],
        mib=24,
    )(where, arrived, in_gain[None], o_own, o_other, gain, near, far, kept, in_hbm(held_other))

    positive_part, negative_part = call(
        plane_body, (shape((48, 256), F32), shape((256, LANES))), [VMEM]
    )(plane)
    owned = exchange(negative_part.reshape(ITEMS, 16, LANES), "item").reshape(256, LANES)
    item_grad = call(item_body, shape((32, 256), F32), [VMEM] * 5)(
        positive_part, hits, owned, hat_part, table_scale
    ).T
    return (layer_out, token_grad, item_grad)


def solution(mesh):
    return jax.shard_map(
        per_device,
        mesh=mesh,
        in_specs=(
            P(("user", "item"), None),
            P(("user", "item"), None),
            P(("user", "item"), None),
            P(("user", "item"), None),
            P(("user", "item")),
            P(),
            P("item", None),
            P(),
            P("item", None),
            P(),
            P(None, "item"),
        ),
        out_specs=(P(("user", "item"), None), P(("user", "item"), None), P("item", "user")),
        check_vma=False,
    )
```

```python
import jax
import jax.numpy as jnp
from jax import lax
from jax.experimental import pallas as pl
from jax.experimental.pallas import tpu as pltpu
from jax.sharding import PartitionSpec as P


norm_epsilon = 1e-05
scale_epsilon = 1e-06
inverse_temp = 20.0
loss_scale = 32.0

F32 = jnp.float32
BF16 = jnp.bfloat16

USERS = 32
ITEMS = 16
PLANE = 16
LANES = 128
ROWS = 512
MOST = 16
WIDTH = 1024
HEAD = 128

FIRST = [[x * 8 + y * 2 for x in range(4)] for y in range(4)] + [
    [x * 8 + y * 2 + 1 for y in range(4)] for x in range(4)
]
SECOND = [[x * 8 + y * 2 for y in range(4)] for x in range(4)] + [
    [x * 8 + y * 2 + 1 for x in range(4)] for y in range(4)
]
SAME_CORE = [[k * 2 + c for k in range(PLANE)] for c in range(2)]
PARTNER = [(k, k ^ 1) for k in range(USERS)]

VMEM = pl.BlockSpec(memory_space=pltpu.VMEM)
ANY = pl.BlockSpec(memory_space=pl.ANY)
HBM = pl.BlockSpec(memory_space=pltpu.HBM)
SMEM = pl.BlockSpec(memory_space=pltpu.SMEM)
W_ROWS = 512
REST = 208


def shape(dims, kind=BF16):
    return jax.ShapeDtypeStruct(dims, kind)


def dot(a, b, contract=((1,), (0,))):
    return lax.dot_general(a, b, (contract, ((), ())), preferred_element_type=F32)


def call(body, outs, specs, scratch=(), mib=8, out_specs=None):
    return pl.pallas_call(
        body,
        out_shape=outs,
        in_specs=specs,
        out_specs=out_specs or jax.tree.map(lambda _: VMEM, outs),
        scratch_shapes=list(scratch),
        compiler_params=pltpu.CompilerParams(vmem_limit_bytes=mib * 2**20),
    )


def column_of(row, n):
    eye = lax.broadcasted_iota(jnp.int32, (n, n), 0) == lax.broadcasted_iota(jnp.int32, (n, n), 1)
    return jnp.sum(jnp.where(eye, row, 0.0), axis=1, keepdims=True)


def reordered(rows):
    at = lax.broadcasted_iota(jnp.int32, (1, WIDTH), 1)
    wanted = (at % 512) // 32 * 64 + at // 512 * 32 + at % 32
    order = lax.broadcasted_iota(jnp.int32, (WIDTH, WIDTH), 0) == wanted
    return dot(rows, jnp.where(order, 1.0, 0.0).astype(BF16)).astype(BF16)


def message_body(
    where, neg_ref, w_ref, o_ref, table_ref, out_ref, neg, w_part, o_part, rows, turned, quads, sems
):
    item, core, place = where[0], where[1], where[2]
    chunk = lax.div(place, 2)
    block = lax.div(chunk, 2) * 4 + core * 2 + lax.rem(chunk, 2)
    copies = (
        pltpu.make_async_copy(
            w_ref.at[pl.ds((place % 2) * 32, 32), pl.ds(block * LANES, LANES)], w_part, sems.at[0]
        ),
        pltpu.make_async_copy(
            o_ref.at[:, pl.ds((core * 2 + place // 8) * LANES, LANES)], o_part, sems.at[1]
        ),
        pltpu.make_async_copy(table_ref.at[:, pl.ds(core * 512, 512)], rows, sems.at[2]),
        pltpu.make_async_copy(neg_ref, neg, sems.at[3]),
    )
    for copy in copies:
        copy.start()
    for copy in copies:
        copy.wait()
    lane = lax.broadcasted_iota(jnp.int32, (ITEMS, 256), 1)
    ids = jnp.sum(
        jnp.where(lane == item * 16 + place, neg[...].astype(F32), 0.0), axis=1, keepdims=True
    ).astype(jnp.int32)
    pick = jnp.where(lane == ids - item * 256, 1.0, 0.0).astype(BF16)
    turned[...] = jnp.transpose(o_part[...].astype(F32))
    part = turned[pl.ds((place % 8) * 16, 16), :]
    part = jnp.concatenate([part[0:8, :], part[8:16, :]], axis=1).astype(BF16)
    group = dot(pick, rows[...])
    quads[...] = jnp.zeros_like(quads)
    for b in range(4):
        quads[:, b, :] = group[:, b * LANES : (b + 1) * LANES]
    for i in range(ITEMS):
        out_ref[i, 0:32, :] = w_part[...]
        out_ref[i, 32:40, :] = part
    out_ref[:, 40:48, :] = quads[...].astype(BF16)


def prepare_body(where, *refs):
    sources, results = refs[:9], refs[9:18]
    scratch, (xs, parcels, lows, hat, turned, in_sems, out_sems) = refs[18:27], refs[27:]
    x_ref, cols_ref, label_ref, parcel_ref, low_ref, hat_ref, scale_ref, ids_ref, gain_ref = results
    tok, len_ref, dest_ref, off_ref, pos_ref, in_gain, tab, neg_ref, out_gain = scratch
    item, core, user = where[0], where[1], where[3]
    copies = [
        pltpu.make_async_copy(a, b, in_sems.at[n]) for n, (a, b) in enumerate(zip(sources, scratch))
    ]
    for copy in copies:
        copy.start()
    for copy in copies:
        copy.wait()
    late = [
        pltpu.make_async_copy(a, b, out_sems.at[n])
        for n, (a, b) in enumerate(((xs, x_ref), (parcels, parcel_ref), (lows, low_ref)))
    ]
    gain = out_gain[...]
    turned_gain = jnp.concatenate([gain[:, 256:512], gain[:, 0:256]], axis=1)
    gain_ref[...] = jnp.where(core == 0, gain, turned_gain)
    normed = layer_norm(tok[...].astype(F32), in_gain[...]).astype(BF16)
    xs[...] = reordered(normed)
    late[0].start()

    lens, dest, off = (r[...].astype(F32) for r in (len_ref, dest_ref, off_ref))
    sub = lax.broadcasted_iota(jnp.int32, (32, 32), 0)
    lane = lax.broadcasted_iota(jnp.int32, (32, 32), 1)
    len_col, dest_col, off_col = (column_of(v, 32) for v in (lens, dest, off))
    start_row = jnp.sum(jnp.where(sub < lane, len_col, 0.0), axis=0, keepdims=True)
    start_col = column_of(start_row, 32)
    row = lax.broadcasted_iota(jnp.int32, (ROWS, 32), 0).astype(F32)
    inside = (row >= start_row) & (row < start_row + lens)
    valid = jnp.sum(jnp.where(inside, 1.0, 0.0), axis=1, keepdims=True) > 0.5
    first = jnp.sum(jnp.where(inside, start_row, 0.0), axis=1, keepdims=True)
    first = jnp.where(valid, first, row[:, 0:1])
    weight = jnp.where(valid, loss_scale, 0.0)
    pos = jnp.transpose(jnp.broadcast_to(pos_ref[...].astype(F32), (LANES, ROWS)))
    at = lax.broadcasted_iota(jnp.int32, (ROWS, LANES), 1)
    local = pos - (item * 256).astype(F32)
    cols_ref[...] = jnp.where(at == 0, first, jnp.where(at == 1, weight, local))

    wide = lax.broadcasted_iota(jnp.int32, (32, LANES), 1).astype(F32)
    to_land = jnp.sum(jnp.where(wide == dest_col, off_col, 0.0), axis=0, keepdims=True)
    to_count = jnp.sum(jnp.where(wide - 32.0 == dest_col, len_col, 0.0), axis=0, keepdims=True)
    label_ref[...] = jnp.broadcast_to(to_land + to_count, (16, LANES)).astype(BF16)

    lane_f = lane.astype(F32)
    first_row = jnp.sum(jnp.where(lane_f == dest_col, start_col, 0.0), axis=0, keepdims=True)
    count_row = jnp.sum(jnp.where(lane_f == dest_col, len_col, 0.0), axis=0, keepdims=True)
    slot = lax.broadcasted_iota(jnp.int32, (ROWS, 32), 0)
    peer = lax.broadcasted_iota(jnp.int32, (ROWS, 32), 1) == slot // MOST
    begin = jnp.sum(jnp.where(peer, first_row, 0.0), axis=1, keepdims=True)
    count = jnp.sum(jnp.where(peer, count_row, 0.0), axis=1, keepdims=True)
    within = (slot[:, 0:1] % MOST).astype(F32)
    source = jnp.where(within < count, begin + within, -1.0)
    send = lax.broadcasted_iota(jnp.int32, (ROWS, ROWS), 1).astype(F32) == source
    parcels[...] = dot(jnp.where(send, 1.0, 0.0).astype(BF16), tok[...]).astype(BF16)
    late[1].start()

    table = tab[...].astype(F32)
    scale = lax.rsqrt(jnp.mean(table * table, axis=1, keepdims=True) + scale_epsilon)
    hat[...] = table * scale
    lows[...] = hat[...].astype(BF16)
    late[2].start()
    turned[...] = jnp.transpose(hat[:, pl.ds((user // 4) * LANES, LANES)])
    hat_ref[...] = turned[pl.ds((user % 4) * 32, 32), :]
    scale_ref[...] = jnp.transpose(jnp.broadcast_to(scale, (256, LANES)))[0:1, :]

    sub = lax.broadcasted_iota(jnp.int32, (ITEMS, 256), 0)
    group = jnp.sum(jnp.where(sub == item, neg_ref[...].astype(F32), 0.0), axis=0, keepdims=True)
    owner = lax.broadcasted_iota(jnp.int32, (1, 256), 1) // 16
    ids_ref[...] = group - (owner * 256).astype(F32)
    for copy in late:
        copy.wait()


def forward_body(got, label, out):
    for i in range(ITEMS):
        out[0, i * 32 : (i + 1) * 32, :] = got[i, 0:32, :]
    left = lax.broadcasted_iota(jnp.int32, (8, LANES), 1) < 64
    for b in range(8):
        even, odd = got[2 * b, 32:40, :].astype(F32), got[2 * b + 1, 32:40, :].astype(F32)
        top = jnp.where(left, even, pltpu.roll(odd, 64, 1))
        bottom = jnp.where(left, pltpu.roll(even, 64, 1), odd)
        out[0, W_ROWS + b * 16 : W_ROWS + (b + 1) * 16, :] = jnp.concatenate(
            [top, bottom], axis=0
        ).astype(BF16)
    quads = got[:, 40:48, :].astype(F32)
    for b in range(4):
        out[0, W_ROWS + 128 + b * 16 : W_ROWS + 144 + b * 16, :] = quads[:, b, :].astype(BF16)
    out[0, W_ROWS + 192 : W_ROWS + 208, :] = label[...]
    for g in range(1, 4):
        out[g] = out[0]


def project(x, w, q):
    both = jnp.concatenate(
        [
            jnp.concatenate([w[n, :W_ROWS, :], w[n + 1, :W_ROWS, :]], axis=0)
            for n in (4 * q, 4 * q + 2)
        ],
        axis=1,
    )
    return jax.nn.silu(dot(x, both)).astype(BF16)


def attend(act, first, mixed_ref):
    v, q, k = act[1], act[2], act[3]
    for b in range(first.shape[0] // 128):
        lo, hi = b * 128, (b + 1) * 128
        at = max(lo - 128, 0)
        rows = lo + lax.broadcasted_iota(jnp.int32, (128, hi - at), 0)
        cols = at + lax.broadcasted_iota(jnp.int32, (128, hi - at), 1)
        allowed = (cols >= first[lo:hi, :]) & (cols <= rows)
        for h in range(2):
            d0, d1 = h * HEAD, (h + 1) * HEAD
            scores = dot(q[lo:hi, d0:d1], k[at:hi, d0:d1], ((1,), (1,))) * HEAD ** (-0.5)
            weights = jnp.where(allowed, jax.nn.silu(scores), 0.0).astype(BF16)
            mixed_ref[lo:hi, d0:d1] = dot(weights, v[at:hi, d0:d1])


def split_rest(w, o_ref, g_ref, label_ref):
    for n in range(8):
        o_ref[:, n * LANES : (n + 1) * LANES] = w[
            :, W_ROWS + n * 16 : W_ROWS + (n + 1) * 16, :
        ].reshape(256, LANES)
    for n in range(4):
        g_ref[:, n * LANES : (n + 1) * LANES] = w[
            :, W_ROWS + 128 + n * 16 : W_ROWS + 144 + n * 16, :
        ].reshape(256, LANES)
    for n in range(PLANE):
        label_ref[n : n + 1, :] = w[n, W_ROWS + 192 : W_ROWS + 208, :].astype(F32)[0:1, :]


def layer_body(
    x_ref,
    w0,
    w1_ref,
    tok_ref,
    cols_ref,
    gain_ref,
    out_ref,
    o0_ref,
    o1_ref,
    g0,
    g1,
    near,
    far,
    kept_ref,
    o0,
    o1,
    x,
    w1,
    tok,
    act,
    m0,
    m1,
    sems,
):
    pairs = ((x_ref, x), (w1_ref, w1), (tok_ref, tok), (w0, kept_ref), (o0, o0_ref), (o1, o1_ref))
    copies = [pltpu.make_async_copy(a, b, sems.at[n]) for n, (a, b) in enumerate(pairs)]
    for copy in copies[:3]:
        copy.start()
    split_rest(w0, o0, g0, near)
    copies[4].start()
    first = cols_ref[:, 0:1].astype(jnp.int32)
    copies[0].wait()
    rows = x[...]
    for q in range(4):
        act[0, q] = project(rows, w0, q)
    attend(act.at[0], first, m0)
    copies[1].wait()
    copies[3].start()
    split_rest(w1, o1, g1, far)
    copies[5].start()
    for q in range(4):
        act[1, q] = project(rows, w1, q)
    attend(act.at[1], first, m1)
    copies[2].wait()
    out_ref[...] = gated_out(tok[...], act.at[0, 0], m0, o0, act.at[1, 0], m1, o1, gain_ref)
    for copy in copies[3:]:
        copy.wait()


def gated_out(rows, u0, m0, o0, u1, m1, o1, gain_ref):
    a, b = m0[...], m1[...]
    width = 512.0
    center = (jnp.sum(a, axis=1, keepdims=True) + jnp.sum(b, axis=1, keepdims=True)) / width
    a, b = a - center, b - center
    spread = (
        jnp.sum(a * a, axis=1, keepdims=True) + jnp.sum(b * b, axis=1, keepdims=True)
    ) / width
    inv = lax.rsqrt(spread + norm_epsilon)
    ga = (a * inv * gain_ref[:, 0:256] * u0[...].astype(F32)).astype(BF16)
    gb = (b * inv * gain_ref[:, 256:512] * u1[...].astype(F32)).astype(BF16)
    delta = dot(ga, o0[...]) + dot(gb, o1[...])
    return (rows.astype(F32) + delta).astype(BF16)


def worker_body(
    where,
    got_ref,
    in_gain,
    o0_ref,
    o1_ref,
    gain_ref,
    near,
    far,
    w0_ref,
    w1_ref,
    out_ref,
    w0,
    w1,
    o0,
    o1,
    act,
    m0,
    m1,
    sems,
):
    core, user = where[1], where[3]
    pairs = ((w0_ref, w0), (w1_ref, w1), (o0_ref, o0), (o1_ref, o1))
    copies = [pltpu.make_async_copy(a, b, sems.at[n]) for n, (a, b) in enumerate(pairs)]
    for copy in copies:
        copy.start()
    lane = lax.broadcasted_iota(jnp.int32, (PLANE, LANES), 1)
    sub = lax.broadcasted_iota(jnp.int32, (PLANE, ROWS), 0)
    slot = lax.broadcasted_iota(jnp.int32, (1, ROWS), 1)
    peer = slot // MOST
    x, y, c = peer // 8, peer // 2 % 4, peer % 2
    spot = jnp.where(c == 0, y * 4 + x, x * 4 + y)

    def of_peer(at):
        total = 0.0
        for ref, mine in ((near, c == core), (far, c != core)):
            value = jnp.sum(jnp.where(lane == at, ref[...], 0.0), axis=1, keepdims=True)
            total = total + jnp.sum(
                jnp.where((sub == spot) & mine, value, 0.0), axis=0, keepdims=True
            )
        return total

    lower, count = of_peer(user), of_peer(user + USERS)
    within = (slot % MOST).astype(F32)
    lands = jnp.where(within < count, lower + within, -1.0)
    here = lax.broadcasted_iota(jnp.int32, (256, ROWS), 0).astype(F32) == lands
    first = jnp.sum(jnp.where(here, lower, 0.0), axis=1, keepdims=True).astype(jnp.int32)
    rows = dot(jnp.where(here, 1.0, 0.0).astype(BF16), got_ref[...]).astype(BF16)
    normed = layer_norm(rows.astype(F32), in_gain[...]).astype(BF16)
    moved = reordered(normed)
    for half, (w, m) in enumerate(((w0, m0), (w1, m1))):
        copies[half].wait()
        for q in range(4):
            act[half, q] = project(moved, w, q)
        attend(act.at[half], first, m)
    copies[2].wait()
    copies[3].wait()
    out_ref[...] = gated_out(rows, act.at[0, 0], m0, o0, act.at[1, 0], m1, o1, gain_ref)


def loss_body(
    where,
    out_ref,
    low_ref,
    cols_ref,
    g0_ref,
    g1_ref,
    grad_ref,
    own_ref,
    send_ref,
    own_inner,
    terms,
):
    c = where[1]

    row = lax.broadcasted_iota(jnp.int32, (256, 256), 0)
    col = lax.broadcasted_iota(jnp.int32, (256, 256), 1)
    swap = jnp.where(col == row % 16 * 16 + row // 16, 1.0, 0.0).astype(BF16)
    g0, g1 = dot(swap, g0_ref[...]), dot(swap, g1_ref[...])
    size = (jnp.sum(g0 * g0, axis=1, keepdims=True) + jnp.sum(g1 * g1, axis=1, keepdims=True)) / WIDTH
    scale = lax.rsqrt(size + scale_epsilon)
    g0, g1 = (g0 * scale).astype(BF16), (g1 * scale).astype(BF16)
    here = c == 0
    group = jnp.concatenate([jnp.where(here, g0, g1), jnp.where(here, g1, g0)], axis=1)
    rows = jnp.concatenate([low_ref[...], group], axis=0)

    out = out_ref[...].astype(F32)
    out_scale = lax.rsqrt(jnp.mean(out * out, axis=1, keepdims=True) + scale_epsilon)
    hat = out * out_scale
    low = hat.astype(BF16)
    factor = inverse_temp / WIDTH
    raw = dot(low, rows, ((1,), (1,)))
    hit = lax.broadcasted_iota(jnp.int32, (ROWS, 256), 1) == cols_ref[:, 2:3].astype(jnp.int32)
    pos = jnp.exp(jnp.sum(jnp.where(hit, raw[:, :256], 0.0), axis=1, keepdims=True) * factor)
    neg = jnp.exp(raw[:, 256:] * factor)
    total = pos + jnp.sum(neg, axis=1, keepdims=True)
    weight = cols_ref[:, 1:2]
    pos_grad = weight * (pos / total - 1.0)
    grads = jnp.concatenate(
        [jnp.where(hit, pos_grad, 0.0).astype(BF16), (weight * neg / total).astype(BF16)], axis=1
    )
    grad_hat = dot(grads, rows) * factor
    inner = jnp.mean(grad_hat * hat, axis=1, keepdims=True)
    grad_ref[...] = ((grad_hat - hat * inner) * out_scale).astype(BF16)
    sums = dot(low, grads, ((0,), (0,))) * factor
    terms[...] = sums.astype(BF16).reshape(PLANE, 2, 32, ROWS)
    for k in range(PLANE):
        own_ref[k] = terms[k, c]
        send_ref[k * 32 : (k + 1) * 32, :] = terms[k, 1 - c]
    products = jnp.sum(grads.astype(F32) * raw, axis=0, keepdims=True) * factor
    own_inner[...] = products
    top = products.astype(BF16).astype(F32)
    send_ref[512:528, :] = split_rows(top, products - top).astype(BF16)


def split_rows(top, rest):
    at = lax.broadcasted_iota(jnp.int32, (16, ROWS), 0)
    return jnp.where(at == 0, top, jnp.where(at == 1, rest, 0.0))


def pair_body(own_ref, inner_ref, got_ref, out_ref):
    other = got_ref[512:528, :].astype(F32)
    inner = inner_ref[...] + other[0:1, :] + other[1:2, :]
    top = inner.astype(BF16).astype(F32)
    tail = split_rows(top, inner - top).astype(BF16)
    for k in range(PLANE):
        mine = own_ref[k].astype(F32) + got_ref[k * 32 : (k + 1) * 32, :].astype(F32)
        out_ref[k, 0:32, :] = mine.astype(BF16)
        out_ref[k, 32:40, :] = tail[0:8, :]


def plane_body(got_ref, ids_ref, pos_ref, neg_ref):
    acc = got_ref[0].astype(F32)
    for k in range(1, PLANE):
        acc = acc + got_ref[k].astype(F32)
    inner = acc[32:33, :] + acc[33:34, :]
    top = inner.astype(BF16).astype(F32)
    full = jnp.concatenate([acc[0:32, :], split_rows(top, inner - top)], axis=0)
    pos_ref[...] = full[:, 0:256]
    tail = jnp.concatenate(
        [full[0:34, 256:512], ids_ref[...], jnp.zeros((93, 256), F32)], axis=0
    )
    neg_ref[...] = jnp.transpose(tail).astype(BF16)


def item_body(pos_ref, got_ref, hat_ref, scale_ref, out_ref):
    got = got_ref[...]
    ids = got.astype(F32)[:, 34:35]
    hits = lax.broadcasted_iota(jnp.int32, (256, 256), 1).astype(F32) == ids
    hits = jnp.where(hits, 1.0, 0.0).astype(BF16)
    total = pos_ref[...] + dot(got, hits, ((0,), (0,)))[0:48, :]
    inner = (total[32:33, :] + total[33:34, :]) / WIDTH
    out_ref[...] = (total[0:32, :] - hat_ref[...] * inner) * scale_ref[...]


def layer_norm(values, gain):
    center = jnp.mean(values, axis=-1, keepdims=True)
    shifted = values - center
    spread = jnp.mean(shifted * shifted, axis=-1, keepdims=True)
    return shifted * lax.rsqrt(spread + norm_epsilon) * gain


def in_hbm(values):
    return pltpu.with_memory_space_constraint(values, pltpu.HBM)


def copies(block, count):
    return jnp.broadcast_to(block[None], (count, *block.shape))


def exchange(blocks, axis, groups=None):
    return lax.all_to_all(blocks, axis, 0, 0, tiled=True, axis_index_groups=groups)


def per_device(
    tokens,
    lengths,
    destination,
    worker_offset,
    positives,
    negatives,
    table,
    in_gain,
    w_uvqk,
    out_gain,
    w_out,
):
    item = lax.axis_index("item")
    user = lax.axis_index("user")
    core = user & 1
    x, y = user >> 3, (user >> 1) & 3
    place = jnp.where(core == 0, y * 4 + x, x * 4 + y)
    where = jnp.stack([item, core, place, user]).astype(jnp.int32)

    first_message = call(
        message_body,
        shape((ITEMS, 48, LANES)),
        [SMEM, HBM, HBM, HBM, HBM],
        scratch=[
            pltpu.VMEM((ITEMS, 256), jnp.int32),
            pltpu.VMEM((32, LANES), BF16),
            pltpu.VMEM((64, LANES), BF16),
            pltpu.VMEM((256, 512), BF16),
            pltpu.VMEM((LANES, 64), F32),
            pltpu.VMEM((ITEMS, 8, LANES), F32),
            pltpu.SemaphoreType.DMA((4,)),
        ],
    )(where, in_hbm(negatives), in_hbm(w_uvqk), in_hbm(w_out.T), in_hbm(table))
    got = exchange(first_message, "item")

    x_rows, cols, labels, parcels, table_low, hat_part, table_scale, group_ids, gain = call(
        prepare_body,
        (
            pltpu.HBM((ROWS, WIDTH), BF16),
            shape((ROWS, LANES), F32),
            shape((16, LANES)),
            pltpu.HBM((ROWS, WIDTH), BF16),
            pltpu.HBM((256, WIDTH), BF16),
            shape((32, 256), F32),
            shape((1, 256), F32),
            shape((1, 256), F32),
            shape((1, 512), F32),
        ),
        [SMEM] + [HBM] * 9,
        scratch=[
            pltpu.VMEM((ROWS, WIDTH), BF16),
            pltpu.VMEM((1, 32), jnp.int32),
            pltpu.VMEM((1, 32), jnp.int32),
            pltpu.VMEM((1, 32), jnp.int32),
            pltpu.VMEM((1, ROWS), jnp.int32),
            pltpu.VMEM((1, WIDTH), F32),
            pltpu.VMEM((256, WIDTH), BF16),
            pltpu.VMEM((ITEMS, 256), jnp.int32),
            pltpu.VMEM((1, 512), F32),
            pltpu.VMEM((ROWS, WIDTH), BF16),
            pltpu.VMEM((ROWS, WIDTH), BF16),
            pltpu.VMEM((256, WIDTH), BF16),
            pltpu.VMEM((256, WIDTH), F32),
            pltpu.VMEM((LANES, 256), F32),
            pltpu.SemaphoreType.DMA((9,)),
            pltpu.SemaphoreType.DMA((3,)),
        ],
        mib=28,
        out_specs=(HBM, VMEM, VMEM, HBM, HBM, VMEM, VMEM, VMEM, VMEM),
    )(
        where,
        *(
            in_hbm(v)
            for v in (
                tokens,
                lengths,
                destination,
                worker_offset,
                positives[None],
                in_gain[None],
                table,
                negatives,
                out_gain[None],
            )
        ),
    )
    got, x_rows, gain = lax.optimization_barrier((got, x_rows, gain))

    message = call(forward_body, shape((4, W_ROWS + REST, LANES)), [VMEM, VMEM])(got, labels)
    mid = exchange(message, "user", FIRST).reshape(4 * (W_ROWS + REST), LANES)
    held = exchange(copies(mid, 4), "user", SECOND).reshape(PLANE, W_ROWS + REST, LANES)
    held, parcels = lax.optimization_barrier((held, parcels))
    held_other = lax.ppermute(held, "user", PARTNER)
    arrived = exchange(parcels.reshape(USERS, MOST, WIDTH), "user").reshape(ROWS, WIDTH)

    home_out, o_own, o_other, g_own, g_other, near, far, kept = call(
        layer_body,
        (
            shape((ROWS, WIDTH)),
            pltpu.HBM((256, WIDTH), BF16),
            pltpu.HBM((256, WIDTH), BF16),
            shape((256, 512)),
            shape((256, 512)),
            shape((PLANE, LANES), F32),
            shape((PLANE, LANES), F32),
            pltpu.HBM((PLANE, W_ROWS + REST, LANES), BF16),
        ),
        [HBM, VMEM, HBM, HBM, VMEM, VMEM],
        scratch=[
            pltpu.VMEM((256, WIDTH), BF16),
            pltpu.VMEM((256, WIDTH), BF16),
            pltpu.VMEM((ROWS, WIDTH), BF16),
            pltpu.VMEM((PLANE, W_ROWS + REST, LANES), BF16),
            pltpu.VMEM((ROWS, WIDTH), BF16),
            pltpu.VMEM((2, 4, ROWS, 256), BF16),
            pltpu.VMEM((ROWS, 256), F32),
            pltpu.VMEM((ROWS, 256), F32),
            pltpu.SemaphoreType.DMA((6,)),
        ],
        mib=20,
        out_specs=(VMEM, HBM, HBM, VMEM, VMEM, VMEM, VMEM, HBM),
    )(in_hbm(x_rows), held, in_hbm(held_other), in_hbm(tokens), cols, gain)

    token_grad, own_terms, sent, own_inner = call(
        loss_body,
        (
            shape((ROWS, WIDTH)),
            shape((PLANE, 32, ROWS)),
            shape((528, ROWS)),
            shape((1, ROWS), F32),
        ),
        [SMEM] + [VMEM] * 5,
        scratch=[pltpu.VMEM((PLANE, 2, 32, ROWS), BF16)],
        mib=16,
    )(where, home_out, table_low, cols, g_own, g_other)
    partner_terms = lax.ppermute(sent, "user", PARTNER)
    pair = call(pair_body, pltpu.HBM((PLANE, 40, ROWS), BF16), [VMEM] * 3, out_specs=VMEM)(
        own_terms, own_inner, partner_terms
    )
    pair, arrived = lax.optimization_barrier((pair, arrived))
    plane = exchange(pair, "user", SAME_CORE)

    layer_out = call(
        worker_body,
        shape((256, WIDTH)),
        [SMEM, VMEM, VMEM, HBM, HBM, VMEM, VMEM, VMEM, HBM, HBM],
        scratch=[
            pltpu.VMEM((PLANE, W_ROWS + REST, LANES), BF16),
            pltpu.VMEM((PLANE, W_ROWS + REST, LANES), BF16),
            pltpu.VMEM((256, WIDTH), BF16),
            pltpu.VMEM((256, WIDTH), BF16),
            pltpu.VMEM((2, 4, 256, 256), BF16),
            pltpu.VMEM((256, 256), F32),
            pltpu.VMEM((256, 256), F32),
            pltpu.SemaphoreType.DMA((4,)),
        ],
        mib=24,
    )(where, arrived, in_gain[None], o_own, o_other, gain, near, far, kept, in_hbm(held_other))

    positive_part, negative_part = call(
        plane_body, (shape((48, 256), F32), shape((256, LANES))), [VMEM] * 2
    )(plane, group_ids)
    owned = exchange(negative_part.reshape(ITEMS, 16, LANES), "item").reshape(256, LANES)
    item_grad = call(item_body, shape((32, 256), F32), [VMEM] * 4)(
        positive_part, owned, hat_part, table_scale
    ).T
    return (layer_out, token_grad, item_grad)


def solution(mesh):
    return jax.shard_map(
        per_device,
        mesh=mesh,
        in_specs=(
            P(("user", "item"), None),
            P(("user", "item"), None),
            P(("user", "item"), None),
            P(("user", "item"), None),
            P(("user", "item")),
            P(),
            P("item", None),
            P(),
            P("item", None),
            P(),
            P(None, "item"),
        ),
        out_specs=(P(("user", "item"), None), P(("user", "item"), None), P("item", "user")),
        check_vma=False,
    )
```

```python
import jax
import jax.numpy as jnp
from jax import lax
from jax.experimental import pallas as pl
from jax.experimental.pallas import tpu as pltpu
from jax.sharding import PartitionSpec as P


norm_epsilon = 1e-05
scale_epsilon = 1e-06
inverse_temp = 20.0
loss_scale = 32.0

F32 = jnp.float32
BF16 = jnp.bfloat16

USERS = 32
ITEMS = 16
PLANE = 16
LANES = 128
ROWS = 512
MOST = 16
WIDTH = 1024
HEAD = 128

FIRST = [[x * 8 + y * 2 for x in range(4)] for y in range(4)] + [
    [x * 8 + y * 2 + 1 for y in range(4)] for x in range(4)
]
SECOND = [[x * 8 + y * 2 for y in range(4)] for x in range(4)] + [
    [x * 8 + y * 2 + 1 for x in range(4)] for y in range(4)
]
SAME_CORE = [[k * 2 + c for k in range(PLANE)] for c in range(2)]
PARTNER = [(k, k ^ 1) for k in range(USERS)]

VMEM = pl.BlockSpec(memory_space=pltpu.VMEM)
ANY = pl.BlockSpec(memory_space=pl.ANY)
HBM = pl.BlockSpec(memory_space=pltpu.HBM)
SMEM = pl.BlockSpec(memory_space=pltpu.SMEM)
W_ROWS = 512
REST = 208


def shape(dims, kind=BF16):
    return jax.ShapeDtypeStruct(dims, kind)


def dot(a, b, contract=((1,), (0,))):
    return lax.dot_general(a, b, (contract, ((), ())), preferred_element_type=F32)


def call(body, outs, specs, scratch=(), mib=8, out_specs=None):
    return pl.pallas_call(
        body,
        out_shape=outs,
        in_specs=specs,
        out_specs=out_specs or jax.tree.map(lambda _: VMEM, outs),
        scratch_shapes=list(scratch),
        compiler_params=pltpu.CompilerParams(vmem_limit_bytes=mib * 2**20),
    )


def column_of(row, n):
    eye = lax.broadcasted_iota(jnp.int32, (n, n), 0) == lax.broadcasted_iota(jnp.int32, (n, n), 1)
    return jnp.sum(jnp.where(eye, row, 0.0), axis=1, keepdims=True)


def reordered(rows):
    at = lax.broadcasted_iota(jnp.int32, (1, WIDTH), 1)
    wanted = (at % 512) // 32 * 64 + at // 512 * 32 + at % 32
    order = lax.broadcasted_iota(jnp.int32, (WIDTH, WIDTH), 0) == wanted
    return dot(rows, jnp.where(order, 1.0, 0.0).astype(BF16)).astype(BF16)


def message_body(
    where, neg_ref, w_ref, o_ref, table_ref, out_ref, neg, w_part, o_part, rows, turned, quads, sems
):
    item, core, place = where[0], where[1], where[2]
    chunk = lax.div(place, 2)
    block = lax.div(chunk, 2) * 4 + core * 2 + lax.rem(chunk, 2)
    copies = (
        pltpu.make_async_copy(
            w_ref.at[pl.ds((place % 2) * 32, 32), pl.ds(block * LANES, LANES)], w_part, sems.at[0]
        ),
        pltpu.make_async_copy(
            o_ref.at[:, pl.ds((core * 2 + place // 8) * LANES, LANES)], o_part, sems.at[1]
        ),
        pltpu.make_async_copy(table_ref.at[:, pl.ds(core * 512, 512)], rows, sems.at[2]),
        pltpu.make_async_copy(neg_ref, neg, sems.at[3]),
    )
    for copy in copies:
        copy.start()
    for copy in copies:
        copy.wait()
    lane = lax.broadcasted_iota(jnp.int32, (ITEMS, 256), 1)
    ids = jnp.sum(
        jnp.where(lane == item * 16 + place, neg[...].astype(F32), 0.0), axis=1, keepdims=True
    ).astype(jnp.int32)
    pick = jnp.where(lane == ids - item * 256, 1.0, 0.0).astype(BF16)
    turned[...] = jnp.transpose(o_part[...].astype(F32))
    part = turned[pl.ds((place % 8) * 16, 16), :]
    part = jnp.concatenate([part[0:8, :], part[8:16, :]], axis=1).astype(BF16)
    group = dot(pick, rows[...])
    quads[...] = jnp.zeros_like(quads)
    for b in range(4):
        quads[:, b, :] = group[:, b * LANES : (b + 1) * LANES]
    for i in range(ITEMS):
        out_ref[i, 0:32, :] = w_part[...]
        out_ref[i, 32:40, :] = part
    out_ref[:, 40:48, :] = quads[...].astype(BF16)


def prepare_body(where, *refs):
    sources, results = refs[:9], refs[9:18]
    scratch, (xs, parcels, lows, hat, turned, in_sems, out_sems) = refs[18:27], refs[27:]
    x_ref, cols_ref, label_ref, parcel_ref, low_ref, hat_ref, scale_ref, ids_ref, gain_ref = results
    tok, len_ref, dest_ref, off_ref, pos_ref, in_gain, tab, neg_ref, out_gain = scratch
    item, core, user = where[0], where[1], where[3]
    copies = [
        pltpu.make_async_copy(a, b, in_sems.at[n]) for n, (a, b) in enumerate(zip(sources, scratch))
    ]
    for copy in copies:
        copy.start()
    for copy in copies:
        copy.wait()
    late = [
        pltpu.make_async_copy(a, b, out_sems.at[n])
        for n, (a, b) in enumerate(((xs, x_ref), (parcels, parcel_ref), (lows, low_ref)))
    ]
    gain = out_gain[...]
    turned_gain = jnp.concatenate([gain[:, 256:512], gain[:, 0:256]], axis=1)
    gain_ref[...] = jnp.where(core == 0, gain, turned_gain)
    normed = layer_norm(tok[...].astype(F32), in_gain[...]).astype(BF16)
    xs[...] = reordered(normed)
    late[0].start()

    lens, dest, off = (r[...].astype(F32) for r in (len_ref, dest_ref, off_ref))
    sub = lax.broadcasted_iota(jnp.int32, (32, 32), 0)
    lane = lax.broadcasted_iota(jnp.int32, (32, 32), 1)
    len_col, dest_col, off_col = (column_of(v, 32) for v in (lens, dest, off))
    start_row = jnp.sum(jnp.where(sub < lane, len_col, 0.0), axis=0, keepdims=True)
    start_col = column_of(start_row, 32)
    row = lax.broadcasted_iota(jnp.int32, (ROWS, 32), 0).astype(F32)
    inside = (row >= start_row) & (row < start_row + lens)
    valid = jnp.sum(jnp.where(inside, 1.0, 0.0), axis=1, keepdims=True) > 0.5
    first = jnp.sum(jnp.where(inside, start_row, 0.0), axis=1, keepdims=True)
    first = jnp.where(valid, first, row[:, 0:1])
    weight = jnp.where(valid, loss_scale, 0.0)
    pos = jnp.transpose(jnp.broadcast_to(pos_ref[...].astype(F32), (LANES, ROWS)))
    at = lax.broadcasted_iota(jnp.int32, (ROWS, LANES), 1)
    local = pos - (item * 256).astype(F32)
    cols_ref[...] = jnp.where(at == 0, first, jnp.where(at == 1, weight, local))

    wide = lax.broadcasted_iota(jnp.int32, (32, LANES), 1).astype(F32)
    to_land = jnp.sum(jnp.where(wide == dest_col, off_col, 0.0), axis=0, keepdims=True)
    to_count = jnp.sum(jnp.where(wide - 32.0 == dest_col, len_col, 0.0), axis=0, keepdims=True)
    label_ref[...] = jnp.broadcast_to(to_land + to_count, (16, LANES)).astype(BF16)

    lane_f = lane.astype(F32)
    first_row = jnp.sum(jnp.where(lane_f == dest_col, start_col, 0.0), axis=0, keepdims=True)
    count_row = jnp.sum(jnp.where(lane_f == dest_col, len_col, 0.0), axis=0, keepdims=True)
    slot = lax.broadcasted_iota(jnp.int32, (ROWS, 32), 0)
    peer = lax.broadcasted_iota(jnp.int32, (ROWS, 32), 1) == slot // MOST
    begin = jnp.sum(jnp.where(peer, first_row, 0.0), axis=1, keepdims=True)
    count = jnp.sum(jnp.where(peer, count_row, 0.0), axis=1, keepdims=True)
    within = (slot[:, 0:1] % MOST).astype(F32)
    source = jnp.where(within < count, begin + within, -1.0)
    send = lax.broadcasted_iota(jnp.int32, (ROWS, ROWS), 1).astype(F32) == source
    parcels[...] = dot(jnp.where(send, 1.0, 0.0).astype(BF16), tok[...]).astype(BF16)
    late[1].start()

    table = tab[...].astype(F32)
    scale = lax.rsqrt(jnp.mean(table * table, axis=1, keepdims=True) + scale_epsilon)
    hat[...] = table * scale
    lows[...] = hat[...].astype(BF16)
    late[2].start()
    turned[...] = jnp.transpose(hat[:, pl.ds((user // 4) * LANES, LANES)])
    hat_ref[...] = turned[pl.ds((user % 4) * 32, 32), :]
    scale_ref[...] = jnp.transpose(jnp.broadcast_to(scale, (256, LANES)))[0:1, :]

    sub = lax.broadcasted_iota(jnp.int32, (ITEMS, 256), 0)
    group = jnp.sum(jnp.where(sub == item, neg_ref[...].astype(F32), 0.0), axis=0, keepdims=True)
    owner = lax.broadcasted_iota(jnp.int32, (1, 256), 1) // 16
    ids_ref[...] = group - (owner * 256).astype(F32)
    for copy in late:
        copy.wait()


def forward_body(got, label, out):
    for i in range(ITEMS):
        out[0, i * 32 : (i + 1) * 32, :] = got[i, 0:32, :]
    left = lax.broadcasted_iota(jnp.int32, (8, LANES), 1) < 64
    for b in range(8):
        even, odd = got[2 * b, 32:40, :].astype(F32), got[2 * b + 1, 32:40, :].astype(F32)
        top = jnp.where(left, even, pltpu.roll(odd, 64, 1))
        bottom = jnp.where(left, pltpu.roll(even, 64, 1), odd)
        out[0, W_ROWS + b * 16 : W_ROWS + (b + 1) * 16, :] = jnp.concatenate(
            [top, bottom], axis=0
        ).astype(BF16)
    quads = got[:, 40:48, :].astype(F32)
    for b in range(4):
        out[0, W_ROWS + 128 + b * 16 : W_ROWS + 144 + b * 16, :] = quads[:, b, :].astype(BF16)
    out[0, W_ROWS + 192 : W_ROWS + 208, :] = label[...]
    for g in range(1, 4):
        out[g] = out[0]


def project(x, w, q):
    both = jnp.concatenate(
        [
            jnp.concatenate([w[n, :W_ROWS, :], w[n + 1, :W_ROWS, :]], axis=0)
            for n in (4 * q, 4 * q + 2)
        ],
        axis=1,
    )
    return jax.nn.silu(dot(x, both)).astype(BF16)


def attend(act, first, mixed_ref):
    v, q, k = act[1], act[2], act[3]
    for b in range(first.shape[0] // 128):
        lo, hi = b * 128, (b + 1) * 128
        at = max(lo - 128, 0)
        rows = lo + lax.broadcasted_iota(jnp.int32, (128, hi - at), 0)
        cols = at + lax.broadcasted_iota(jnp.int32, (128, hi - at), 1)
        allowed = (cols >= first[lo:hi, :]) & (cols <= rows)
        for h in range(2):
            d0, d1 = h * HEAD, (h + 1) * HEAD
            scores = dot(q[lo:hi, d0:d1], k[at:hi, d0:d1], ((1,), (1,))) * HEAD ** (-0.5)
            weights = jnp.where(allowed, jax.nn.silu(scores), 0.0).astype(BF16)
            mixed_ref[lo:hi, d0:d1] = dot(weights, v[at:hi, d0:d1])


def split_rest(w, o_ref, g_ref, label_ref):
    for n in range(8):
        o_ref[:, n * LANES : (n + 1) * LANES] = w[
            :, W_ROWS + n * 16 : W_ROWS + (n + 1) * 16, :
        ].reshape(256, LANES)
    for n in range(4):
        g_ref[:, n * LANES : (n + 1) * LANES] = w[
            :, W_ROWS + 128 + n * 16 : W_ROWS + 144 + n * 16, :
        ].reshape(256, LANES)
    for n in range(PLANE):
        label_ref[n : n + 1, :] = w[n, W_ROWS + 192 : W_ROWS + 208, :].astype(F32)[0:1, :]


def layer_body(
    x_ref,
    w0,
    w1_ref,
    tok_ref,
    cols_ref,
    gain_ref,
    out_ref,
    o0_ref,
    o1_ref,
    g0,
    g1,
    near,
    far,
    kept_ref,
    o0,
    o1,
    x,
    w1,
    tok,
    act,
    m0,
    m1,
    sems,
):
    pairs = ((x_ref, x), (w1_ref, w1), (tok_ref, tok), (w0, kept_ref), (o0, o0_ref), (o1, o1_ref))
    copies = [pltpu.make_async_copy(a, b, sems.at[n]) for n, (a, b) in enumerate(pairs)]
    for copy in copies[:3]:
        copy.start()
    split_rest(w0, o0, g0, near)
    copies[4].start()
    first = cols_ref[:, 0:1].astype(jnp.int32)
    copies[0].wait()
    rows = x[...]
    for q in range(4):
        act[0, q] = project(rows, w0, q)
    attend(act.at[0], first, m0)
    copies[1].wait()
    copies[3].start()
    split_rest(w1, o1, g1, far)
    copies[5].start()
    for q in range(4):
        act[1, q] = project(rows, w1, q)
    attend(act.at[1], first, m1)
    copies[2].wait()
    out_ref[...] = gated_out(tok[...], act.at[0, 0], m0, o0, act.at[1, 0], m1, o1, gain_ref)
    for copy in copies[3:]:
        copy.wait()


def gated_out(rows, u0, m0, o0, u1, m1, o1, gain_ref):
    a, b = m0[...], m1[...]
    width = 512.0
    center = (jnp.sum(a, axis=1, keepdims=True) + jnp.sum(b, axis=1, keepdims=True)) / width
    a, b = a - center, b - center
    spread = (
        jnp.sum(a * a, axis=1, keepdims=True) + jnp.sum(b * b, axis=1, keepdims=True)
    ) / width
    inv = lax.rsqrt(spread + norm_epsilon)
    ga = (a * inv * gain_ref[:, 0:256] * u0[...].astype(F32)).astype(BF16)
    gb = (b * inv * gain_ref[:, 256:512] * u1[...].astype(F32)).astype(BF16)
    delta = dot(ga, o0[...]) + dot(gb, o1[...])
    return (rows.astype(F32) + delta).astype(BF16)


def worker_body(
    where,
    got_ref,
    in_gain,
    o0_ref,
    o1_ref,
    gain_ref,
    near,
    far,
    w0_ref,
    w1_ref,
    out_ref,
    w0,
    w1,
    o0,
    o1,
    act,
    m0,
    m1,
    sems,
):
    core, user = where[1], where[3]
    pairs = ((w0_ref, w0), (w1_ref, w1), (o0_ref, o0), (o1_ref, o1))
    copies = [pltpu.make_async_copy(a, b, sems.at[n]) for n, (a, b) in enumerate(pairs)]
    for copy in copies:
        copy.start()
    lane = lax.broadcasted_iota(jnp.int32, (PLANE, LANES), 1)
    sub = lax.broadcasted_iota(jnp.int32, (PLANE, ROWS), 0)
    slot = lax.broadcasted_iota(jnp.int32, (1, ROWS), 1)
    peer = slot // MOST
    x, y, c = peer // 8, peer // 2 % 4, peer % 2
    spot = jnp.where(c == 0, y * 4 + x, x * 4 + y)

    def of_peer(at):
        total = 0.0
        for ref, mine in ((near, c == core), (far, c != core)):
            value = jnp.sum(jnp.where(lane == at, ref[...], 0.0), axis=1, keepdims=True)
            total = total + jnp.sum(
                jnp.where((sub == spot) & mine, value, 0.0), axis=0, keepdims=True
            )
        return total

    lower, count = of_peer(user), of_peer(user + USERS)
    within = (slot % MOST).astype(F32)
    lands = jnp.where(within < count, lower + within, -1.0)
    here = lax.broadcasted_iota(jnp.int32, (256, ROWS), 0).astype(F32) == lands
    first = jnp.sum(jnp.where(here, lower, 0.0), axis=1, keepdims=True).astype(jnp.int32)
    rows = dot(jnp.where(here, 1.0, 0.0).astype(BF16), got_ref[...]).astype(BF16)
    normed = layer_norm(rows.astype(F32), in_gain[...]).astype(BF16)
    moved = reordered(normed)
    for half, (w, m) in enumerate(((w0, m0), (w1, m1))):
        copies[half].wait()
        for q in range(4):
            act[half, q] = project(moved, w, q)
        attend(act.at[half], first, m)
    copies[2].wait()
    copies[3].wait()
    out_ref[...] = gated_out(rows, act.at[0, 0], m0, o0, act.at[1, 0], m1, o1, gain_ref)


def loss_body(
    where,
    out_ref,
    low_ref,
    cols_ref,
    g0_ref,
    g1_ref,
    grad_ref,
    own_ref,
    send_ref,
    own_inner,
    terms,
    grad,
    sem,
):
    c = where[1]
    out_copy = pltpu.make_async_copy(grad, grad_ref, sem)

    row = lax.broadcasted_iota(jnp.int32, (256, 256), 0)
    col = lax.broadcasted_iota(jnp.int32, (256, 256), 1)
    swap = jnp.where(col == row % 16 * 16 + row // 16, 1.0, 0.0).astype(BF16)
    g0, g1 = dot(swap, g0_ref[...]), dot(swap, g1_ref[...])
    size = (jnp.sum(g0 * g0, axis=1, keepdims=True) + jnp.sum(g1 * g1, axis=1, keepdims=True)) / WIDTH
    scale = lax.rsqrt(size + scale_epsilon)
    g0, g1 = (g0 * scale).astype(BF16), (g1 * scale).astype(BF16)
    here = c == 0
    group = jnp.concatenate([jnp.where(here, g0, g1), jnp.where(here, g1, g0)], axis=1)
    rows = jnp.concatenate([low_ref[...], group], axis=0)

    out = out_ref[...].astype(F32)
    out_scale = lax.rsqrt(jnp.mean(out * out, axis=1, keepdims=True) + scale_epsilon)
    hat = out * out_scale
    low = hat.astype(BF16)
    factor = inverse_temp / WIDTH
    raw = dot(low, rows, ((1,), (1,)))
    hit = lax.broadcasted_iota(jnp.int32, (ROWS, 256), 1) == cols_ref[:, 2:3].astype(jnp.int32)
    pos = jnp.exp(jnp.sum(jnp.where(hit, raw[:, :256], 0.0), axis=1, keepdims=True) * factor)
    neg = jnp.exp(raw[:, 256:] * factor)
    total = pos + jnp.sum(neg, axis=1, keepdims=True)
    weight = cols_ref[:, 1:2]
    pos_grad = weight * (pos / total - 1.0)
    grads = jnp.concatenate(
        [jnp.where(hit, pos_grad, 0.0).astype(BF16), (weight * neg / total).astype(BF16)], axis=1
    )
    grad_hat = dot(grads, rows) * factor
    inner = jnp.mean(grad_hat * hat, axis=1, keepdims=True)
    grad[...] = ((grad_hat - hat * inner) * out_scale).astype(BF16)
    out_copy.start()
    sums = dot(low, grads, ((0,), (0,))) * factor
    terms[...] = sums.astype(BF16).reshape(PLANE, 2, 32, ROWS)
    for k in range(PLANE):
        own_ref[k] = terms[k, c]
        send_ref[k * 32 : (k + 1) * 32, :] = terms[k, 1 - c]
    products = jnp.sum(grads.astype(F32) * raw, axis=0, keepdims=True) * factor
    own_inner[...] = products
    top = products.astype(BF16).astype(F32)
    send_ref[512:528, :] = split_rows(top, products - top).astype(BF16)
    out_copy.wait()


def split_rows(top, rest):
    at = lax.broadcasted_iota(jnp.int32, (16, ROWS), 0)
    return jnp.where(at == 0, top, jnp.where(at == 1, rest, 0.0))


def quarter(source, target, sems, n):
    at = pl.ds(n * 4, 4)
    return pltpu.make_async_copy(source.at[at], target.at[at], sems.at[n])


def pair_body(own_ref, inner_ref, got_ref, out_ref, out, sems):
    other = got_ref[512:528, :].astype(F32)
    inner = inner_ref[...] + other[0:1, :] + other[1:2, :]
    top = inner.astype(BF16).astype(F32)
    tail = split_rows(top, inner - top).astype(BF16)
    for k in range(PLANE):
        mine = own_ref[k].astype(F32) + got_ref[k * 32 : (k + 1) * 32, :].astype(F32)
        out[k, 0:32, :] = mine.astype(BF16)
        out[k, 32:40, :] = tail[0:8, :]
        if k % 4 == 3:
            quarter(out, out_ref, sems, k // 4).start()
    for n in range(4):
        quarter(out, out_ref, sems, n).wait()


def plane_body(got_ref, ids_ref, pos_ref, neg_ref, got, sems):
    for n in range(4):
        quarter(got_ref, got, sems, n).start()
    acc = 0.0
    for k in range(PLANE):
        if k % 4 == 0:
            quarter(got_ref, got, sems, k // 4).wait()
        acc = acc + got[k].astype(F32)
    inner = acc[32:33, :] + acc[33:34, :]
    top = inner.astype(BF16).astype(F32)
    full = jnp.concatenate([acc[0:32, :], split_rows(top, inner - top)], axis=0)
    pos_ref[...] = full[:, 0:256]
    tail = jnp.concatenate(
        [full[0:34, 256:512], ids_ref[...], jnp.zeros((93, 256), F32)], axis=0
    )
    neg_ref[...] = jnp.transpose(tail).astype(BF16)


def item_body(pos_ref, got_ref, hat_ref, scale_ref, out_ref):
    got = got_ref[...]
    ids = got.astype(F32)[:, 34:35]
    hits = lax.broadcasted_iota(jnp.int32, (256, 256), 1).astype(F32) == ids
    hits = jnp.where(hits, 1.0, 0.0).astype(BF16)
    total = pos_ref[...] + dot(got, hits, ((0,), (0,)))[0:48, :]
    inner = (total[32:33, :] + total[33:34, :]) / WIDTH
    out_ref[...] = (total[0:32, :] - hat_ref[...] * inner) * scale_ref[...]


def layer_norm(values, gain):
    center = jnp.mean(values, axis=-1, keepdims=True)
    shifted = values - center
    spread = jnp.mean(shifted * shifted, axis=-1, keepdims=True)
    return shifted * lax.rsqrt(spread + norm_epsilon) * gain


def in_hbm(values):
    return pltpu.with_memory_space_constraint(values, pltpu.HBM)


def copies(block, count):
    return jnp.broadcast_to(block[None], (count, *block.shape))


def exchange(blocks, axis, groups=None):
    return lax.all_to_all(blocks, axis, 0, 0, tiled=True, axis_index_groups=groups)


def per_device(
    tokens,
    lengths,
    destination,
    worker_offset,
    positives,
    negatives,
    table,
    in_gain,
    w_uvqk,
    out_gain,
    w_out,
):
    item = lax.axis_index("item")
    user = lax.axis_index("user")
    core = user & 1
    x, y = user >> 3, (user >> 1) & 3
    place = jnp.where(core == 0, y * 4 + x, x * 4 + y)
    where = jnp.stack([item, core, place, user]).astype(jnp.int32)

    first_message = call(
        message_body,
        shape((ITEMS, 48, LANES)),
        [SMEM, HBM, HBM, HBM, HBM],
        scratch=[
            pltpu.VMEM((ITEMS, 256), jnp.int32),
            pltpu.VMEM((32, LANES), BF16),
            pltpu.VMEM((64, LANES), BF16),
            pltpu.VMEM((256, 512), BF16),
            pltpu.VMEM((LANES, 64), F32),
            pltpu.VMEM((ITEMS, 8, LANES), F32),
            pltpu.SemaphoreType.DMA((4,)),
        ],
    )(where, in_hbm(negatives), in_hbm(w_uvqk), in_hbm(w_out.T), in_hbm(table))
    got = exchange(first_message, "item")

    x_rows, cols, labels, parcels, table_low, hat_part, table_scale, group_ids, gain = call(
        prepare_body,
        (
            pltpu.HBM((ROWS, WIDTH), BF16),
            shape((ROWS, LANES), F32),
            shape((16, LANES)),
            pltpu.HBM((ROWS, WIDTH), BF16),
            pltpu.HBM((256, WIDTH), BF16),
            shape((32, 256), F32),
            shape((1, 256), F32),
            shape((1, 256), F32),
            shape((1, 512), F32),
        ),
        [SMEM] + [HBM] * 9,
        scratch=[
            pltpu.VMEM((ROWS, WIDTH), BF16),
            pltpu.VMEM((1, 32), jnp.int32),
            pltpu.VMEM((1, 32), jnp.int32),
            pltpu.VMEM((1, 32), jnp.int32),
            pltpu.VMEM((1, ROWS), jnp.int32),
            pltpu.VMEM((1, WIDTH), F32),
            pltpu.VMEM((256, WIDTH), BF16),
            pltpu.VMEM((ITEMS, 256), jnp.int32),
            pltpu.VMEM((1, 512), F32),
            pltpu.VMEM((ROWS, WIDTH), BF16),
            pltpu.VMEM((ROWS, WIDTH), BF16),
            pltpu.VMEM((256, WIDTH), BF16),
            pltpu.VMEM((256, WIDTH), F32),
            pltpu.VMEM((LANES, 256), F32),
            pltpu.SemaphoreType.DMA((9,)),
            pltpu.SemaphoreType.DMA((3,)),
        ],
        mib=28,
        out_specs=(HBM, VMEM, VMEM, HBM, HBM, VMEM, VMEM, VMEM, VMEM),
    )(
        where,
        *(
            in_hbm(v)
            for v in (
                tokens,
                lengths,
                destination,
                worker_offset,
                positives[None],
                in_gain[None],
                table,
                negatives,
                out_gain[None],
            )
        ),
    )
    got, x_rows, gain = lax.optimization_barrier((got, x_rows, gain))

    message = call(forward_body, shape((4, W_ROWS + REST, LANES)), [VMEM, VMEM])(got, labels)
    mid = exchange(message, "user", FIRST).reshape(4 * (W_ROWS + REST), LANES)
    held = exchange(copies(mid, 4), "user", SECOND).reshape(PLANE, W_ROWS + REST, LANES)
    held, parcels = lax.optimization_barrier((held, parcels))
    held_other = lax.ppermute(held, "user", PARTNER)
    arrived = exchange(parcels.reshape(USERS, MOST, WIDTH), "user").reshape(ROWS, WIDTH)

    home_out, o_own, o_other, g_own, g_other, near, far, kept = call(
        layer_body,
        (
            shape((ROWS, WIDTH)),
            pltpu.HBM((256, WIDTH), BF16),
            pltpu.HBM((256, WIDTH), BF16),
            shape((256, 512)),
            shape((256, 512)),
            shape((PLANE, LANES), F32),
            shape((PLANE, LANES), F32),
            pltpu.HBM((PLANE, W_ROWS + REST, LANES), BF16),
        ),
        [HBM, VMEM, HBM, HBM, VMEM, VMEM],
        scratch=[
            pltpu.VMEM((256, WIDTH), BF16),
            pltpu.VMEM((256, WIDTH), BF16),
            pltpu.VMEM((ROWS, WIDTH), BF16),
            pltpu.VMEM((PLANE, W_ROWS + REST, LANES), BF16),
            pltpu.VMEM((ROWS, WIDTH), BF16),
            pltpu.VMEM((2, 4, ROWS, 256), BF16),
            pltpu.VMEM((ROWS, 256), F32),
            pltpu.VMEM((ROWS, 256), F32),
            pltpu.SemaphoreType.DMA((6,)),
        ],
        mib=20,
        out_specs=(VMEM, HBM, HBM, VMEM, VMEM, VMEM, VMEM, HBM),
    )(in_hbm(x_rows), held, in_hbm(held_other), in_hbm(tokens), cols, gain)

    token_grad, own_terms, sent, own_inner = call(
        loss_body,
        (
            pltpu.HBM((ROWS, WIDTH), BF16),
            shape((PLANE, 32, ROWS)),
            shape((528, ROWS)),
            shape((1, ROWS), F32),
        ),
        [SMEM] + [VMEM] * 5,
        scratch=[
            pltpu.VMEM((PLANE, 2, 32, ROWS), BF16),
            pltpu.VMEM((ROWS, WIDTH), BF16),
            pltpu.SemaphoreType.DMA,
        ],
        mib=16,
        out_specs=(HBM, VMEM, VMEM, VMEM),
    )(where, home_out, table_low, cols, g_own, g_other)
    partner_terms = lax.ppermute(sent, "user", PARTNER)
    blocks = [pltpu.VMEM((PLANE, 40, ROWS), BF16), pltpu.SemaphoreType.DMA((4,))]
    pair = call(pair_body, pltpu.HBM((PLANE, 40, ROWS), BF16), [VMEM] * 3, out_specs=HBM, scratch=blocks)(
        own_terms, own_inner, partner_terms
    )
    pair, arrived = lax.optimization_barrier((pair, arrived))
    plane = exchange(pair, "user", SAME_CORE)

    layer_out = call(
        worker_body,
        shape((256, WIDTH)),
        [SMEM, VMEM, VMEM, HBM, HBM, VMEM, VMEM, VMEM, HBM, HBM],
        scratch=[
            pltpu.VMEM((PLANE, W_ROWS + REST, LANES), BF16),
            pltpu.VMEM((PLANE, W_ROWS + REST, LANES), BF16),
            pltpu.VMEM((256, WIDTH), BF16),
            pltpu.VMEM((256, WIDTH), BF16),
            pltpu.VMEM((2, 4, 256, 256), BF16),
            pltpu.VMEM((256, 256), F32),
            pltpu.VMEM((256, 256), F32),
            pltpu.SemaphoreType.DMA((4,)),
        ],
        mib=24,
    )(where, arrived, in_gain[None], o_own, o_other, gain, near, far, kept, in_hbm(held_other))

    positive_part, negative_part = call(
        plane_body, (shape((48, 256), F32), shape((256, LANES))), [HBM, VMEM], scratch=blocks
    )(in_hbm(plane), group_ids)
    owned = exchange(negative_part.reshape(ITEMS, 16, LANES), "item").reshape(256, LANES)
    item_grad = call(item_body, shape((32, 256), F32), [VMEM] * 4)(
        positive_part, owned, hat_part, table_scale
    ).T
    return (layer_out, token_grad, item_grad)


def solution(mesh):
    return jax.shard_map(
        per_device,
        mesh=mesh,
        in_specs=(
            P(("user", "item"), None),
            P(("user", "item"), None),
            P(("user", "item"), None),
            P(("user", "item"), None),
            P(("user", "item")),
            P(),
            P("item", None),
            P(),
            P("item", None),
            P(),
            P(None, "item"),
        ),
        out_specs=(P(("user", "item"), None), P(("user", "item"), None), P("item", "user")),
        check_vma=False,
    )
```
